32 devices in a mesh: dp: 16 (over z, x, core), pair: 2 (over y).
Axes of the slice: x: 2, y: 2, z: 4, core: 2. Of those that a mesh axis runs over, the one named last changes fastest.
Arguments:
- hidden: bfloat16 [64, 64, 768], P(('dp', 'pair')), may hold values from -12 to 12
- features: bfloat16 [64, 257, 1408], P(('dp', 'pair')), may hold values from -6 to 6
- text_lengths: int32 [64], P(('dp', 'pair')), may hold values from 1 to 32
- cotangent: bfloat16 [64, 64, 768], P(('dp', 'pair')), may hold values from -12 to 12
- self_project: bfloat16 [3, 768, 768], P(None, ('dp', 'pair')), may hold values from -0.21875 to 0.21875
- self_output: bfloat16 [768, 768], P(('dp', 'pair')), may hold values from -0.625 to 0.625
- self_bias: bfloat16 [3, 768], P(None, ('dp', 'pair')), may hold values from -3 to 3
- norm_gain: bfloat16 [4, 768], P(None, ('dp', 'pair')), may hold values from 0.25 to 1.75
- norm_bias: bfloat16 [4, 768], P(None, ('dp', 'pair')), may hold values from -3 to 3
- cross_query: bfloat16 [768, 768], P(('dp', 'pair')), may hold values from -0.21875 to 0.21875
- cross_output: bfloat16 [768, 768], P(('dp', 'pair')), may hold values from -0.75 to 0.75
- image_project: bfloat16 [2, 1408, 768], P(None, None, ('dp', 'pair')), may hold values from -0.15625 to 0.15625
- cross_bias: bfloat16 [3, 768], P(None, ('dp', 'pair')), may hold values from -3 to 3
- expand_weight: bfloat16 [2, 768, 3072], P(None, None, ('dp', 'pair')), may hold values from -0.21875 to 0.21875
- expand_bias: bfloat16 [2, 3072], P(None, ('dp', 'pair')), may hold values from -3 to 3
- reduce_weight: bfloat16 [2, 3072, 768], P(None, ('dp', 'pair')), may hold values from -0.109375 to 0.109375
- reduce_bias: bfloat16 [2, 768], P(None, ('dp', 'pair')), may hold values from -3 to 3
Outputs:
- layer_out: bfloat16 [64, 64, 768], P(('dp', 'pair'))
- hidden_grad: float32 [64, 64, 768], P(('dp', 'pair'))
- feature_grad: float32 [64, 257, 1408], P(('dp', 'pair'))
- grad_self_project: float32 [3, 768, 768], P(None, ('dp', 'pair'))
- grad_self_output: float32 [768, 768], P(('dp', 'pair'))
- grad_self_bias: float32 [3, 768], P(None, ('dp', 'pair'))
- grad_norm_gain: float32 [4, 768], P(None, ('dp', 'pair'))
- grad_norm_bias: float32 [4, 768], P(None, ('dp', 'pair'))
- grad_cross_query: float32 [768, 768], P(('dp', 'pair'))
- grad_cross_output: float32 [768, 768], P(('dp', 'pair'))
- grad_image_project: float32 [2, 1408, 768], P(None, None, ('dp', 'pair'))
- grad_cross_bias: float32 [3, 768], P(None, ('dp', 'pair'))
- grad_expand_weight: float32 [2, 768, 3072], P(None, None, ('dp', 'pair'))
- grad_expand_bias: float32 [2, 3072], P(None, ('dp', 'pair'))
- grad_reduce_weight: float32 [2, 3072, 768], P(None, ('dp', 'pair'))
- grad_reduce_bias: float32 [2, 768], P(None, ('dp', 'pair'))
The draws below stay inside these ranges and needn't reach their ends.
Inputs may be any that keep to these rules, and one draw needn't show every extreme that they name: `text_lengths`: text rows at or beyond an item's length are padding that no row attends to.
All inputs are finite; a program needn't handle non-finite values.
Results may differ from the reference program's by a relative error of at most 0.02.
Values may be sent and summed in bfloat16 or wider, within the bound.
No kernel may reach another device: no remote copies, remote signals or barrier semaphores. Data moves between devices by JAX's collectives and lax.ppermute only.
A program may use at most 320 MiB of HBM per device.

```python
import math
import jax
import jax.numpy as jnp
from jax import lax

D = 768
HEAD = 64
FF = 3072
VW = 1408
IMG = 257
NQ = 32
NT = 32
ROWS = 64
ITEMS = 64


def touch_ends(entries, rng, low, high):
    longest = entries.shape.index(max(entries.shape))
    spots = []
    for shift in (0, 1):
        where = [jax.random.randint(jax.random.fold_in(rng, axis), (), 0, length) for axis, length in enumerate(entries.shape)]
        where[longest] = (where[longest] + shift) % entries.shape[longest]
        spots.append(tuple(where))
    return entries.at[spots[0]].set(low).at[spots[1]].set(high)


def raised(values, key, source, target, parts, factor):
    owner, partner = [(jnp.arange(values.shape[axis_at]) // (values.shape[axis_at] // parts)).reshape([-1 if axis == axis_at else 1 for axis in range(values.ndim)]) for axis_at in (source, target)]
    chosen = jax.random.permutation(key, parts)[partner]
    strong = (owner == chosen) | (owner == (partner + parts // 2) % parts)
    return jnp.where(strong, factor * values, values)


def block_levels(own_key, extent, pieces, smallest, high):
    def one(dim, shards_of):
        draws = jax.random.uniform(jax.random.fold_in(jax.random.fold_in(own_key, 6), dim), (shards_of,), jnp.float32, smallest / len(pieces), high / len(pieces))
        return jnp.repeat(jnp.exp(draws), extent[dim] // shards_of).reshape((-1,) + (1,) * (len(extent) - dim - 1))

    factor_of = one(*pieces[0])
    for cut in pieces[1:]:
        factor_of = factor_of * one(*cut)
    return factor_of


def gaussian(key, dims, width, bound, pieces=(), kind=jnp.bfloat16):
    entries = jax.random.normal(key, dims, jnp.float32) * width
    if len(pieces) > 0:
        entries = block_levels(key, dims, pieces, -0.22, 0.18) * entries
    return jnp.clip(entries, min=-bound, max=bound).astype(kind)


def bell_draw_with(stream_key, dims, scale, bound, pieces, heavy, held_as=jnp.bfloat16):
    entries = scale * jax.random.normal(stream_key, dims, jnp.float32)
    if pieces:
        entries = entries * block_levels(stream_key, dims, pieces, -0.22, 0.18)
    return jnp.clip(raised(entries, jax.random.fold_in(stream_key, 3), *heavy), -bound, bound).astype(held_as)


def setup_inputs(seed: int = 0) -> dict:
    streams_of = jax.random.split(jax.random.key(seed), 18)
    hidden = bell_draw_with(streams_of[0], (ITEMS, ROWS, D), 1.0, 12.0, ((0, 32),), (0, 2, 32, 2.75))
    features = gaussian(streams_of[1], (ITEMS, IMG, VW), 1.0, 6.0, ((0, 32),))
    text_lengths = touch_ends(jax.random.randint(streams_of[2], (ITEMS,), 1, NT + 1), jax.random.fold_in(streams_of[2], 1), 1, NT).astype(jnp.int32)
    cotangent = bell_draw_with(streams_of[3], (ITEMS, ROWS, D), 1.0, 12.0, ((0, 32),), (0, 2, 32, 2.75))
    self_project = gaussian(streams_of[4], (3, D, D), D ** -0.5, 0.21875, ((1, 32),))
    self_output = gaussian(streams_of[5], (D, D), (D // 8) ** -0.5, 0.625, ((0, 32),))
    self_bias = gaussian(streams_of[6], (3, D), 0.5, 3.0, ((1, 32),))
    norm_gain = jnp.clip(1.0 + 0.15 * jax.random.normal(streams_of[7], (4, D), jnp.float32), 0.25, 1.75).astype(jnp.bfloat16)
    norm_bias = gaussian(streams_of[8], (4, D), 0.5, 3.0, ((1, 32),))
    cross_query = gaussian(streams_of[9], (D, D), D ** -0.5, 0.21875, ((0, 32),))
    cross_output = gaussian(streams_of[10], (D, D), (D // 12) ** -0.5, 0.75, ((0, 32),))
    image_project = gaussian(streams_of[11], (2, VW, D), VW ** -0.5, 0.15625, ((2, 32),))
    cross_bias = gaussian(streams_of[12], (3, D), 0.5, 3.0, ((1, 32),))
    expand_weight = gaussian(streams_of[13], (2, D, FF), D ** -0.5, 0.21875, ((2, 32),))
    expand_bias = gaussian(streams_of[14], (2, FF), 0.5, 3.0, ((1, 32),))
    reduce_weight = gaussian(streams_of[15], (2, FF, D), FF ** -0.5, 0.109375, ((1, 32),))
    reduce_bias = gaussian(streams_of[16], (2, D), 0.5, 3.0, ((1, 32),))
    return {"hidden": hidden, "features": features, "text_lengths": text_lengths, "cotangent": cotangent, "self_project": self_project, "self_output": self_output, "self_bias": self_bias, "norm_gain": norm_gain, "norm_bias": norm_bias, "cross_query": cross_query, "cross_output": cross_output, "image_project": image_project, "cross_bias": cross_bias, "expand_weight": expand_weight, "expand_bias": expand_bias, "reduce_weight": reduce_weight, "reduce_bias": reduce_bias}


eps = 1e-06
masked_off = 1000000000.0
highest = lax.Precision.HIGHEST

@jax.custom_vjp
def low(v):
    return lax.optimization_barrier(v.astype(jnp.bfloat16)).astype(jnp.float32)

@jax.custom_vjp
def low_back(v):
    return v

def low_keep(v):
    return (low(v), None)

def low_pass(kept, grad):
    return (grad,)

def back_keep(v):
    return (v, None)

def back_low(kept, grad):
    return (low(grad),)
low.defvjp(low_keep, low_pass)
low_back.defvjp(back_keep, back_low)

def both_ways(tensor):
    return low_back(low(tensor))

def linear(inputs, weight):
    return jnp.einsum('gqd,de->gqe', inputs, weight, precision=highest)

def layer_norm(values, norm_scale, norm_shift):
    center = values - lax.optimization_barrier(jnp.mean(values, axis=-1, keepdims=True))
    spread = lax.optimization_barrier(jnp.mean(center * center, axis=-1, keepdims=True))
    return center * lax.rsqrt(spread + eps) * norm_scale + norm_shift

def split_heads(values):
    return values.reshape(values.shape[0], values.shape[1], values.shape[2] // HEAD, HEAD)

def mask_bias(lengths, row_count):
    row_index = jnp.arange(row_count)[:, None]
    col_index = jnp.arange(row_count)[None, :]
    allowed = (col_index < NQ) | (row_index >= NQ) & (col_index <= row_index) & (col_index - NQ < lengths[:, None, None])
    return jnp.where(allowed, jnp.float32(0.0), jnp.float32(-masked_off))[:, None]

def attend(queries, key_rows, value_rows, mask_add):
    raw_scores = jnp.einsum('gqhe,gkhe->ghqk', split_heads(queries), split_heads(key_rows), precision=highest)
    scores = low_back(raw_scores * HEAD ** (-0.5) + mask_add)
    weights = jax.nn.softmax(scores, axis=-1)
    mixture = jnp.einsum('ghqk,gkhe->gqhe', low(weights), split_heads(value_rows), precision=highest)
    return mixture.reshape(queries.shape)

def feed_forward(inputs, rows_low, w_in, b_in, w_out, b_out, norm_scale, norm_shift):
    pre_act = low_back(linear(rows_low, w_in) + b_in)
    active = low(jax.nn.gelu(pre_act, approximate=False))
    branch_sum = low_back(linear(active, w_out) + b_out) + inputs
    return layer_norm(branch_sum, norm_scale, norm_shift)

def forward(hidden32, feature32, mask_add, self_project, self_output, self_bias, norm_gain, norm_bias, cross_query, cross_output, image_project, cross_bias, expand_weight, expand_bias, reduce_weight, reduce_bias):
    queries = both_ways(linear(hidden32, self_project[0]) + self_bias[0])
    key_rows = both_ways(linear(hidden32, self_project[1]))
    value_rows = both_ways(linear(hidden32, self_project[2]) + self_bias[1])
    mixture = both_ways(attend(queries, key_rows, value_rows, mask_add))
    pre_one = low_back(linear(mixture, self_output) + self_bias[2]) + hidden32
    first_norm = layer_norm(pre_one, norm_gain[0], norm_bias[0])
    first_low = low(first_norm)
    cross_rows = both_ways(linear(first_low[:, :NQ], cross_query) + cross_bias[0])
    image_keys = both_ways(linear(feature32, image_project[0]))
    image_values = both_ways(linear(feature32, image_project[1]) + cross_bias[1])
    looked = both_ways(attend(cross_rows, image_keys, image_values, 0.0))
    pre_two = low_back(linear(looked, cross_output) + cross_bias[2]) + first_norm[:, :NQ]
    second = layer_norm(pre_two, norm_gain[1], norm_bias[1])
    out_query = feed_forward(second, low(second), expand_weight[0], expand_bias[0], reduce_weight[0], reduce_bias[0], norm_gain[2], norm_bias[2])
    out_text = feed_forward(first_norm[:, NQ:], first_low[:, NQ:], expand_weight[1], expand_bias[1], reduce_weight[1], reduce_bias[1], norm_gain[3], norm_bias[3])
    return jnp.concatenate([out_query, out_text], axis=1)

def reference(hidden, features, text_lengths, cotangent, self_project, self_output, self_bias, norm_gain, norm_bias, cross_query, cross_output, image_project, cross_bias, expand_weight, expand_bias, reduce_weight, reduce_bias):
    weights = tuple((member.astype(jnp.float32) for member in (self_project, self_output, self_bias, norm_gain, norm_bias, cross_query, cross_output, image_project, cross_bias, expand_weight, expand_bias, reduce_weight, reduce_bias)))
    group_size = math.gcd(ITEMS, 64)
    group_count = ITEMS // group_size

    def regroup(whole_array):
        return whole_array.reshape((group_count, group_size) + whole_array.shape[1:])

    def one_group(totals, group_data):
        item_rows, item_feats, lengths, upstream = group_data
        mask_add = mask_bias(lengths, ROWS)

        def run_layer(rows32, feats32, *params):
            return forward(rows32, feats32, mask_add, *params)
        result, pull_back = jax.vjp(run_layer, item_rows.astype(jnp.float32), item_feats.astype(jnp.float32), *weights)
        gradients = pull_back(upstream.astype(jnp.float32))
        totals = tuple((summed + update for summed, update in zip(totals, gradients[2:])))
        return (totals, (result.astype(jnp.bfloat16), gradients[0], gradients[1]))
    initial = tuple((jnp.zeros_like(member) for member in weights))
    totals, stacked = lax.scan(one_group, initial, (regroup(hidden), regroup(features), regroup(text_lengths), regroup(cotangent)))
    layer_out = stacked[0].reshape(hidden.shape)
    hidden_grad = stacked[1].reshape(hidden.shape)
    feature_grad = stacked[2].reshape(features.shape)
    return (layer_out, hidden_grad, feature_grad, totals[0], totals[1], totals[2], totals[3], totals[4], totals[5], totals[6], totals[7], totals[8], totals[9], totals[10], totals[11], totals[12])
```

```python
import functools

import jax
import jax.numpy as jnp
from jax import lax
from jax.experimental import pallas as pl
from jax.experimental.pallas import tpu as pltpu
from jax.sharding import Mesh, PartitionSpec as P

HEAD = 64
NQ = 32
GROUP = 256
PER = GROUP // HEAD
eps = 1e-06
masked_off = 1000000000.0
AXES = ("z", "x", "c", "y")
BF = jnp.bfloat16
F32 = jnp.float32


def coords(index):
    return (index // 8, index // 4 % 2, index // 2 % 2, index % 2)


def pairs(count, move):
    result = []
    for source in range(count):
        z, x, c, y = move(*coords(source))
        result.append((source, ((z * 2 + x) * 2 + c) * 2 + y))
    return result


def step_a(z, x, c, y):
    return (z, x ^ 1, c, y) if c == 0 else (z, x, c, y ^ 1)


def step_b(z, x, c, y):
    return (z, x, c, y ^ 1) if c == 0 else (z, x ^ 1, c, y)


def step_c(z, x, c, y):
    return (z, x, c ^ 1, y)


def swap(value, move):
    count = lax.axis_size(AXES)
    return lax.ppermute(value, AXES, pairs(count, move))


def swap_z(value, distance):
    return swap(value, lambda z, x, c, y: (z ^ distance, x, c, y))


def rows_join(parts):
    return jnp.concatenate(parts, axis=0)


def gather_z(unit):
    planes = lax.axis_size("z")
    if planes == 4:
        return rows_join([unit] + [swap_z(unit, k) for k in (1, 2, 3)])
    return lax.all_gather(unit, "z", axis=0, tiled=True)


def gather_plane(rows):
    for move in (step_a, step_b, step_c):
        rows = rows_join([rows, swap(rows, move)])
    return rows


def gather_all(unit):
    return gather_plane(gather_z(unit))


def add_low(kept, received):
    return kept.astype(F32) + received.astype(F32)


def halve(kept, sent, move):
    return add_low(kept, swap(sent.astype(BF), move))


def scatter_plane(kept, sent):
    total = halve(kept, sent, step_c)
    for move in (step_b, step_a):
        half = total.shape[0] // 2
        total = halve(total[:half], total[half:], move)
    return total


def scatter_z(total):
    planes = lax.axis_size("z")
    low = total.astype(BF)
    if planes == 4:
        own = total.shape[0] // 4
        result = total[:own].astype(F32)
        for k in (1, 2, 3):
            result = result + swap_z(low[k * own : (k + 1) * own], k).astype(F32)
        return result
    return lax.psum_scatter(low, "z", scatter_dimension=0, tiled=True).astype(F32)


def scatter_all(kept, sent):
    return scatter_z(scatter_plane(kept, sent))


def slot_owner(count):
    z, x, c, y = (lax.axis_index(name) for name in AXES)
    planes = count // 8
    slot = jnp.arange(count)
    k = slot % planes
    alpha = slot // planes % 2
    beta = slot // (2 * planes) % 2
    core = c ^ (slot // (4 * planes))
    flip_x = jnp.where(core == 0, alpha, beta)
    flip_y = jnp.where(core == 0, beta, alpha)
    plane = (z ^ k) if planes == 4 else k
    return ((plane * 2 + (x ^ flip_x)) * 2 + core) * 2 + (y ^ flip_y)


def order_matrix(width):
    count = lax.axis_size(AXES)
    each = width // count
    source = (slot_owner(count)[:, None] * each + jnp.arange(each)[None, :]).reshape(-1)
    return (jnp.arange(width)[:, None] == source[None, :]).astype(BF)


def dot(left, right):
    return lax.dot_general(
        left, right, (((left.ndim - 1,), (0,)), ((), ())), preferred_element_type=F32
    )


def dot_t(left, right):
    return lax.dot_general(
        left, right, (((left.ndim - 1,), (1,)), ((), ())), preferred_element_type=F32
    )


def outer(left, right):
    lead = tuple(range(left.ndim - 1))
    return lax.dot_general(left, right, ((lead, lead), ((), ())), preferred_element_type=F32)


def column_sum(values):
    return jnp.sum(values.astype(F32), axis=tuple(range(values.ndim - 1)))


def layer_norm(values, scale, shift):
    center = values - jnp.mean(values, axis=-1, keepdims=True)
    spread = jnp.mean(center * center, axis=-1, keepdims=True)
    return center * lax.rsqrt(spread + eps) * scale + shift


def norm_back(values, scale, gradient):
    center = values - jnp.mean(values, axis=-1, keepdims=True)
    spread = jnp.mean(center * center, axis=-1, keepdims=True)
    inverse = lax.rsqrt(spread + eps)
    normal = center * inverse
    inner = gradient * scale
    result = inverse * (
        inner
        - jnp.mean(inner, axis=-1, keepdims=True)
        - normal * jnp.mean(inner * normal, axis=-1, keepdims=True)
    )
    return result, column_sum(gradient * normal), column_sum(gradient)


def exact_gelu(values):
    return jax.nn.gelu(values, approximate=False)


def head_masks():
    lane = lax.broadcasted_iota(jnp.int32, (1, GROUP), 1) // HEAD
    return [(lane == h).astype(F32).astype(BF) for h in range(PER)]


def spread_heads(rows, masks):
    return jnp.concatenate([rows * mask for mask in masks], axis=0)


def fold_heads(stacked, masks, count):
    total = None
    for h, mask in enumerate(masks):
        part = stacked[h * count : (h + 1) * count] * mask.astype(F32)
        total = part if total is None else total + part
    return total


def softmax_rows(scores):
    shifted = jnp.exp(scores - jnp.max(scores, axis=-1, keepdims=True))
    return shifted / jnp.sum(shifted, axis=-1, keepdims=True)


def self_mask(length, rows):
    shape = (PER * rows, rows)
    row = lax.broadcasted_iota(jnp.int32, shape, 0) % rows
    col = lax.broadcasted_iota(jnp.int32, shape, 1)
    allowed = (col < NQ) | ((row >= NQ) & (col <= row) & (col - NQ < length))
    return jnp.where(allowed, F32(0.0), F32(-masked_off))


def self_forward_kernel(items, width, length_ref, qkv_ref, out_ref):
    masks = head_masks()
    count = qkv_ref.shape[0] // items
    for i in range(items):
        rows = pl.ds(i * count, count)
        mask_add = self_mask(length_ref[i], count)
        for g in range(width // GROUP):
            cols = [pl.ds(n * width + g * GROUP, GROUP) for n in range(3)]
            q = spread_heads(qkv_ref[rows, cols[0]], masks)
            scores = dot_t(q, qkv_ref[rows, cols[1]]) * HEAD ** (-0.5) + mask_add
            weights = softmax_rows(scores).astype(BF)
            mixed = dot(weights, qkv_ref[rows, cols[2]])
            out_ref[rows, cols[0]] = fold_heads(mixed, masks, count).astype(BF)


def attend_group_back(q, k, v, mask_add, grad, masks, count):
    q = spread_heads(q, masks)
    grad = spread_heads(grad, masks)
    weights = softmax_rows(dot_t(q, k) * HEAD ** (-0.5) + mask_add)
    grad_value = outer(weights.astype(BF), grad).astype(BF)
    grad_weight = dot_t(grad, v)
    grad_score = (
        weights * (grad_weight - jnp.sum(grad_weight * weights, axis=-1, keepdims=True))
    ).astype(BF)
    grad_query = fold_heads(dot(grad_score, k), masks, count) * HEAD ** (-0.5)
    grad_key = outer(grad_score, q) * HEAD ** (-0.5)
    return grad_query.astype(BF), grad_key.astype(BF), grad_value


def self_backward_kernel(items, width, length_ref, qkv_ref, grad_ref, out_ref):
    masks = head_masks()
    count = qkv_ref.shape[0] // items
    for i in range(items):
        rows = pl.ds(i * count, count)
        mask_add = self_mask(length_ref[i], count)
        for g in range(width // GROUP):
            cols = [pl.ds(n * width + g * GROUP, GROUP) for n in range(3)]
            results = attend_group_back(
                *[qkv_ref[rows, col] for col in cols],
                mask_add,
                grad_ref[rows, cols[0]],
                masks,
                count,
            )
            for col, value in zip(cols, results):
                out_ref[rows, col] = value


def cross_forward_kernel(items, width, q_ref, k_ref, v_ref, out_ref):
    masks = head_masks()
    count = q_ref.shape[0] // items
    for i in range(items):
        rows = pl.ds(i * count, count)
        for g in range(width // GROUP):
            cols = pl.ds(g * GROUP, GROUP)
            q = spread_heads(q_ref[rows, cols], masks)
            scores = dot_t(q, k_ref[i, :, cols]) * HEAD ** (-0.5)
            mixed = dot(softmax_rows(scores).astype(BF), v_ref[i, :, cols])
            out_ref[rows, cols] = fold_heads(mixed, masks, count).astype(BF)


def cross_backward_kernel(items, width, q_ref, k_ref, v_ref, grad_ref, dq_ref, dk_ref, dv_ref):
    masks = head_masks()
    count = q_ref.shape[0] // items
    for i in range(items):
        rows = pl.ds(i * count, count)
        for g in range(width // GROUP):
            cols = pl.ds(g * GROUP, GROUP)
            dq, dk, dv = attend_group_back(
                q_ref[rows, cols],
                k_ref[i, :, cols],
                v_ref[i, :, cols],
                F32(0.0),
                grad_ref[rows, cols],
                masks,
                count,
            )
            dq_ref[rows, cols] = dq
            dk_ref[i, :, cols] = dk
            dv_ref[i, :, cols] = dv


def whole_blocks(count):
    return [pl.BlockSpec(memory_space=pltpu.VMEM)] * count


def kernel_call(body, name, out_shapes, lengths, *arrays):
    specs = whole_blocks(len(arrays))
    if lengths is not None:
        specs = [pl.BlockSpec(memory_space=pltpu.SMEM)] + specs
        arrays = (lengths,) + arrays
    return pl.pallas_call(
        body,
        name=name,
        out_shape=out_shapes,
        in_specs=specs,
        out_specs=jax.tree.map(lambda _: pl.BlockSpec(memory_space=pltpu.VMEM), out_shapes),
    )(*arrays)


def shards(
    hidden,
    features,
    text_lengths,
    cotangent,
    self_project,
    self_output,
    self_bias,
    norm_gain,
    norm_bias,
    cross_query,
    cross_output,
    image_project,
    cross_bias,
    expand_weight,
    expand_bias,
    reduce_weight,
    reduce_bias,
):
    items, item_rows, width = hidden.shape
    each = self_output.shape[0]
    image_width = features.shape[2]
    ff_each = reduce_weight.shape[1]
    count = lax.axis_size(AXES)
    planes = count // 8
    rows = items * item_rows
    text_rows = item_rows - NQ
    order = order_matrix(width)

    def by_slot(values):
        return dot(values, order).astype(BF)

    def by_place(values):
        return dot_t(values.astype(BF), order)

    unit_self = jnp.concatenate(
        [self_project[0], self_project[1], self_project[2], self_output], axis=1
    )
    image_rows = jnp.swapaxes(image_project, 1, 2)
    unit_cross = jnp.concatenate(
        [image_rows[0], image_rows[1], cross_query, cross_output], axis=1
    )
    vectors = jnp.concatenate([self_bias, norm_gain, norm_bias, cross_bias, reduce_bias], axis=0)
    n_vectors = vectors.shape[0]
    unit_small = jnp.concatenate([vectors.reshape(1, -1), expand_bias.reshape(1, -1)], axis=1)
    unit_ff = [
        jnp.concatenate([expand_weight[j].T, reduce_weight[j]], axis=1) for j in range(2)
    ]
    w_self = gather_all(unit_self)
    small = gather_all(unit_small)
    w_cross = gather_all(unit_cross)
    w_ff = [gather_z(unit) for unit in unit_ff]

    w_qkv, w_mix = w_self[:, : 3 * width], w_self[:, 3 * width :]
    w_ikey, w_ivalue = w_cross[:, :image_width], w_cross[:, image_width : 2 * image_width]
    w_cquery = w_cross[:, 2 * image_width : 2 * image_width + width]
    w_cout = w_cross[:, 2 * image_width + width :]
    w_up = [w[:, :width] for w in w_ff]
    w_down = [w[:, width:] for w in w_ff]
    small_rows = small[:, : n_vectors * each].reshape(count, n_vectors, each)
    small_rows = jnp.swapaxes(small_rows, 0, 1).reshape(n_vectors, width)
    small_all = by_place(small_rows)
    b_self, gain, shift, b_cross, b_down = (
        small_all[0:3],
        small_all[3:7],
        small_all[7:11],
        small_all[11:14],
        small_all[14:16],
    )
    b_up = jnp.swapaxes(
        small[:planes, n_vectors * each :].reshape(planes, 2, ff_each), 0, 1
    ).reshape(2, planes * ff_each)
    b_up = b_up.astype(F32)

    flat = hidden.reshape(rows, width)
    flat_slot = by_slot(flat)
    b_qkv = jnp.concatenate([b_self[0], jnp.zeros_like(b_self[0]), b_self[1]])
    qkv = (dot(flat_slot, w_qkv) + b_qkv).astype(BF)
    mixture = kernel_call(
        functools.partial(self_forward_kernel, items, width),
        "self_forward",
        jax.ShapeDtypeStruct((rows, width), BF),
        text_lengths,
        qkv,
    )
    mixture_slot = by_slot(mixture)
    pre_one = dot(mixture_slot, w_mix) + b_self[2] + flat.astype(F32)
    first = layer_norm(pre_one, gain[0], shift[0]).reshape(items, item_rows, width)
    first_query = first[:, :NQ].reshape(items * NQ, width)
    first_text = first[:, NQ:].reshape(items * text_rows, width)

    query_slot = by_slot(first_query.astype(BF))
    cross_rows = (dot(query_slot, w_cquery) + b_cross[0]).astype(BF)
    image_keys = by_place(dot_t(features, w_ikey)).astype(BF)
    b_value_slot = small_rows[12].astype(F32)
    image_values = by_place(
        (dot_t(features, w_ivalue) + b_value_slot).astype(BF)
    ).astype(BF)
    looked = kernel_call(
        functools.partial(cross_forward_kernel, items, width),
        "cross_forward",
        jax.ShapeDtypeStruct((items * NQ, width), BF),
        None,
        cross_rows,
        image_keys,
        image_values,
    )
    looked_slot = by_slot(looked)
    pre_two = dot(looked_slot, w_cout) + b_cross[2] + first_query
    second = layer_norm(pre_two, gain[1], shift[1])

    upstream = cotangent.astype(F32)
    branches = []
    for j, values in ((1, first_text), (0, second)):
        cot = (upstream[:, NQ:] if j else upstream[:, :NQ]).reshape(values.shape)
        low = gather_plane(values.astype(BF))
        half = low.shape[0] // 2
        pre_act = dot_t(low, w_up[j]) + b_up[j]
        active = exact_gelu(pre_act).astype(BF)
        partial = dot(active, w_down[j])
        branch_sum = scatter_plane(partial[:half], partial[half:]) + b_down[j] + values
        out = layer_norm(branch_sum, gain[2 + j], shift[2 + j])
        grad_sum, gain_grad, shift_grad = norm_back(branch_sum, gain[2 + j], cot)
        grad_low = grad_sum.astype(BF)
        grad_all = gather_plane(grad_low)
        _, pull_back = jax.vjp(exact_gelu, pre_act)
        grad_pre = pull_back(dot_t(grad_all, w_down[j]))[0].astype(BF)
        grad_part = dot(grad_pre, w_up[j])
        grad_rows = scatter_plane(grad_part[:half], grad_part[half:]) + grad_sum
        grad_up = scatter_z(outer(grad_pre, low).astype(BF))
        grad_down = scatter_z(outer(active, grad_all).astype(BF))
        branches.append(
            (
                out,
                gain_grad,
                shift_grad,
                grad_rows,
                grad_up,
                grad_down,
                column_sum(grad_pre),
                column_sum(grad_low),
            )
        )
    text, query = branches
    layer_out = jnp.concatenate(
        [
            query[0].reshape(items, NQ, width),
            text[0].reshape(items, text_rows, width),
        ],
        axis=1,
    ).astype(BF)

    half = width // 2

    def weight_grad(left_slot, right):
        return scatter_all(
            outer(left_slot[..., :half], right).astype(BF),
            outer(left_slot[..., half:], right).astype(BF),
        )

    grad_two, gain_one, shift_one = norm_back(pre_two, gain[1], query[3])
    grad_two_low = grad_two.astype(BF)
    grad_looked = by_place(dot_t(grad_two_low, w_cout)).astype(BF)
    wide = jax.ShapeDtypeStruct(image_keys.shape, BF)
    grad_cross, grad_ikey, grad_ivalue = kernel_call(
        functools.partial(cross_backward_kernel, items, width),
        "cross_backward",
        (jax.ShapeDtypeStruct((items * NQ, width), BF), wide, wide),
        None,
        cross_rows,
        image_keys,
        image_values,
        grad_looked,
    )
    ikey_slot = by_slot(grad_ikey)
    ivalue_slot = by_slot(grad_ivalue)
    feature_grad = dot(ikey_slot, w_ikey) + dot(ivalue_slot, w_ivalue)
    grad_first_query = grad_two + by_place(dot_t(grad_cross, w_cquery))
    grad_image = [weight_grad(slot, features) for slot in (ikey_slot, ivalue_slot)]
    grad_cquery = weight_grad(query_slot, grad_cross)
    grad_cout = weight_grad(looked_slot, grad_two_low)

    grad_first = jnp.concatenate(
        [
            grad_first_query.reshape(items, NQ, width),
            text[3].reshape(items, text_rows, width),
        ],
        axis=1,
    ).reshape(rows, width)
    grad_one, gain_zero, shift_zero = norm_back(pre_one, gain[0], grad_first)
    grad_one_low = grad_one.astype(BF)
    grad_mixture = by_place(dot_t(grad_one_low, w_mix)).astype(BF)
    grad_qkv = kernel_call(
        functools.partial(self_backward_kernel, items, width),
        "self_backward",
        jax.ShapeDtypeStruct((rows, 3 * width), BF),
        text_lengths,
        qkv,
        grad_mixture,
    )
    hidden_grad = grad_one + by_place(dot_t(grad_qkv, w_qkv))
    grad_mix = weight_grad(mixture_slot, grad_one_low)
    grad_project = weight_grad(flat_slot, grad_qkv)

    qkv_sums = column_sum(grad_qkv)
    sums = jnp.stack(
        [
            qkv_sums[:width],
            qkv_sums[2 * width :],
            column_sum(grad_one_low),
            gain_zero,
            gain_one,
            query[1],
            text[1],
            shift_zero,
            shift_one,
            query[2],
            text[2],
            column_sum(grad_cross),
            column_sum(grad_ivalue),
            column_sum(grad_two_low),
            query[7],
            text[7],
        ]
    )
    sums_slot = jnp.swapaxes(by_slot(sums.astype(BF)), 0, 1)
    own_sums = jnp.swapaxes(scatter_all(sums_slot[:half], sums_slot[half:]), 0, 1)
    own_up_bias = scatter_z(jnp.stack([query[6], text[6]], axis=1))
    return (
        layer_out,
        hidden_grad.reshape(items, item_rows, width),
        feature_grad,
        jnp.stack([grad_project[:, n * width : (n + 1) * width] for n in range(3)]),
        grad_mix,
        own_sums[0:3],
        own_sums[3:7],
        own_sums[7:11],
        grad_cquery,
        grad_cout,
        jnp.stack([part.T for part in grad_image]),
        own_sums[11:14],
        jnp.stack([query[4].T, text[4].T]),
        own_up_bias.T,
        jnp.stack([query[5], text[5]]),
        own_sums[14:16],
    )


def solution(mesh):
    dp, pair = mesh.devices.shape
    fine = Mesh(mesh.devices.reshape(dp // 4, 2, 2, pair), AXES)
    first, second, third = P(AXES), P(None, AXES), P(None, None, AXES)
    in_specs = (
        first, first, first, first,
        second, first, second, second, second, first, first,
        third, second, third, second, second, second,
    )
    out_specs = (
        first, first, first,
        second, first, second, second, second, first, first,
        third, second, third, second, second, second,
    )
    return jax.shard_map(shards, mesh=fine, in_specs=in_specs, out_specs=out_specs, check_vma=False)
```

```python
import functools

import jax
import jax.numpy as jnp
from jax import lax
from jax.experimental import pallas as pl
from jax.experimental.pallas import tpu as pltpu
from jax.sharding import Mesh, PartitionSpec as P

HEAD = 64
NQ = 32
GROUP = 256
PER = GROUP // HEAD
eps = 1e-06
masked_off = 1000000000.0
AXES = ("z", "x", "c", "y")
BF = jnp.bfloat16
F32 = jnp.float32


def coords(index):
    return (index // 8, index // 4 % 2, index // 2 % 2, index % 2)


def pairs(count, move):
    result = []
    for source in range(count):
        z, x, c, y = move(*coords(source))
        result.append((source, ((z * 2 + x) * 2 + c) * 2 + y))
    return result


def step_a(z, x, c, y):
    return (z, x ^ 1, c, y) if c == 0 else (z, x, c, y ^ 1)


def step_b(z, x, c, y):
    return (z, x, c, y ^ 1) if c == 0 else (z, x ^ 1, c, y)


def step_c(z, x, c, y):
    return (z, x, c ^ 1, y)


def swap(value, move):
    count = lax.axis_size(AXES)
    return lax.ppermute(value, AXES, pairs(count, move))


def swap_z(value, distance):
    return swap(value, lambda z, x, c, y: (z ^ distance, x, c, y))


def gather_z(unit):
    if lax.axis_size("z") == 4:
        return [unit] + [swap_z(unit, k) for k in (1, 2, 3)]
    return [lax.all_gather(unit, "z", axis=0, tiled=True)]


def gather_all(unit):
    near = jnp.concatenate(gather_z(unit), axis=0)
    a = swap(near, step_a)
    b = [swap(near, step_b), swap(a, step_b)]
    pieces = [near, a] + b
    return pieces + [swap(piece, step_c) for piece in pieces]


def gather_plane(rows):
    for move in (step_a, step_b):
        rows = jnp.concatenate([rows, swap(rows, move)], axis=0)
    return [rows, swap(rows, step_c)]


def scatter_plane(kept, sent):
    for move in (step_c, step_b):
        total = kept.astype(F32) + swap(sent, move).astype(F32)
        half = total.shape[0] // 2
        kept, sent = total[:half], total[half:].astype(BF)
    return kept, swap(sent, step_a)


def scatter_z(blocks):
    if lax.axis_size("z") == 4:
        total = blocks[0].astype(F32)
        for k in (1, 2, 3):
            total = total + swap_z(blocks[k].astype(BF), k).astype(F32)
        return total
    low = jnp.concatenate(blocks, axis=0).astype(BF)
    return lax.psum_scatter(low, "z", scatter_dimension=0, tiled=True).astype(F32)


def scatter_all(kept, sent):
    kept, received = scatter_plane(kept, sent)
    total = kept.astype(F32) + received.astype(F32)
    planes = lax.axis_size("z")
    each = total.shape[0] // planes
    return scatter_z([total[k * each : (k + 1) * each] for k in range(planes)])


def slot_owner(count):
    z, x, c, y = (lax.axis_index(name) for name in AXES)
    planes = count // 8
    slot = jnp.arange(count)
    k = slot % planes
    alpha = slot // planes % 2
    beta = slot // (2 * planes) % 2
    core = c ^ (slot // (4 * planes))
    flip_x = jnp.where(core == 0, alpha, beta)
    flip_y = jnp.where(core == 0, beta, alpha)
    plane = (z ^ k) if planes == 4 else k
    return ((plane * 2 + (x ^ flip_x)) * 2 + core) * 2 + (y ^ flip_y)


def place_of_slot(width):
    count = lax.axis_size(AXES)
    each = width // count
    source = (slot_owner(count)[:, None] * each + jnp.arange(each)[None, :]).reshape(-1)
    return (source[:, None] == jnp.arange(width)[None, :]).astype(BF)


def by_slot(values, order):
    return dot_t(values, order).astype(BF)


def by_slot_turned(values, order):
    return dot_t(order, values).astype(BF)


def by_place(values, order):
    return dot(values.astype(BF), order)


def dot(left, right):
    return lax.dot_general(
        left, right, (((left.ndim - 1,), (0,)), ((), ())), preferred_element_type=F32
    )


def dot_t(left, right):
    return lax.dot_general(
        left, right, (((left.ndim - 1,), (1,)), ((), ())), preferred_element_type=F32
    )


def outer(left, right):
    lead = tuple(range(left.ndim - 1))
    return lax.dot_general(left, right, ((lead, lead), ((), ())), preferred_element_type=F32)


def column_sum(values):
    return jnp.sum(values.astype(F32), axis=0, keepdims=True)


def layer_norm(values, scale, shift):
    center = values - jnp.mean(values, axis=-1, keepdims=True)
    spread = jnp.mean(center * center, axis=-1, keepdims=True)
    return center * lax.rsqrt(spread + eps) * scale + shift


def norm_back(values, scale, gradient):
    center = values - jnp.mean(values, axis=-1, keepdims=True)
    spread = jnp.mean(center * center, axis=-1, keepdims=True)
    inverse = lax.rsqrt(spread + eps)
    normal = center * inverse
    inner = gradient * scale
    result = inverse * (
        inner
        - jnp.mean(inner, axis=-1, keepdims=True)
        - normal * jnp.mean(inner * normal, axis=-1, keepdims=True)
    )
    return result, column_sum(gradient * normal), column_sum(gradient)


def gelu_parts(values):
    half = F32(0.5) + F32(0.5) * lax.erf(values * F32(0.5**0.5))
    return half


def gelu_slope(values):
    density = jnp.exp(values * values * F32(-0.5)) * F32((2.0 * 3.141592653589793) ** -0.5)
    return gelu_parts(values) + values * density


def head_masks():
    lane = lax.broadcasted_iota(jnp.int32, (1, GROUP), 1) // HEAD
    return [(lane == h).astype(F32).astype(BF) for h in range(PER)]


def spread_heads(rows, masks):
    return jnp.concatenate([rows * mask for mask in masks], axis=0)


def fold_heads(stacked, masks, count):
    total = None
    for h, mask in enumerate(masks):
        part = stacked[h * count : (h + 1) * count] * mask.astype(F32)
        total = part if total is None else total + part
    return total


def softmax_rows(scores):
    shifted = jnp.exp(scores - jnp.max(scores, axis=-1, keepdims=True))
    return shifted / jnp.sum(shifted, axis=-1, keepdims=True)


def self_mask(length, rows):
    shape = (PER * rows, rows)
    row = lax.broadcasted_iota(jnp.int32, shape, 0) % rows
    col = lax.broadcasted_iota(jnp.int32, shape, 1)
    allowed = (col < NQ) | ((row >= NQ) & (col <= row) & (col - NQ < length))
    return jnp.where(allowed, F32(0.0), F32(-masked_off))


def attend_group_back(q, k, v, mask_add, grad, masks, count):
    q = spread_heads(q, masks)
    grad = spread_heads(grad, masks)
    weights = softmax_rows(dot_t(q, k) * HEAD ** (-0.5) + mask_add)
    grad_value = outer(weights.astype(BF), grad).astype(BF)
    grad_weight = dot_t(grad, v)
    grad_score = (
        weights * (grad_weight - jnp.sum(grad_weight * weights, axis=-1, keepdims=True))
    ).astype(BF)
    grad_query = fold_heads(dot(grad_score, k), masks, count) * HEAD ** (-0.5)
    grad_key = outer(grad_score, q) * HEAD ** (-0.5)
    return grad_query.astype(BF), grad_key.astype(BF), grad_value


def fetch(pieces, start, target, sems):
    width = target.shape[1]
    copies = []
    row = 0
    for n, piece in enumerate(pieces):
        count = piece.shape[0]
        source = piece.at[:, pl.ds(start, width)]
        copies.append(
            pltpu.make_async_copy(source, target.at[pl.ds(row, count)], sems.at[n])
        )
        row += count
    for copy in copies:
        copy.start()
    return copies


def finish(copies):
    for copy in copies:
        copy.wait()


def self_forward_kernel(items, n_pieces, refs):
    length_ref, hidden_ref, order_ref = refs[:3]
    pieces = refs[3 : 3 + n_pieces]
    qkv_ref, mix_ref, pre_ref, query_ref, text_ref, low_ref, vec_ref, w_ref, sems = refs[
        3 + n_pieces :
    ]
    rows_all, width = hidden_ref.shape
    copies = fetch(pieces, 0, w_ref, sems)
    order = order_ref[...]
    hidden_slot = by_slot(hidden_ref[...], order)
    finish(copies)
    vec = outer(w_ref[:, pl.ds(4 * width, 128)], order)[: vec_ref.shape[0]]
    vec_ref[...] = vec
    bias = [vec[0:1], F32(0.0), vec[1:2]]
    for n in range(3):
        cols = pl.ds(n * width, width)
        qkv_ref[:, cols] = (dot(hidden_slot, w_ref[:, cols]) + bias[n]).astype(BF)
    masks = head_masks()
    count = rows_all // items
    for i in range(items):
        rows = pl.ds(i * count, count)
        mask_add = self_mask(length_ref[i], count)
        for g in range(width // GROUP):
            cols = [pl.ds(n * width + g * GROUP, GROUP) for n in range(3)]
            q = spread_heads(qkv_ref[rows, cols[0]], masks)
            scores = dot_t(q, qkv_ref[rows, cols[1]]) * HEAD ** (-0.5) + mask_add
            weights = softmax_rows(scores).astype(BF)
            mixed = dot(weights, qkv_ref[rows, cols[2]])
            mix_ref[rows, cols[0]] = fold_heads(mixed, masks, count).astype(BF)
    mixture_slot = by_slot(mix_ref[...], order)
    pre = dot(mixture_slot, w_ref[:, pl.ds(3 * width, width)])
    pre = pre + vec[2:3] + hidden_ref[...].astype(F32)
    pre_ref[...] = pre
    first = layer_norm(pre, vec[3:4], vec[7:8])
    text = count - NQ
    for i in range(items):
        query_ref[pl.ds(i * NQ, NQ), :] = first[i * count : i * count + NQ]
        part = first[i * count + NQ : (i + 1) * count]
        text_ref[pl.ds(i * text, text), :] = part
        low_ref[pl.ds(i * text, text), :] = part.astype(BF)


def image_kernel(n_pieces, refs):
    feature_ref, order_ref, vec_ref = refs[:3]
    pieces = refs[3 : 3 + n_pieces]
    key_ref, value_ref, w_ref, sems = refs[3 + n_pieces :]
    items, _, image_width = feature_ref.shape
    copies = fetch(pieces, 0, w_ref, sems)
    order = order_ref[...]
    bias_slot = dot_t(vec_ref[...].astype(BF), order)[12:13]
    finish(copies)
    for i in range(items):
        rows = feature_ref[i]
        keys = dot_t(rows, w_ref[:, pl.ds(0, image_width)])
        key_ref[i] = by_place(keys, order).astype(BF)
        values = dot_t(rows, w_ref[:, pl.ds(image_width, image_width)]) + bias_slot
        value_ref[i] = by_place(values, order).astype(BF)


def cross_forward_kernel(start, n_pieces, refs):
    first_ref, key_ref, value_ref, order_ref, vec_ref = refs[:5]
    pieces = refs[5 : 5 + n_pieces]
    rows_ref, look_ref, pre_ref, second_ref, low_ref, w_ref, sems = refs[5 + n_pieces :]
    copies = fetch(pieces, start, w_ref, sems)
    items = key_ref.shape[0]
    width = first_ref.shape[1]
    count = first_ref.shape[0] // items
    order = order_ref[...]
    vec = vec_ref[...]
    masks = head_masks()
    first_slot = by_slot(first_ref[...].astype(BF), order)
    finish(copies)
    rows_ref[...] = (dot(first_slot, w_ref[:, pl.ds(0, width)]) + vec[11:12]).astype(BF)
    for i in range(items):
        rows = pl.ds(i * count, count)
        for g in range(width // GROUP):
            cols = pl.ds(g * GROUP, GROUP)
            q = spread_heads(rows_ref[rows, cols], masks)
            scores = dot_t(q, key_ref[i, :, cols]) * HEAD ** (-0.5)
            mixed = dot(softmax_rows(scores).astype(BF), value_ref[i, :, cols])
            look_ref[rows, cols] = fold_heads(mixed, masks, count).astype(BF)
    pre = dot(by_slot(look_ref[...], order), w_ref[:, pl.ds(width, width)])
    pre = pre + vec[13:14] + first_ref[...]
    pre_ref[...] = pre
    second = layer_norm(pre, vec[4:5], vec[8:9])
    second_ref[...] = second
    low_ref[...] = second.astype(BF)


def branch_up_kernel(branch, n_pieces, refs):
    low_refs, bias_ref = refs[:2], refs[2]
    pieces = refs[3 : 3 + n_pieces]
    pre_ref, act_ref, kept_ref, sent_ref, w_ref, sems = refs[3 + n_pieces :]
    half, width = low_refs[0].shape
    copies = fetch(pieces, branch * 2 * width, w_ref, sems)
    finish(copies)
    for n, (low_ref, out_ref) in enumerate(zip(low_refs, (kept_ref, sent_ref))):
        rows = pl.ds(n * half, half)
        pre = dot_t(low_ref[...], w_ref[:, pl.ds(0, width)]) + bias_ref[...]
        pre_ref[rows, :] = pre
        active = (pre * gelu_parts(pre)).astype(BF)
        act_ref[rows, :] = active
        out_ref[...] = dot(active, w_ref[:, pl.ds(width, width)]).astype(out_ref.dtype)


def branch_end_kernel(branch, refs):
    kept_ref, got_ref, value_ref, cot_ref, vec_ref = refs[:5]
    out_ref, grad_ref, low_ref, sum_ref = refs[5:]
    items, count, _ = cot_ref.shape
    vec = vec_ref[...]
    gain, shift = vec[5 + branch : 6 + branch], vec[9 + branch : 10 + branch]
    total = kept_ref[...] + got_ref[...].astype(F32)
    total = total + vec[14 + branch : 15 + branch] + value_ref[...]
    start, size = (NQ, count - NQ) if branch else (0, NQ)
    cot = jnp.concatenate([cot_ref[i, start : start + size, :] for i in range(items)], axis=0)
    out_ref[...] = layer_norm(total, gain, shift).astype(BF)
    grad, gain_grad, shift_grad = norm_back(total, gain, cot.astype(F32))
    grad_ref[...] = grad
    low = grad.astype(BF)
    low_ref[...] = low
    sum_ref[0:1, :] = gain_grad
    sum_ref[1:2, :] = shift_grad
    sum_ref[2:3, :] = column_sum(low)


def branch_down_kernel(branch, n_pieces, n_blocks, refs):
    grad_refs, low_refs, (pre_ref, act_ref) = refs[:2], refs[2:4], refs[4:6]
    pieces = refs[6 : 6 + n_pieces]
    rest = refs[6 + n_pieces :]
    kept_ref, sent_ref = rest[:2]
    block_refs = rest[2 : 2 + n_blocks]
    w_ref, sems = rest[2 + n_blocks :]
    half, width = low_refs[0].shape
    copies = fetch(pieces, branch * 2 * width, w_ref, sems)
    finish(copies)
    grads = []
    for n, out_ref in enumerate((kept_ref, sent_ref)):
        rows = pl.ds(n * half, half)
        back = dot_t(grad_refs[n][...], w_ref[:, pl.ds(width, width)])
        grad_pre = (gelu_slope(pre_ref[rows, :]) * back).astype(BF)
        grads.append(grad_pre)
        out_ref[...] = dot(grad_pre, w_ref[:, pl.ds(0, width)]).astype(out_ref.dtype)
    grad_pre = jnp.concatenate(grads, axis=0)
    low = jnp.concatenate([ref[...] for ref in low_refs], axis=0)
    grad_low = jnp.concatenate([ref[...] for ref in grad_refs], axis=0)
    up = outer(grad_pre, low).astype(BF)
    down = outer(act_ref[...], grad_low).astype(BF)
    sums = outer(grad_pre, jnp.ones((2 * half, 128), BF)).astype(BF)
    row = 0
    for block_ref in block_refs:
        size = block_ref.shape[0]
        block_ref[:, pl.ds(0, width)] = up[row : row + size]
        block_ref[:, pl.ds(width, width)] = down[row : row + size]
        block_ref[:, pl.ds(2 * width, 128)] = sums[row : row + size]
        row += size


def cross_backward_kernel(start, n_pieces, refs):
    kept_ref, got_ref, sum_ref, pre_ref, q_ref, k_ref, v_ref, order_ref, vec_ref = refs[:9]
    pieces = refs[9 : 9 + n_pieces]
    dq_ref, dk_ref, dv_ref, low_ref, first_ref, row_ref, w_ref, sems = refs[9 + n_pieces :]
    copies = fetch(pieces, start, w_ref, sems)
    items = k_ref.shape[0]
    width = q_ref.shape[1]
    count = q_ref.shape[0] // items
    order = order_ref[...]
    vec = vec_ref[...]
    masks = head_masks()
    gradient = kept_ref[...] + got_ref[...].astype(F32) + sum_ref[...]
    grad_two, gain_grad, shift_grad = norm_back(pre_ref[...], vec[4:5], gradient)
    low = grad_two.astype(BF)
    low_ref[...] = low
    finish(copies)
    looked = by_place(dot_t(low, w_ref[:, pl.ds(width, width)]), order).astype(BF)
    value_sum = []
    for g in range(width // GROUP):
        cols = pl.ds(g * GROUP, GROUP)
        total = None
        for i in range(items):
            rows = pl.ds(i * count, count)
            dq, dk, dv = attend_group_back(
                q_ref[rows, cols],
                k_ref[i, :, cols],
                v_ref[i, :, cols],
                F32(0.0),
                looked[i * count : (i + 1) * count, g * GROUP : (g + 1) * GROUP],
                masks,
                count,
            )
            dq_ref[rows, cols] = dq
            dk_ref[i, :, cols] = dk
            dv_ref[i, :, cols] = dv
            part = column_sum(dv)
            total = part if total is None else total + part
        value_sum.append(total)
    grad_cross = dq_ref[...]
    back = dot_t(grad_cross, w_ref[:, pl.ds(0, width)])
    first_ref[...] = grad_two + by_place(back, order)
    row_ref[0:1, :] = gain_grad
    row_ref[1:2, :] = shift_grad
    row_ref[2:3, :] = column_sum(grad_cross)
    row_ref[3:4, :] = jnp.concatenate(value_sum, axis=1)
    row_ref[4:5, :] = column_sum(low)


def cross_weights_kernel(refs):
    dq_ref, dk_ref, dv_ref, low_ref, first_ref, look_ref, feature_ref, order_ref = refs[:8]
    kept_ref, sent_ref = refs[8:]
    items, _, image_width = feature_ref.shape
    half, width = order_ref.shape[0] // 2, order_ref.shape[1]
    for part, out_ref in enumerate((kept_ref, sent_ref)):
        order = order_ref[pl.ds(part * half, half), :]
        for n, grad_ref in enumerate((dk_ref, dv_ref)):
            total = None
            for i in range(items):
                turned = by_slot_turned(grad_ref[i], order)
                product = dot(turned, feature_ref[i])
                total = product if total is None else total + product
            out_ref[:, pl.ds(n * image_width, image_width)] = total.astype(BF)
        start = 2 * image_width
        turned = by_slot_turned(first_ref[...].astype(BF), order)
        out_ref[:, pl.ds(start, width)] = dot(turned, dq_ref[...]).astype(BF)
        turned = by_slot_turned(look_ref[...], order)
        out_ref[:, pl.ds(start + width, width)] = dot(turned, low_ref[...]).astype(BF)


def feature_kernel(n_pieces, refs):
    dk_ref, dv_ref, order_ref = refs[:3]
    pieces = refs[3 : 3 + n_pieces]
    out_ref, w_ref, sems = refs[3 + n_pieces :]
    items, _, image_width = out_ref.shape
    copies = fetch(pieces, 0, w_ref, sems)
    order = order_ref[...]
    slots = [[by_slot(ref[i], order) for ref in (dk_ref, dv_ref)] for i in range(items)]
    finish(copies)
    for i in range(items):
        total = dot(slots[i][0], w_ref[:, pl.ds(0, image_width)])
        out_ref[i] = total + dot(slots[i][1], w_ref[:, pl.ds(image_width, image_width)])


def self_backward_kernel(items, n_pieces, refs):
    length_ref, query_ref, kept_ref, got_ref, text_ref, pre_ref, qkv_ref = refs[:7]
    mix_ref, hidden_ref, order_ref, vec_ref = refs[7:11]
    row_refs = refs[11:14]
    pieces = refs[14 : 14 + n_pieces]
    grad_ref, one_ref, g_kept_ref, g_sent_ref, w_ref, sum_ref, sems = refs[14 + n_pieces :]
    copies = fetch(pieces, 3 * pre_ref.shape[1], w_ref, sems)
    rows_all, width = pre_ref.shape
    count = rows_all // items
    text = count - NQ
    order = order_ref[...]
    vec = vec_ref[...]
    masks = head_masks()
    text_grad = kept_ref[...] + got_ref[...].astype(F32) + text_ref[...]
    query_grad = query_ref[...]
    gradient = []
    for i in range(items):
        gradient.append(query_grad[i * NQ : (i + 1) * NQ])
        gradient.append(text_grad[i * text : (i + 1) * text])
    gradient = jnp.concatenate(gradient, axis=0)
    grad_one, gain_grad, shift_grad = norm_back(pre_ref[...], vec[3:4], gradient)
    one_ref[...] = grad_one
    low = grad_one.astype(BF)
    finish(copies)
    grad_mix = by_place(dot_t(low, w_ref[...]), order).astype(BF)
    sums = [None, None, None]
    for i in range(items):
        rows = pl.ds(i * count, count)
        mask_add = self_mask(length_ref[i], count)
        for g in range(width // GROUP):
            cols = [pl.ds(n * width + g * GROUP, GROUP) for n in range(3)]
            results = attend_group_back(
                *[qkv_ref[rows, col] for col in cols],
                mask_add,
                grad_mix[i * count : (i + 1) * count, g * GROUP : (g + 1) * GROUP],
                masks,
                count,
            )
            for col, value in zip(cols, results):
                grad_ref[rows, col] = value
    query_rows, query_ends, text_ends = row_refs
    sum_ref[...] = jnp.zeros(sum_ref.shape, F32)
    total = column_sum(grad_ref[...])
    listed = [
        total[:, :width],
        total[:, 2 * width :],
        column_sum(low),
        gain_grad,
        query_rows[0:1, :],
        query_ends[0:1, :],
        text_ends[0:1, :],
        shift_grad,
        query_rows[1:2, :],
        query_ends[1:2, :],
        text_ends[1:2, :],
        query_rows[2:3, :],
        query_rows[3:4, :],
        query_rows[4:5, :],
        query_ends[2:3, :],
        text_ends[2:3, :],
    ]
    for n, value in enumerate(listed):
        sum_ref[n : n + 1, :] = value
    sums = sum_ref[...].astype(BF)
    half = width // 2
    for part, out_ref in enumerate((g_kept_ref, g_sent_ref)):
        block = order_ref[pl.ds(part * half, half), :]
        turned = by_slot_turned(hidden_ref[...], block)
        for n in range(3):
            cols = pl.ds(n * width, width)
            out_ref[:, cols] = dot(turned, grad_ref[:, cols]).astype(BF)
        turned = by_slot_turned(mix_ref[...], block)
        out_ref[:, pl.ds(3 * width, width)] = dot(turned, low).astype(BF)
        out_ref[:, pl.ds(4 * width, 128)] = dot_t(block, sums).astype(BF)


def hidden_kernel(n_pieces, refs):
    grad_ref, one_ref, order_ref = refs[:3]
    pieces = refs[3 : 3 + n_pieces]
    out_ref, w_ref, sems = refs[3 + n_pieces :]
    copies = fetch(pieces, 0, w_ref, sems)
    finish(copies)
    back = dot_t(grad_ref[...], w_ref[...])
    out_ref[...] = one_ref[...] + by_place(back, order_ref[...])


def shaped(*dims, kind=F32):
    return jax.ShapeDtypeStruct(dims, kind)


def kernel_call(body, name, outs, inputs, pieces=(), loaded=None, lengths=None, extra=()):
    vmem = pl.BlockSpec(memory_space=pltpu.VMEM)
    specs = [vmem] * len(inputs) + [pl.BlockSpec(memory_space=pl.ANY)] * len(pieces)
    arrays = tuple(inputs) + tuple(pieces)
    if lengths is not None:
        specs = [pl.BlockSpec(memory_space=pltpu.SMEM)] + specs
        arrays = (lengths,) + arrays
    scratch = []
    if loaded is not None:
        rows = sum(piece.shape[0] for piece in pieces)
        scratch = [pltpu.VMEM((rows, loaded), BF)] + list(extra)
        scratch.append(pltpu.SemaphoreType.DMA((len(pieces),)))
    return pl.pallas_call(
        lambda *refs: body(refs),
        name=name,
        out_shape=outs,
        in_specs=specs,
        out_specs=jax.tree.map(lambda _: vmem, outs),
        scratch_shapes=scratch,
    )(*arrays)


def shards(
    hidden,
    features,
    text_lengths,
    cotangent,
    self_project,
    self_output,
    self_bias,
    norm_gain,
    norm_bias,
    cross_query,
    cross_output,
    image_project,
    cross_bias,
    expand_weight,
    expand_bias,
    reduce_weight,
    reduce_bias,
):
    part = functools.partial
    items, item_rows, width = hidden.shape
    each = self_output.shape[0]
    image_rows, image_width = features.shape[1:]
    ff_each = reduce_weight.shape[1]
    planes = lax.axis_size("z")
    rows = items * item_rows
    query_rows, text_rows = items * NQ, items * (item_rows - NQ)
    ff = planes * ff_each
    turns = ff_each // each
    order = place_of_slot(width)
    flat = hidden.reshape(rows, width)

    vectors = jnp.concatenate([self_bias, norm_gain, norm_bias, cross_bias, reduce_bias], axis=0)
    n_vectors = vectors.shape[0]
    up_bias = jnp.swapaxes(expand_bias.reshape(2 * turns, each), 0, 1)
    filler = jnp.zeros((each, 128 - n_vectors - 2 * turns), BF)
    unit_self = jnp.concatenate(
        [self_project[0], self_project[1], self_project[2], self_output]
        + [vectors.T, up_bias, filler],
        axis=1,
    )
    image_turned = jnp.swapaxes(image_project, 1, 2)
    unit_cross = jnp.concatenate(
        [image_turned[0], image_turned[1], cross_query, cross_output], axis=1
    )
    unit_ff = jnp.concatenate(
        [expand_weight[0].T, reduce_weight[0], expand_weight[1].T, reduce_weight[1]], axis=1
    )
    w_self = gather_all(unit_self)
    w_cross = gather_all(unit_cross)
    w_ff = gather_z(unit_ff)
    b_up = w_self[0][:, 4 * width + n_vectors : 4 * width + n_vectors + 2 * turns]
    b_up = b_up.reshape(planes, each, 2, turns).transpose(2, 0, 3, 1).reshape(2, 1, ff)
    b_up = b_up.astype(F32)
    cross_start = 2 * image_width

    qkv, mixture, pre_one, first_query, first_text, text_low, vec = kernel_call(
        part(self_forward_kernel, items, len(w_self)),
        "self_forward",
        (
            shaped(rows, 3 * width, kind=BF),
            shaped(rows, width, kind=BF),
            shaped(rows, width),
            shaped(query_rows, width),
            shaped(text_rows, width),
            shaped(text_rows, width, kind=BF),
            shaped(n_vectors, width),
        ),
        (flat, order),
        w_self,
        4 * width + 128,
        text_lengths,
    )

    wide = shaped(items, image_rows, width, kind=BF)
    image_keys, image_values = kernel_call(
        part(image_kernel, len(w_cross)),
        "image_rows",
        (wide, wide),
        (features, order, vec),
        w_cross,
        cross_start,
    )
    cross_rows, looked, pre_two, second, second_low = kernel_call(
        part(cross_forward_kernel, cross_start, len(w_cross)),
        "cross_forward",
        (
            shaped(query_rows, width, kind=BF),
            shaped(query_rows, width, kind=BF),
            shaped(query_rows, width),
            shaped(query_rows, width),
            shaped(query_rows, width, kind=BF),
        ),
        (first_query, image_keys, image_values, order, vec),
        w_cross,
        2 * width,
    )

    branches = [None, None]
    for j, values, low in ((1, first_text, text_low), (0, second, second_low)):
        count = values.shape[0]
        low_all = gather_plane(low)
        half = 4 * count
        pre_act, active, kept, sent = kernel_call(
            part(branch_up_kernel, j, len(w_ff)),
            "branch_up_%d" % j,
            (
                shaped(2 * half, ff),
                shaped(2 * half, ff, kind=BF),
                shaped(half, width),
                shaped(half, width, kind=BF),
            ),
            (*low_all, b_up[j]),
            w_ff,
            2 * width,
        )
        out, grad_sum, grad_low, ends = kernel_call(
            part(branch_end_kernel, j),
            "branch_end_%d" % j,
            (
                shaped(count, width, kind=BF),
                shaped(count, width),
                shaped(count, width, kind=BF),
                shaped(8, width),
            ),
            (*scatter_plane(kept, sent), values, cotangent, vec),
        )
        blocks = [ff // len(w_ff)] * len(w_ff)
        kept, sent, *grads = kernel_call(
            part(branch_down_kernel, j, len(w_ff), len(blocks)),
            "branch_down_%d" % j,
            (shaped(half, width), shaped(half, width, kind=BF))
            + tuple(shaped(size, 2 * width + 128, kind=BF) for size in blocks),
            (*gather_plane(grad_low), *low_all, pre_act, active),
            w_ff,
            2 * width,
        )
        branches[j] = (out, grad_sum, ends, scatter_plane(kept, sent), scatter_z(grads))
    query, text = branches
    layer_out = jnp.concatenate(
        [query[0].reshape(items, NQ, width), text[0].reshape(items, item_rows - NQ, width)],
        axis=1,
    )

    grad_cross, grad_ikey, grad_ivalue, two_low, grad_first, cross_ends = kernel_call(
        part(cross_backward_kernel, cross_start, len(w_cross)),
        "cross_backward",
        (
            shaped(query_rows, width, kind=BF),
            wide,
            wide,
            shaped(query_rows, width, kind=BF),
            shaped(query_rows, width),
            shaped(8, width),
        ),
        (*query[3], query[1], pre_two, cross_rows, image_keys, image_values, order, vec),
        w_cross,
        2 * width,
    )
    packed = shaped(width // 2, cross_start + 2 * width, kind=BF)
    own_cross = scatter_all(
        *kernel_call(
            cross_weights_kernel,
            "cross_weights",
            (packed, packed),
            (grad_cross, grad_ikey, grad_ivalue, two_low, first_query, looked, features, order),
        )
    )

    packed = shaped(width // 2, 4 * width + 128, kind=BF)
    grad_qkv, grad_one, kept, sent = kernel_call(
        part(self_backward_kernel, items, len(w_self)),
        "self_backward",
        (shaped(rows, 3 * width, kind=BF), shaped(rows, width), packed, packed),
        (
            grad_first,
            *text[3],
            text[1],
            pre_one,
            qkv,
            mixture,
            flat,
            order,
            vec,
            cross_ends,
            query[2],
            text[2],
        ),
        w_self,
        width,
        text_lengths,
        (pltpu.VMEM((128, width), F32),),
    )
    own_self = scatter_all(kept, sent)
    feature_grad = kernel_call(
        part(feature_kernel, len(w_cross)),
        "feature_grad",
        shaped(items, image_rows, image_width),
        (grad_ikey, grad_ivalue, order),
        w_cross,
        cross_start,
    )
    hidden_grad = kernel_call(
        part(hidden_kernel, len(w_self)),
        "hidden_grad",
        shaped(rows, width),
        (grad_qkv, grad_one, order),
        w_self,
        3 * width,
    )

    own_sums = own_self[:, 4 * width : 4 * width + n_vectors].T
    own_up = [branch[4][:, :width].T for branch in branches]
    own_down = [branch[4][:, width : 2 * width] for branch in branches]
    own_up_bias = [branch[4][:, 2 * width] for branch in branches]
    return (
        layer_out,
        hidden_grad.reshape(items, item_rows, width),
        feature_grad,
        jnp.stack([own_self[:, n * width : (n + 1) * width] for n in range(3)]),
        own_self[:, 3 * width : 4 * width],
        own_sums[0:3],
        own_sums[3:7],
        own_sums[7:11],
        own_cross[:, cross_start : cross_start + width],
        own_cross[:, cross_start + width :],
        jnp.stack([own_cross[:, n * image_width : (n + 1) * image_width].T for n in range(2)]),
        own_sums[11:14],
        jnp.stack(own_up),
        jnp.stack(own_up_bias),
        jnp.stack(own_down),
        own_sums[14:16],
    )


def solution(mesh):
    dp, pair = mesh.devices.shape
    fine = Mesh(mesh.devices.reshape(dp // 4, 2, 2, pair), AXES)
    first, second, third = P(AXES), P(None, AXES), P(None, None, AXES)
    in_specs = (
        first, first, first, first,
        second, first, second, second, second, first, first,
        third, second, third, second, second, second,
    )
    out_specs = (
        first, first, first,
        second, first, second, second, second, first, first,
        third, second, third, second, second, second,
    )
    return jax.shard_map(shards, mesh=fine, in_specs=in_specs, out_specs=out_specs, check_vma=False)
```

```python
import functools

import jax
import jax.numpy as jnp
from jax import lax
from jax.experimental import pallas as pl
from jax.experimental.pallas import tpu as pltpu
from jax.sharding import Mesh, PartitionSpec as P

HEAD = 64
NQ = 32
GROUP = 256
PER = GROUP // HEAD
eps = 1e-06
masked_off = 1000000000.0
AXES = ("z", "x", "c", "y")
BF = jnp.bfloat16
F32 = jnp.float32


def coords(index):
    return (index // 8, index // 4 % 2, index // 2 % 2, index % 2)


def pairs(count, move):
    result = []
    for source in range(count):
        z, x, c, y = move(*coords(source))
        result.append((source, ((z * 2 + x) * 2 + c) * 2 + y))
    return result


def step_a(z, x, c, y):
    return (z, x ^ 1, c, y) if c == 0 else (z, x, c, y ^ 1)


def step_b(z, x, c, y):
    return (z, x, c, y ^ 1) if c == 0 else (z, x ^ 1, c, y)


def step_c(z, x, c, y):
    return (z, x, c ^ 1, y)


def swap(value, move):
    count = lax.axis_size(AXES)
    return lax.ppermute(value, AXES, pairs(count, move))


def swap_z(value, distance):
    return swap(value, lambda z, x, c, y: (z ^ distance, x, c, y))


def gather_z(unit, *gates):
    if lax.axis_size("z") == 4:
        near = jnp.concatenate([unit, swap_z(unit, 2)], axis=0)
        near = after(near, *gates)
        return near, jnp.concatenate([near, swap_z(near, 1)], axis=0)
    near = lax.all_gather(unit, "z", axis=0, tiled=True)
    return near, near


def gather_all(near):
    a, b = swap(near, step_a), swap(near, step_b)
    pieces = [near, a, b, swap(a, step_b)]
    return pieces + [swap(piece, step_c) for piece in pieces]


def gather_plane(rows):
    for move in (step_a, step_b):
        rows = jnp.concatenate([rows, swap(rows, move)], axis=0)
    return [rows, swap(rows, step_c)]


def after(value, *earlier):
    return lax.optimization_barrier((value,) + earlier)[0]


def add_low(left, right):
    return (left.astype(F32) + right.astype(F32)).astype(BF)


def halved(kept, got):
    half = got.shape[0] // 2
    return add_low(kept[:half], got[:half]), add_low(kept[half:], got[half:])


def scatter_plane(kept, sent):
    for move in (step_c, step_b):
        kept, sent = halved(kept, swap(sent, move))
    return kept, swap(sent, step_a)


def step_z1(z, x, c, y):
    return (z ^ 1, x, c, y)


def step_z2(z, x, c, y):
    return (z ^ 2, x, c, y)


def scatter_rest(kept, got):
    return lax.psum_scatter(add_low(kept, got), "z", scatter_dimension=0, tiled=True).astype(F32)


def slot_owner(count):
    z, x, c, y = (lax.axis_index(name) for name in AXES)
    planes = count // 8
    slot = jnp.arange(count)
    k = slot % planes
    alpha = slot // planes % 2
    beta = slot // (2 * planes) % 2
    core = c ^ (slot // (4 * planes))
    flip_x = jnp.where(core == 0, alpha, beta)
    flip_y = jnp.where(core == 0, beta, alpha)
    plane = z ^ (k % 2 * 2 + k // 2) if planes == 4 else k
    return ((plane * 2 + (x ^ flip_x)) * 2 + core) * 2 + (y ^ flip_y)


def place_of_slot(width):
    count = lax.axis_size(AXES)
    each = width // count
    source = (slot_owner(count)[:, None] * each + jnp.arange(each)[None, :]).reshape(-1)
    return (source[:, None] == jnp.arange(width)[None, :]).astype(BF)


def by_slot(values, order):
    return dot_t(values, order).astype(BF)


def by_slot_turned(values, order):
    return dot_t(order, values).astype(BF)


def by_place(values, order):
    return dot(values.astype(BF), order)


def dot(left, right):
    return lax.dot_general(
        left, right, (((left.ndim - 1,), (0,)), ((), ())), preferred_element_type=F32
    )


def dot_t(left, right):
    return lax.dot_general(
        left, right, (((left.ndim - 1,), (1,)), ((), ())), preferred_element_type=F32
    )


def outer(left, right):
    lead = tuple(range(left.ndim - 1))
    return lax.dot_general(left, right, ((lead, lead), ((), ())), preferred_element_type=F32)


def column_sum(values):
    return jnp.sum(values.astype(F32), axis=0, keepdims=True)


def layer_norm(values, scale, shift):
    center = values - jnp.mean(values, axis=-1, keepdims=True)
    spread = jnp.mean(center * center, axis=-1, keepdims=True)
    return center * lax.rsqrt(spread + eps) * scale + shift


def norm_back(values, scale, gradient):
    center = values - jnp.mean(values, axis=-1, keepdims=True)
    spread = jnp.mean(center * center, axis=-1, keepdims=True)
    inverse = lax.rsqrt(spread + eps)
    normal = center * inverse
    inner = gradient * scale
    result = inverse * (
        inner
        - jnp.mean(inner, axis=-1, keepdims=True)
        - normal * jnp.mean(inner * normal, axis=-1, keepdims=True)
    )
    return result, column_sum(gradient * normal), column_sum(gradient)


def gelu_parts(values):
    half = F32(0.5) + F32(0.5) * lax.erf(values * F32(0.5**0.5))
    return half


def gelu_slope(values):
    density = jnp.exp(values * values * F32(-0.5)) * F32((2.0 * 3.141592653589793) ** -0.5)
    return gelu_parts(values) + values * density


def head_masks():
    lane = lax.broadcasted_iota(jnp.int32, (1, GROUP), 1) // HEAD
    return [(lane == h).astype(F32).astype(BF) for h in range(PER)]


def spread_heads(rows, masks):
    return jnp.concatenate([rows * mask for mask in masks], axis=0)


def fold_heads(stacked, masks, count):
    total = None
    for h, mask in enumerate(masks):
        part = stacked[h * count : (h + 1) * count] * mask.astype(F32)
        total = part if total is None else total + part
    return total


def softmax_rows(scores):
    shifted = jnp.exp(scores - jnp.max(scores, axis=-1, keepdims=True))
    return shifted / jnp.sum(shifted, axis=-1, keepdims=True)


def self_mask(length, rows):
    shape = (PER * rows, rows)
    row = lax.broadcasted_iota(jnp.int32, shape, 0) % rows
    col = lax.broadcasted_iota(jnp.int32, shape, 1)
    allowed = (col < NQ) | ((row >= NQ) & (col <= row) & (col - NQ < length))
    return jnp.where(allowed, F32(0.0), F32(-masked_off))


def attend_group_back(q, k, v, mask_add, grad, masks, count):
    q = spread_heads(q, masks)
    grad = spread_heads(grad, masks)
    weights = softmax_rows(dot_t(q, k) * HEAD ** (-0.5) + mask_add)
    grad_value = outer(weights.astype(BF), grad).astype(BF)
    grad_weight = dot_t(grad, v)
    grad_score = (
        weights * (grad_weight - jnp.sum(grad_weight * weights, axis=-1, keepdims=True))
    ).astype(BF)
    grad_query = fold_heads(dot(grad_score, k), masks, count) * HEAD ** (-0.5)
    grad_key = outer(grad_score, q) * HEAD ** (-0.5)
    return grad_query.astype(BF), grad_key.astype(BF), grad_value


def fetch(pieces, start, target, sems):
    width = target.shape[1]
    copies = []
    row = 0
    for n, piece in enumerate(pieces):
        count = piece.shape[0]
        source = piece.at[:, pl.ds(start, width)]
        copies.append(
            pltpu.make_async_copy(source, target.at[pl.ds(row, count)], sems.at[n])
        )
        row += count
    for copy in copies:
        copy.start()
    return copies


def finish(copies):
    for copy in copies:
        copy.wait()


def turned_rows(rows):
    rows = list(rows)
    each = rows[0].shape[1]
    rows.append(jnp.zeros((128 - sum(row.shape[0] for row in rows), each), F32))
    return jnp.concatenate(rows, axis=0).T.astype(BF)


def pack_kernel(refs):
    project_ref, output_ref, up_ref, down_ref, bias_ref = refs[:5]
    vector_refs, self_ref, ff_ref = refs[5:-2], refs[-2], refs[-1]
    width = output_ref.shape[1]
    for n in range(3):
        self_ref[:, pl.ds(n * width, width)] = project_ref[n]
    self_ref[:, pl.ds(3 * width, width)] = output_ref[...]
    vectors = turned_rows(ref[...].astype(F32) for ref in vector_refs)
    self_ref[:, pl.ds(4 * width, 128)] = vectors
    for n in range(2):
        start = n * (2 * width + 128)
        ff_ref[:, pl.ds(start, width)] = up_ref[n]
        ff_ref[:, pl.ds(start + width, width)] = down_ref[n]
        bias = bias_ref[n : n + 1, :].astype(F32)
        ff_ref[:, pl.ds(start + 2 * width, 128)] = turned_rows([bias])


def self_forward_kernel(items, n_pieces, refs):
    length_ref, hidden_ref, order_ref = refs[:3]
    pieces = refs[3 : 3 + n_pieces]
    qkv_ref, mix_ref, pre_ref, query_ref, text_ref, low_ref, vec_ref, w_ref, sems = refs[
        3 + n_pieces :
    ]
    rows_all, width = hidden_ref.shape
    copies = fetch(pieces, 0, w_ref, sems)
    order = order_ref[...]
    hidden_slot = by_slot(hidden_ref[...], order)
    finish(copies)
    vec = outer(w_ref[:, pl.ds(4 * width, 128)], order)[: vec_ref.shape[0]]
    vec_ref[...] = vec
    bias = [vec[0:1], F32(0.0), vec[1:2]]
    for n in range(3):
        cols = pl.ds(n * width, width)
        qkv_ref[:, cols] = (dot(hidden_slot, w_ref[:, cols]) + bias[n]).astype(BF)
    masks = head_masks()
    count = rows_all // items
    for i in range(items):
        rows = pl.ds(i * count, count)
        mask_add = self_mask(length_ref[i], count)
        for g in range(width // GROUP):
            cols = [pl.ds(n * width + g * GROUP, GROUP) for n in range(3)]
            q = spread_heads(qkv_ref[rows, cols[0]], masks)
            scores = dot_t(q, qkv_ref[rows, cols[1]]) * HEAD ** (-0.5) + mask_add
            weights = softmax_rows(scores).astype(BF)
            mixed = dot(weights, qkv_ref[rows, cols[2]])
            mix_ref[rows, cols[0]] = fold_heads(mixed, masks, count).astype(BF)
    mixture_slot = by_slot(mix_ref[...], order)
    pre = dot(mixture_slot, w_ref[:, pl.ds(3 * width, width)])
    pre = pre + vec[2:3] + hidden_ref[...].astype(F32)
    pre_ref[...] = pre
    first = layer_norm(pre, vec[3:4], vec[7:8])
    text = count - NQ
    for i in range(items):
        query_ref[pl.ds(i * NQ, NQ), :] = first[i * count : i * count + NQ]
        part = first[i * count + NQ : (i + 1) * count]
        text_ref[pl.ds(i * text, text), :] = part
        low_ref[pl.ds(i * text, text), :] = part.astype(BF)


def image_kernel(n_pieces, refs):
    feature_ref, order_ref, vec_ref = refs[:3]
    pieces = refs[3 : 3 + n_pieces]
    key_ref, value_ref, w_ref, sems = refs[3 + n_pieces :]
    items, _, image_width = feature_ref.shape
    copies = fetch(pieces, 0, w_ref, sems)
    order = order_ref[...]
    bias_slot = dot_t(vec_ref[...].astype(BF), order)[12:13]
    finish(copies)
    for i in range(items):
        rows = feature_ref[i]
        keys = dot_t(rows, w_ref[:, pl.ds(0, image_width)])
        key_ref[i] = by_place(keys, order).astype(BF)
        values = dot_t(rows, w_ref[:, pl.ds(image_width, image_width)]) + bias_slot
        value_ref[i] = by_place(values, order).astype(BF)


def cross_forward_kernel(start, n_pieces, refs):
    first_ref, key_ref, value_ref, order_ref, vec_ref = refs[:5]
    pieces = refs[5 : 5 + n_pieces]
    rows_ref, look_ref, pre_ref, second_ref, low_ref, w_ref, sems = refs[5 + n_pieces :]
    copies = fetch(pieces, start, w_ref, sems)
    items = key_ref.shape[0]
    width = first_ref.shape[1]
    count = first_ref.shape[0] // items
    order = order_ref[...]
    vec = vec_ref[...]
    masks = head_masks()
    first_slot = by_slot(first_ref[...].astype(BF), order)
    finish(copies)
    rows_ref[...] = (dot(first_slot, w_ref[:, pl.ds(0, width)]) + vec[11:12]).astype(BF)
    for i in range(items):
        rows = pl.ds(i * count, count)
        for g in range(width // GROUP):
            cols = pl.ds(g * GROUP, GROUP)
            q = spread_heads(rows_ref[rows, cols], masks)
            scores = dot_t(q, key_ref[i, :, cols]) * HEAD ** (-0.5)
            mixed = dot(softmax_rows(scores).astype(BF), value_ref[i, :, cols])
            look_ref[rows, cols] = fold_heads(mixed, masks, count).astype(BF)
    pre = dot(by_slot(look_ref[...], order), w_ref[:, pl.ds(width, width)])
    pre = pre + vec[13:14] + first_ref[...]
    pre_ref[...] = pre
    second = layer_norm(pre, vec[4:5], vec[8:9])
    second_ref[...] = second
    low_ref[...] = second.astype(BF)


def branch_up_kernel(branch, n_pieces, refs):
    low_refs = refs[:2]
    pieces = refs[2 : 2 + n_pieces]
    pre_ref, act_ref, kept_ref, sent_ref, w_ref, sems = refs[2 + n_pieces :]
    half, width = low_refs[0].shape
    copies = fetch(pieces, branch * (2 * width + 128), w_ref, sems)
    finish(copies)
    first_lane = (lax.broadcasted_iota(jnp.int32, (8, 128), 1) == 0).astype(F32).astype(BF)
    bias = dot_t(first_lane, w_ref[:, pl.ds(2 * width, 128)])[0:1]
    for n, (low_ref, out_ref) in enumerate(zip(low_refs, (kept_ref, sent_ref))):
        rows = pl.ds(n * half, half)
        pre = dot_t(low_ref[...], w_ref[:, pl.ds(0, width)]) + bias
        pre_ref[rows, :] = pre
        active = (pre * gelu_parts(pre)).astype(BF)
        act_ref[rows, :] = active
        out_ref[...] = dot(active, w_ref[:, pl.ds(width, width)]).astype(out_ref.dtype)


def branch_end_kernel(branch, refs):
    kept_ref, got_ref, value_ref, cot_ref, vec_ref = refs[:5]
    out_ref, grad_ref, low_ref, sum_ref = refs[5:]
    items, count, _ = cot_ref.shape
    vec = vec_ref[...]
    gain, shift = vec[5 + branch : 6 + branch], vec[9 + branch : 10 + branch]
    total = kept_ref[...].astype(F32) + got_ref[...].astype(F32)
    total = total + vec[14 + branch : 15 + branch] + value_ref[...]
    start, size = (NQ, count - NQ) if branch else (0, NQ)
    cot = jnp.concatenate([cot_ref[i, start : start + size, :] for i in range(items)], axis=0)
    out_ref[...] = layer_norm(total, gain, shift).astype(BF)
    grad, gain_grad, shift_grad = norm_back(total, gain, cot.astype(F32))
    grad_ref[...] = grad
    low = grad.astype(BF)
    low_ref[...] = low
    sum_ref[0:1, :] = gain_grad
    sum_ref[1:2, :] = shift_grad
    sum_ref[2:3, :] = column_sum(low)


def branch_down_kernel(branch, n_pieces, refs):
    grad_refs, low_refs, (pre_ref, act_ref) = refs[:2], refs[2:4], refs[4:6]
    pieces = refs[6 : 6 + n_pieces]
    rest = refs[6 + n_pieces :]
    kept_ref, sent_ref, own_ref, w_ref, sems = rest
    half, width = low_refs[0].shape
    copies = fetch(pieces, branch * (2 * width + 128), w_ref, sems)
    finish(copies)
    grads = []
    for n, out_ref in enumerate((kept_ref, sent_ref)):
        rows = pl.ds(n * half, half)
        back = dot_t(grad_refs[n][...], w_ref[:, pl.ds(width, width)])
        grad_pre = (gelu_slope(pre_ref[rows, :]) * back).astype(BF)
        grads.append(grad_pre)
        out_ref[...] = dot(grad_pre, w_ref[:, pl.ds(0, width)]).astype(out_ref.dtype)
    grad_pre = jnp.concatenate(grads, axis=0)
    low = jnp.concatenate([ref[...] for ref in low_refs], axis=0)
    grad_low = jnp.concatenate([ref[...] for ref in grad_refs], axis=0)
    own_ref[:, pl.ds(0, width)] = outer(grad_pre, low).astype(BF)
    own_ref[:, pl.ds(width, width)] = outer(act_ref[...], grad_low).astype(BF)
    sums = outer(grad_pre, jnp.ones((2 * half, 128), BF)).astype(BF)
    own_ref[:, pl.ds(2 * width, 128)] = sums


def cross_backward_kernel(start, n_pieces, refs):
    kept_ref, got_ref, sum_ref, pre_ref, q_ref, k_ref, v_ref, order_ref, vec_ref = refs[:9]
    pieces = refs[9 : 9 + n_pieces]
    dq_ref, dk_ref, dv_ref, low_ref, first_ref, row_ref, w_ref, sems = refs[9 + n_pieces :]
    copies = fetch(pieces, start, w_ref, sems)
    items = k_ref.shape[0]
    width = q_ref.shape[1]
    count = q_ref.shape[0] // items
    order = order_ref[...]
    vec = vec_ref[...]
    masks = head_masks()
    gradient = kept_ref[...].astype(F32) + got_ref[...].astype(F32) + sum_ref[...]
    grad_two, gain_grad, shift_grad = norm_back(pre_ref[...], vec[4:5], gradient)
    low = grad_two.astype(BF)
    low_ref[...] = low
    finish(copies)
    looked = by_place(dot_t(low, w_ref[:, pl.ds(width, width)]), order).astype(BF)
    value_sum = []
    for g in range(width // GROUP):
        cols = pl.ds(g * GROUP, GROUP)
        total = None
        for i in range(items):
            rows = pl.ds(i * count, count)
            dq, dk, dv = attend_group_back(
                q_ref[rows, cols],
                k_ref[i, :, cols],
                v_ref[i, :, cols],
                F32(0.0),
                looked[i * count : (i + 1) * count, g * GROUP : (g + 1) * GROUP],
                masks,
                count,
            )
            dq_ref[rows, cols] = dq
            dk_ref[i, :, cols] = dk
            dv_ref[i, :, cols] = dv
            part = column_sum(dv)
            total = part if total is None else total + part
        value_sum.append(total)
    grad_cross = dq_ref[...]
    back = dot_t(grad_cross, w_ref[:, pl.ds(0, width)])
    first_ref[...] = grad_two + by_place(back, order)
    row_ref[0:1, :] = gain_grad
    row_ref[1:2, :] = shift_grad
    row_ref[2:3, :] = column_sum(grad_cross)
    row_ref[3:4, :] = jnp.concatenate(value_sum, axis=1)
    row_ref[4:5, :] = column_sum(low)


def cross_weights_kernel(refs):
    dq_ref, dk_ref, dv_ref, low_ref, first_ref, look_ref, feature_ref, order_ref = refs[:8]
    kept_ref, sent_ref = refs[8:]
    items, _, image_width = feature_ref.shape
    half, width = order_ref.shape[0] // 2, order_ref.shape[1]
    for part, out_ref in enumerate((kept_ref, sent_ref)):
        order = order_ref[pl.ds(part * half, half), :]
        for n, grad_ref in enumerate((dk_ref, dv_ref)):
            total = None
            for i in range(items):
                turned = by_slot_turned(grad_ref[i], order)
                product = dot(turned, feature_ref[i])
                total = product if total is None else total + product
            out_ref[:, pl.ds(n * image_width, image_width)] = total.astype(BF)
        start = 2 * image_width
        turned = by_slot_turned(first_ref[...].astype(BF), order)
        out_ref[:, pl.ds(start, width)] = dot(turned, dq_ref[...]).astype(BF)
        turned = by_slot_turned(look_ref[...], order)
        out_ref[:, pl.ds(start + width, width)] = dot(turned, low_ref[...]).astype(BF)


def feature_kernel(n_pieces, refs):
    dk_ref, dv_ref, order_ref = refs[:3]
    pieces = refs[3 : 3 + n_pieces]
    out_ref, w_ref, sems = refs[3 + n_pieces :]
    items, _, image_width = out_ref.shape
    copies = fetch(pieces, 0, w_ref, sems)
    order = order_ref[...]
    slots = [[by_slot(ref[i], order) for ref in (dk_ref, dv_ref)] for i in range(items)]
    finish(copies)
    for i in range(items):
        total = dot(slots[i][0], w_ref[:, pl.ds(0, image_width)])
        out_ref[i] = total + dot(slots[i][1], w_ref[:, pl.ds(image_width, image_width)])


def self_backward_kernel(items, n_pieces, refs):
    length_ref, query_ref, kept_ref, got_ref, text_ref, pre_ref, qkv_ref = refs[:7]
    mix_ref, hidden_ref, order_ref, vec_ref = refs[7:11]
    row_refs = refs[11:14]
    pieces = refs[14 : 14 + n_pieces]
    grad_ref, one_ref, g_kept_ref, g_sent_ref, w_ref, sum_ref, sems = refs[14 + n_pieces :]
    copies = fetch(pieces, 3 * pre_ref.shape[1], w_ref, sems)
    rows_all, width = pre_ref.shape
    count = rows_all // items
    text = count - NQ
    order = order_ref[...]
    vec = vec_ref[...]
    masks = head_masks()
    text_grad = kept_ref[...].astype(F32) + got_ref[...].astype(F32) + text_ref[...]
    query_grad = query_ref[...]
    gradient = []
    for i in range(items):
        gradient.append(query_grad[i * NQ : (i + 1) * NQ])
        gradient.append(text_grad[i * text : (i + 1) * text])
    gradient = jnp.concatenate(gradient, axis=0)
    grad_one, gain_grad, shift_grad = norm_back(pre_ref[...], vec[3:4], gradient)
    one_ref[...] = grad_one
    low = grad_one.astype(BF)
    finish(copies)
    grad_mix = by_place(dot_t(low, w_ref[...]), order).astype(BF)
    sums = [None, None, None]
    for i in range(items):
        rows = pl.ds(i * count, count)
        mask_add = self_mask(length_ref[i], count)
        for g in range(width // GROUP):
            cols = [pl.ds(n * width + g * GROUP, GROUP) for n in range(3)]
            results = attend_group_back(
                *[qkv_ref[rows, col] for col in cols],
                mask_add,
                grad_mix[i * count : (i + 1) * count, g * GROUP : (g + 1) * GROUP],
                masks,
                count,
            )
            for col, value in zip(cols, results):
                grad_ref[rows, col] = value
    query_rows, query_ends, text_ends = row_refs
    sum_ref[...] = jnp.zeros(sum_ref.shape, F32)
    total = column_sum(grad_ref[...])
    listed = [
        total[:, :width],
        total[:, 2 * width :],
        column_sum(low),
        gain_grad,
        query_rows[0:1, :],
        query_ends[0:1, :],
        text_ends[0:1, :],
        shift_grad,
        query_rows[1:2, :],
        query_ends[1:2, :],
        text_ends[1:2, :],
        query_rows[2:3, :],
        query_rows[3:4, :],
        query_rows[4:5, :],
        query_ends[2:3, :],
        text_ends[2:3, :],
    ]
    for n, value in enumerate(listed):
        sum_ref[n : n + 1, :] = value
    sums = sum_ref[...].astype(BF)
    half = width // 2
    for part, out_ref in enumerate((g_kept_ref, g_sent_ref)):
        block = order_ref[pl.ds(part * half, half), :]
        turned = by_slot_turned(hidden_ref[...], block)
        for n in range(3):
            cols = pl.ds(n * width, width)
            out_ref[:, cols] = dot(turned, grad_ref[:, cols]).astype(BF)
        turned = by_slot_turned(mix_ref[...], block)
        out_ref[:, pl.ds(3 * width, width)] = dot(turned, low).astype(BF)
        out_ref[:, pl.ds(4 * width, 128)] = dot_t(block, sums).astype(BF)


def hidden_kernel(n_pieces, refs):
    grad_ref, one_ref, order_ref = refs[:3]
    pieces = refs[3 : 3 + n_pieces]
    out_ref, w_ref, sems = refs[3 + n_pieces :]
    copies = fetch(pieces, 0, w_ref, sems)
    finish(copies)
    back = dot_t(grad_ref[...], w_ref[...])
    out_ref[...] = one_ref[...] + by_place(back, order_ref[...])


def shaped(*dims, kind=F32):
    return jax.ShapeDtypeStruct(dims, kind)


def kernel_call(
    body, name, outs, inputs, pieces=(), loaded=None, lengths=None, extra=(), cost=8
):
    vmem = pl.BlockSpec(memory_space=pltpu.VMEM)
    specs = [vmem] * len(inputs) + [pl.BlockSpec(memory_space=pl.ANY)] * len(pieces)
    arrays = tuple(inputs) + tuple(pieces)
    if lengths is not None:
        specs = [pl.BlockSpec(memory_space=pltpu.SMEM)] + specs
        arrays = (lengths,) + arrays
    scratch = []
    if loaded is not None:
        rows = sum(piece.shape[0] for piece in pieces)
        scratch = [pltpu.VMEM((rows, loaded), BF)] + list(extra)
        scratch.append(pltpu.SemaphoreType.DMA((len(pieces),)))
    return pl.pallas_call(
        lambda *refs: body(refs),
        name=name,
        out_shape=outs,
        in_specs=specs,
        out_specs=jax.tree.map(lambda _: vmem, outs),
        scratch_shapes=scratch,
        cost_estimate=pl.CostEstimate(
            flops=cost * 900_000_000, bytes_accessed=cost * 3_000_000, transcendentals=0
        ),
    )(*arrays)


def shards(
    hidden,
    features,
    text_lengths,
    cotangent,
    self_project,
    self_output,
    self_bias,
    norm_gain,
    norm_bias,
    cross_query,
    cross_output,
    image_project,
    cross_bias,
    expand_weight,
    expand_bias,
    reduce_weight,
    reduce_bias,
):
    part = functools.partial
    items, item_rows, width = hidden.shape
    each = self_output.shape[0]
    image_rows, image_width = features.shape[1:]
    ff_each = reduce_weight.shape[1]
    planes = lax.axis_size("z")
    rows = items * item_rows
    query_rows, text_rows = items * NQ, items * (item_rows - NQ)
    ff = planes * ff_each
    order = place_of_slot(width)
    flat = hidden.reshape(rows, width)

    vectors = (self_bias, norm_gain, norm_bias, cross_bias, reduce_bias)
    n_vectors = sum(v.shape[0] for v in vectors)
    ff_width = 2 * width + 128
    up_turned = jnp.swapaxes(expand_weight, 1, 2)
    unit_self, unit_ff = kernel_call(
        pack_kernel,
        "pack",
        (shaped(each, 4 * width + 128, kind=BF), shaped(ff_each, 2 * ff_width, kind=BF)),
        (self_project, self_output, up_turned, reduce_weight, expand_bias, *vectors),
        cost=1,
    )
    image_turned = jnp.swapaxes(image_project, 1, 2)
    unit_cross = jnp.concatenate(
        [image_turned[0], image_turned[1], cross_query, cross_output], axis=1
    )
    w_ff = [lax.all_gather(unit_ff, "z", axis=0, tiled=True)]
    half_self, near_self = gather_z(unit_self)
    w_self = gather_all(near_self)
    near_cross = gather_z(after(unit_cross, half_self), near_self)[1]
    w_cross = gather_all(after(near_cross, w_self[1]))
    cross_start = 2 * image_width

    qkv, mixture, pre_one, first_query, first_text, text_low, vec = kernel_call(
        part(self_forward_kernel, items, len(w_self)),
        "self_forward",
        (
            shaped(rows, 3 * width, kind=BF),
            shaped(rows, width, kind=BF),
            shaped(rows, width),
            shaped(query_rows, width),
            shaped(text_rows, width),
            shaped(text_rows, width, kind=BF),
            shaped(n_vectors, width),
        ),
        (flat, order),
        w_self,
        4 * width + 128,
        text_lengths,
    )

    wide = shaped(items, image_rows, width, kind=BF)
    image_keys, image_values = kernel_call(
        part(image_kernel, len(w_cross)),
        "image_rows",
        (wide, wide),
        (features, order, vec),
        w_cross,
        cross_start,
    )
    cross_rows, looked, pre_two, second, second_low = kernel_call(
        part(cross_forward_kernel, cross_start, len(w_cross)),
        "cross_forward",
        (
            shaped(query_rows, width, kind=BF),
            shaped(query_rows, width, kind=BF),
            shaped(query_rows, width),
            shaped(query_rows, width),
            shaped(query_rows, width, kind=BF),
        ),
        (first_query, image_keys, image_values, order, vec),
        w_cross,
        2 * width,
    )

    branches = [None, None]
    for j, values, low in ((1, first_text, text_low), (0, second, second_low)):
        count = values.shape[0]
        low_all = gather_plane(low)
        half = 4 * count
        pre_act, active, kept, sent = kernel_call(
            part(branch_up_kernel, j, len(w_ff)),
            "branch_up_%d" % j,
            (
                shaped(2 * half, ff),
                shaped(2 * half, ff, kind=BF),
                shaped(half, width),
                shaped(half, width, kind=BF),
            ),
            low_all,
            w_ff,
            ff_width,
        )
        out, grad_sum, grad_low, ends = kernel_call(
            part(branch_end_kernel, j),
            "branch_end_%d" % j,
            (
                shaped(count, width, kind=BF),
                shaped(count, width),
                shaped(count, width, kind=BF),
                shaped(8, width),
            ),
            (*scatter_plane(kept, sent), values, cotangent, vec),
        )
        kept, sent, grads = kernel_call(
            part(branch_down_kernel, j, len(w_ff)),
            "branch_down_%d" % j,
            (
                shaped(half, width),
                shaped(half, width, kind=BF),
                shaped(ff, ff_width, kind=BF),
            ),
            (*gather_plane(grad_low), *low_all, pre_act, active),
            w_ff,
            2 * width,
        )
        own = lax.psum_scatter(grads, "z", scatter_dimension=0, tiled=True)
        branches[j] = (out, grad_sum, ends, scatter_plane(kept, sent), own)
    query, text = branches
    layer_out = jnp.concatenate(
        [query[0].reshape(items, NQ, width), text[0].reshape(items, item_rows - NQ, width)],
        axis=1,
    )

    query_got = after(query[3][1], text[3][1])
    grad_cross, grad_ikey, grad_ivalue, two_low, grad_first, cross_ends = kernel_call(
        part(cross_backward_kernel, cross_start, len(w_cross)),
        "cross_backward",
        (
            shaped(query_rows, width, kind=BF),
            wide,
            wide,
            shaped(query_rows, width, kind=BF),
            shaped(query_rows, width),
            shaped(8, width),
        ),
        (query[3][0], query_got, query[1], pre_two, cross_rows, image_keys, image_values, order, vec),
        w_cross,
        2 * width,
    )
    packed = shaped(width // 2, cross_start + 2 * width, kind=BF)
    cross_kept, cross_sent = kernel_call(
        cross_weights_kernel,
        "cross_weights",
        (packed, packed),
        (grad_cross, grad_ikey, grad_ivalue, two_low, first_query, looked, features, order),
        cost=13,
    )
    grad_first = after(grad_first, cross_sent)
    cross_kept, cross_sent = halved(cross_kept, swap(cross_sent, step_c))

    packed = shaped(width // 2, 4 * width + 128, kind=BF)
    grad_qkv, grad_one, kept, sent = kernel_call(
        part(self_backward_kernel, items, len(w_self)),
        "self_backward",
        (shaped(rows, 3 * width, kind=BF), shaped(rows, width), packed, packed),
        (
            grad_first,
            *text[3],
            text[1],
            pre_one,
            qkv,
            mixture,
            flat,
            order,
            vec,
            cross_ends,
            query[2],
            text[2],
        ),
        w_self,
        width,
        text_lengths,
        (pltpu.VMEM((128, width), F32),),
    )
    sent = after(sent, cross_sent)
    cross_got = swap(cross_sent, step_b)
    kept, sent = halved(kept, swap(sent, step_c))
    feature_order = after(order, sent)
    cross_got = after(cross_got, sent)
    cross_kept, cross_sent = halved(cross_kept, cross_got)
    hidden_order = after(order, cross_sent)
    got = after(swap(sent, step_b), cross_sent)
    kept, sent = halved(kept, got)
    cross_got = after(swap(cross_sent, step_a), sent)
    got = swap(sent, step_a)
    if planes == 4:
        cross_kept, cross_sent = halved(cross_kept, cross_got)
        got = after(got, cross_sent)
        kept, sent = halved(kept, got)
        cross_got = after(swap(cross_sent, step_z1), sent)
        cross_kept, cross_sent = halved(cross_kept, cross_got)
        got = after(swap(sent, step_z1), cross_sent)
        kept, sent = halved(kept, got)
        own_cross = cross_kept.astype(F32) + swap(cross_sent, step_z2).astype(F32)
        own_self = kept.astype(F32) + swap(sent, step_z2).astype(F32)
    else:
        own_cross = scatter_rest(cross_kept, cross_got)
        own_self = scatter_rest(kept, got)
    own_ff = [after(branch[4], sent).astype(F32) for branch in branches]
    feature_grad = kernel_call(
        part(feature_kernel, len(w_cross)),
        "feature_grad",
        shaped(items, image_rows, image_width),
        (grad_ikey, grad_ivalue, feature_order),
        w_cross,
        cross_start,
    )
    hidden_grad = kernel_call(
        part(hidden_kernel, len(w_self)),
        "hidden_grad",
        shaped(rows, width),
        (grad_qkv, grad_one, hidden_order),
        w_self,
        3 * width,
    )

    own_sums = own_self[:, 4 * width : 4 * width + n_vectors].T
    own_up = [own[:, :width].T for own in own_ff]
    own_down = [own[:, width : 2 * width] for own in own_ff]
    own_up_bias = [own[:, 2 * width] for own in own_ff]
    return (
        layer_out,
        hidden_grad.reshape(items, item_rows, width),
        feature_grad,
        jnp.stack([own_self[:, n * width : (n + 1) * width] for n in range(3)]),
        own_self[:, 3 * width : 4 * width],
        own_sums[0:3],
        own_sums[3:7],
        own_sums[7:11],
        own_cross[:, cross_start : cross_start + width],
        own_cross[:, cross_start + width :],
        jnp.stack([own_cross[:, n * image_width : (n + 1) * image_width].T for n in range(2)]),
        own_sums[11:14],
        jnp.stack(own_up),
        jnp.stack(own_up_bias),
        jnp.stack(own_down),
        own_sums[14:16],
    )


def solution(mesh):
    dp, pair = mesh.devices.shape
    fine = Mesh(mesh.devices.reshape(dp // 4, 2, 2, pair), AXES)
    first, second, third = P(AXES), P(None, AXES), P(None, None, AXES)
    in_specs = (
        first, first, first, first,
        second, first, second, second, second, first, first,
        third, second, third, second, second, second,
    )
    out_specs = (
        first, first, first,
        second, first, second, second, second, first, first,
        third, second, third, second, second, second,
    )
    return jax.shard_map(shards, mesh=fine, in_specs=in_specs, out_specs=out_specs, check_vma=False)
```

```python
import functools

import jax
import jax.numpy as jnp
from jax import lax
from jax.experimental import pallas as pl
from jax.experimental.pallas import tpu as pltpu
from jax.sharding import Mesh, PartitionSpec as P

HEAD = 64
NQ = 32
GROUP = 256
PER = GROUP // HEAD
eps = 1e-06
masked_off = 1000000000.0
LATE = 4
AXES = ("z", "x", "c", "y")
BF = jnp.bfloat16
F32 = jnp.float32


def coords(index):
    return (index // 8, index // 4 % 2, index // 2 % 2, index % 2)


def pairs(count, move):
    result = []
    for source in range(count):
        z, x, c, y = move(*coords(source))
        result.append((source, ((z * 2 + x) * 2 + c) * 2 + y))
    return result


def step_a(z, x, c, y):
    return (z, x ^ 1, c, y) if c == 0 else (z, x, c, y ^ 1)


def step_b(z, x, c, y):
    return (z, x, c, y ^ 1) if c == 0 else (z, x ^ 1, c, y)


def step_c(z, x, c, y):
    return (z, x, c ^ 1, y)


def swap(value, move):
    count = lax.axis_size(AXES)
    return lax.ppermute(value, AXES, pairs(count, move))


def swap_z(value, distance):
    return swap(value, lambda z, x, c, y: (z ^ distance, x, c, y))


def gather_z(unit):
    if lax.axis_size("z") == 4:
        near = jnp.concatenate([unit, swap_z(unit, 2)], axis=0)
        return jnp.concatenate([near, swap_z(near, 1)], axis=0)
    return lax.all_gather(unit, "z", axis=0, tiled=True)


def gather_z_direct(unit):
    if lax.axis_size("z") == 4:
        one, two, three = (swap_z(unit, k) for k in (1, 2, 3))
        return jnp.concatenate([unit, two, one, three], axis=0)
    return lax.all_gather(unit, "z", axis=0, tiled=True)


def gather_all(near, first=(), last=()):
    a = swap(after(near, *first), step_a)
    b = swap(after(near, *last), step_b)
    pieces = [near, a, b, swap(a, step_b)]
    pieces.append(swap(after(near, *last), step_c))
    return pieces + [swap(piece, step_c) for piece in pieces[1:3]]


def finish_all(pieces, *gates):
    return pieces + [swap(after(pieces[3], *gates), step_c)]


def gather_plane(rows, first=(), second=()):
    rows = jnp.concatenate([rows, after(swap(rows, step_a), *first)], axis=0)
    rows = jnp.concatenate([rows, after(swap(rows, step_b), *second)], axis=0)
    return [rows, swap(rows, step_c)]


def after(value, *earlier):
    return lax.optimization_barrier((value,) + earlier)[0]


def add_low(left, right):
    return (left.astype(F32) + right.astype(F32)).astype(BF)


def halved(kept, got):
    half = got.shape[0] // 2
    return add_low(kept[:half], got[:half]), add_low(kept[half:], got[half:])


def scatter_plane(kept, sent):
    for move in (step_c, step_b):
        kept, sent = halved(kept, swap(sent, move))
    return kept, swap(sent, step_a)


def step_z1(z, x, c, y):
    return (z ^ 1, x, c, y)


def step_z2(z, x, c, y):
    return (z ^ 2, x, c, y)


def scatter_rest(kept, got):
    return lax.psum_scatter(add_low(kept, got), "z", scatter_dimension=0, tiled=True).astype(F32)


def slot_owner(count):
    z, x, c, y = (lax.axis_index(name) for name in AXES)
    planes = count // 8
    slot = jnp.arange(count)
    k = slot % planes
    alpha = slot // planes % 2
    beta = slot // (2 * planes) % 2
    core = c ^ (slot // (4 * planes))
    flip_x = jnp.where(core == 0, alpha, beta)
    flip_y = jnp.where(core == 0, beta, alpha)
    plane = z ^ (k % 2 * 2 + k // 2) if planes == 4 else k
    return ((plane * 2 + (x ^ flip_x)) * 2 + core) * 2 + (y ^ flip_y)


def place_of_slot(width):
    count = lax.axis_size(AXES)
    each = width // count
    source = (slot_owner(count)[:, None] * each + jnp.arange(each)[None, :]).reshape(-1)
    return (source[:, None] == jnp.arange(width)[None, :]).astype(BF)


def by_slot(values, order):
    return dot_t(values, order).astype(BF)


def by_slot_turned(values, order):
    return dot_t(order, values).astype(BF)


def by_place(values, order):
    return dot(values.astype(BF), order)


def dot(left, right):
    return lax.dot_general(
        left, right, (((left.ndim - 1,), (0,)), ((), ())), preferred_element_type=F32
    )


def dot_t(left, right):
    return lax.dot_general(
        left, right, (((left.ndim - 1,), (1,)), ((), ())), preferred_element_type=F32
    )


def outer(left, right):
    lead = tuple(range(left.ndim - 1))
    return lax.dot_general(left, right, ((lead, lead), ((), ())), preferred_element_type=F32)


def column_sum(values):
    return jnp.sum(values.astype(F32), axis=0, keepdims=True)


def layer_norm(values, scale, shift):
    center = values - jnp.mean(values, axis=-1, keepdims=True)
    spread = jnp.mean(center * center, axis=-1, keepdims=True)
    return center * lax.rsqrt(spread + eps) * scale + shift


def norm_back(values, scale, gradient):
    center = values - jnp.mean(values, axis=-1, keepdims=True)
    spread = jnp.mean(center * center, axis=-1, keepdims=True)
    inverse = lax.rsqrt(spread + eps)
    normal = center * inverse
    inner = gradient * scale
    result = inverse * (
        inner
        - jnp.mean(inner, axis=-1, keepdims=True)
        - normal * jnp.mean(inner * normal, axis=-1, keepdims=True)
    )
    return result, column_sum(gradient * normal), column_sum(gradient)


def gelu_parts(values):
    half = F32(0.5) + F32(0.5) * lax.erf(values * F32(0.5**0.5))
    return half


def gelu_slope(values):
    density = jnp.exp(values * values * F32(-0.5)) * F32((2.0 * 3.141592653589793) ** -0.5)
    return gelu_parts(values) + values * density


def head_masks():
    lane = lax.broadcasted_iota(jnp.int32, (1, GROUP), 1) // HEAD
    return [(lane == h).astype(F32).astype(BF) for h in range(PER)]


def spread_heads(rows, masks):
    return jnp.concatenate([rows * mask for mask in masks], axis=0)


def fold_heads(stacked, masks, count):
    total = None
    for h, mask in enumerate(masks):
        part = stacked[h * count : (h + 1) * count] * mask.astype(F32)
        total = part if total is None else total + part
    return total


def softmax_rows(scores):
    shifted = jnp.exp(scores - jnp.max(scores, axis=-1, keepdims=True))
    return shifted / jnp.sum(shifted, axis=-1, keepdims=True)


def self_mask(length, rows):
    shape = (PER * rows, rows)
    row = lax.broadcasted_iota(jnp.int32, shape, 0) % rows
    col = lax.broadcasted_iota(jnp.int32, shape, 1)
    allowed = (col < NQ) | ((row >= NQ) & (col <= row) & (col - NQ < length))
    return jnp.where(allowed, F32(0.0), F32(-masked_off))


def attend_group_back(q, k, v, mask_add, grad, masks, count):
    q = spread_heads(q, masks)
    grad = spread_heads(grad, masks)
    weights = softmax_rows(dot_t(q, k) * HEAD ** (-0.5) + mask_add)
    grad_value = outer(weights.astype(BF), grad).astype(BF)
    grad_weight = dot_t(grad, v)
    grad_score = (
        weights * (grad_weight - jnp.sum(grad_weight * weights, axis=-1, keepdims=True))
    ).astype(BF)
    grad_query = fold_heads(dot(grad_score, k), masks, count) * HEAD ** (-0.5)
    grad_key = outer(grad_score, q) * HEAD ** (-0.5)
    return grad_query.astype(BF), grad_key.astype(BF), grad_value


def repeat(count, body):
    def step(i, carry):
        body(i)
        return carry

    lax.fori_loop(0, count, step, 0)


def stretch(i, count):
    return pl.ds(pl.multiple_of(i * count, count), count)


def fetch(pieces, start, target, sems):
    width = target.shape[1]
    copies = []
    row = 0
    for n, piece in enumerate(pieces):
        count = piece.shape[0]
        source = piece.at[:, pl.ds(start, width)]
        copies.append(
            pltpu.make_async_copy(source, target.at[pl.ds(row, count)], sems.at[n])
        )
        row += count
    for copy in copies:
        copy.start()
    return copies


def finish(copies):
    for copy in copies:
        copy.wait()


def turned_rows(rows):
    rows = list(rows)
    each = rows[0].shape[1]
    rows.append(jnp.zeros((128 - sum(row.shape[0] for row in rows), each), F32))
    return jnp.concatenate(rows, axis=0).T.astype(BF)


def pack_kernel(refs):
    project_ref, output_ref, up_ref, down_ref, bias_ref = refs[:5]
    vector_refs, self_ref, ff_ref = refs[5:-2], refs[-2], refs[-1]
    width = output_ref.shape[1]
    for n in range(3):
        self_ref[:, pl.ds(n * width, width)] = project_ref[n]
    self_ref[:, pl.ds(3 * width, width)] = output_ref[...]
    vectors = turned_rows(ref[...].astype(F32) for ref in vector_refs)
    self_ref[:, pl.ds(4 * width, 128)] = vectors
    for n in range(2):
        start = n * (2 * width + 128)
        ff_ref[:, pl.ds(start, width)] = up_ref[n]
        ff_ref[:, pl.ds(start + width, width)] = down_ref[n]
        bias = bias_ref[n : n + 1, :].astype(F32)
        ff_ref[:, pl.ds(start + 2 * width, 128)] = turned_rows([bias])


def self_forward_kernel(items, n_pieces, refs):
    length_ref, hidden_ref, order_ref = refs[:3]
    pieces = refs[3 : 3 + n_pieces]
    qkv_ref, mix_ref, pre_ref, query_ref, text_ref, low_ref, vec_ref, w_ref, sems = refs[
        3 + n_pieces :
    ]
    rows_all, width = hidden_ref.shape
    copies = fetch(pieces, 0, w_ref, sems)
    order = order_ref[...]
    hidden_slot = by_slot(hidden_ref[...], order)
    finish(copies)
    vec = outer(w_ref[:, pl.ds(4 * width, 128)], order)[: vec_ref.shape[0]]
    vec_ref[...] = vec
    bias = [vec[0:1], F32(0.0), vec[1:2]]
    for n in range(3):
        cols = pl.ds(n * width, width)
        qkv_ref[:, cols] = (dot(hidden_slot, w_ref[:, cols]) + bias[n]).astype(BF)
    masks = head_masks()
    count = rows_all // items

    def attend(i):
        rows = stretch(i, count)
        mask_add = self_mask(length_ref[i], count)
        for g in range(width // GROUP):
            cols = [pl.ds(n * width + g * GROUP, GROUP) for n in range(3)]
            q = spread_heads(qkv_ref[rows, cols[0]], masks)
            scores = dot_t(q, qkv_ref[rows, cols[1]]) * HEAD ** (-0.5) + mask_add
            weights = softmax_rows(scores).astype(BF)
            mixed = dot(weights, qkv_ref[rows, cols[2]])
            mix_ref[rows, cols[0]] = fold_heads(mixed, masks, count).astype(BF)

    repeat(items, attend)
    mixture_slot = by_slot(mix_ref[...], order)
    pre = dot(mixture_slot, w_ref[:, pl.ds(3 * width, width)])
    pre = pre + vec[2:3] + hidden_ref[...].astype(F32)
    pre_ref[...] = pre
    first = layer_norm(pre, vec[3:4], vec[7:8])
    text = count - NQ
    for i in range(items):
        query_ref[pl.ds(i * NQ, NQ), :] = first[i * count : i * count + NQ]
        part = first[i * count + NQ : (i + 1) * count]
        text_ref[pl.ds(i * text, text), :] = part
        low_ref[pl.ds(i * text, text), :] = part.astype(BF)


def image_kernel(n_pieces, refs):
    feature_ref, order_ref, vec_ref = refs[:3]
    pieces = refs[3 : 3 + n_pieces]
    key_ref, value_ref, w_ref, sems = refs[3 + n_pieces :]
    items, _, image_width = feature_ref.shape
    copies = fetch(pieces, 0, w_ref, sems)
    order = order_ref[...]
    bias_slot = dot_t(vec_ref[...].astype(BF), order)[12:13]
    finish(copies)

    def project(i):
        rows = feature_ref[i]
        keys = dot_t(rows, w_ref[:, pl.ds(0, image_width)])
        key_ref[i] = by_place(keys, order_ref[...]).astype(BF)
        values = dot_t(rows, w_ref[:, pl.ds(image_width, image_width)]) + bias_slot
        value_ref[i] = by_place(values, order_ref[...]).astype(BF)

    repeat(items, project)


def cross_forward_kernel(start, n_pieces, refs):
    first_ref, key_ref, value_ref, order_ref, vec_ref = refs[:5]
    pieces = refs[5 : 5 + n_pieces]
    rows_ref, look_ref, pre_ref, second_ref, low_ref, w_ref, sems = refs[5 + n_pieces :]
    copies = fetch(pieces, start, w_ref, sems)
    items = key_ref.shape[0]
    width = first_ref.shape[1]
    count = first_ref.shape[0] // items
    order = order_ref[...]
    vec = vec_ref[...]
    masks = head_masks()
    first_slot = by_slot(first_ref[...].astype(BF), order)
    finish(copies)
    rows_ref[...] = (dot(first_slot, w_ref[:, pl.ds(0, width)]) + vec[11:12]).astype(BF)

    def attend(i):
        rows = stretch(i, count)
        for g in range(width // GROUP):
            cols = pl.ds(g * GROUP, GROUP)
            q = spread_heads(rows_ref[rows, cols], masks)
            scores = dot_t(q, key_ref[i, :, cols]) * HEAD ** (-0.5)
            mixed = dot(softmax_rows(scores).astype(BF), value_ref[i, :, cols])
            look_ref[rows, cols] = fold_heads(mixed, masks, count).astype(BF)

    repeat(items, attend)
    pre = dot(by_slot(look_ref[...], order), w_ref[:, pl.ds(width, width)])
    pre = pre + vec[13:14] + first_ref[...]
    pre_ref[...] = pre
    second = layer_norm(pre, vec[4:5], vec[8:9])
    second_ref[...] = second
    low_ref[...] = second.astype(BF)


def branch_up_kernel(branch, n_pieces, refs):
    low_refs = refs[:2]
    pieces = refs[2 : 2 + n_pieces]
    pre_ref, act_ref, kept_ref, sent_ref, w_ref, sems = refs[2 + n_pieces :]
    half, width = low_refs[0].shape
    copies = fetch(pieces, branch * (2 * width + 128), w_ref, sems)
    finish(copies)
    first_lane = (lax.broadcasted_iota(jnp.int32, (8, 128), 1) == 0).astype(F32).astype(BF)
    bias = dot_t(first_lane, w_ref[:, pl.ds(2 * width, 128)])[0:1]
    for n, (low_ref, out_ref) in enumerate(zip(low_refs, (kept_ref, sent_ref))):
        rows = pl.ds(n * half, half)
        pre = dot_t(low_ref[...], w_ref[:, pl.ds(0, width)]) + bias
        pre_ref[rows, :] = pre
        active = (pre * gelu_parts(pre)).astype(BF)
        act_ref[rows, :] = active
        out_ref[...] = dot(active, w_ref[:, pl.ds(width, width)]).astype(out_ref.dtype)


def branch_end_kernel(branch, refs):
    kept_ref, got_ref, value_ref, cot_ref, vec_ref = refs[:5]
    out_ref, grad_ref, low_ref, sum_ref = refs[5:]
    items, count, _ = cot_ref.shape
    vec = vec_ref[...]
    gain, shift = vec[5 + branch : 6 + branch], vec[9 + branch : 10 + branch]
    total = kept_ref[...].astype(F32) + got_ref[...].astype(F32)
    total = total + vec[14 + branch : 15 + branch] + value_ref[...]
    start, size = (NQ, count - NQ) if branch else (0, NQ)
    cot = jnp.concatenate([cot_ref[i, start : start + size, :] for i in range(items)], axis=0)
    out_ref[...] = layer_norm(total, gain, shift).astype(BF)
    grad, gain_grad, shift_grad = norm_back(total, gain, cot.astype(F32))
    grad_ref[...] = grad
    low = grad.astype(BF)
    low_ref[...] = low
    sum_ref[0:1, :] = gain_grad
    sum_ref[1:2, :] = shift_grad
    sum_ref[2:3, :] = column_sum(low)


def branch_down_kernel(branch, n_pieces, refs):
    grad_refs, low_refs, (pre_ref, act_ref) = refs[:2], refs[2:4], refs[4:6]
    pieces = refs[6 : 6 + n_pieces]
    rest = refs[6 + n_pieces :]
    kept_ref, sent_ref, own_ref, w_ref, sems = rest
    half, width = low_refs[0].shape
    copies = fetch(pieces, branch * (2 * width + 128), w_ref, sems)
    finish(copies)
    grads = []
    for n, out_ref in enumerate((kept_ref, sent_ref)):
        rows = pl.ds(n * half, half)
        back = dot_t(grad_refs[n][...], w_ref[:, pl.ds(width, width)])
        grad_pre = (gelu_slope(pre_ref[rows, :]) * back).astype(BF)
        grads.append(grad_pre)
        out_ref[...] = dot(grad_pre, w_ref[:, pl.ds(0, width)]).astype(out_ref.dtype)
    grad_pre = jnp.concatenate(grads, axis=0)
    low = jnp.concatenate([ref[...] for ref in low_refs], axis=0)
    grad_low = jnp.concatenate([ref[...] for ref in grad_refs], axis=0)
    own_ref[:, pl.ds(0, width)] = outer(grad_pre, low).astype(BF)
    own_ref[:, pl.ds(width, width)] = outer(act_ref[...], grad_low).astype(BF)
    sums = outer(grad_pre, jnp.ones((2 * half, 128), BF)).astype(BF)
    own_ref[:, pl.ds(2 * width, 128)] = sums


def cross_backward_kernel(start, n_pieces, refs):
    kept_ref, got_ref, sum_ref, pre_ref, q_ref, k_ref, v_ref, order_ref, vec_ref = refs[:9]
    pieces = refs[9 : 9 + n_pieces]
    dq_ref, dk_ref, dv_ref, low_ref, first_ref, row_ref, w_ref, look_ref, sems = refs[
        9 + n_pieces :
    ]
    copies = fetch(pieces, start, w_ref, sems)
    items = k_ref.shape[0]
    width = q_ref.shape[1]
    count = q_ref.shape[0] // items
    order = order_ref[...]
    vec = vec_ref[...]
    masks = head_masks()
    gradient = kept_ref[...].astype(F32) + got_ref[...].astype(F32) + sum_ref[...]
    grad_two, gain_grad, shift_grad = norm_back(pre_ref[...], vec[4:5], gradient)
    low = grad_two.astype(BF)
    low_ref[...] = low
    finish(copies)
    look_ref[...] = by_place(dot_t(low, w_ref[:, pl.ds(width, width)]), order).astype(BF)

    def attend(i):
        rows = stretch(i, count)
        for g in range(width // GROUP):
            cols = pl.ds(g * GROUP, GROUP)
            dq, dk, dv = attend_group_back(
                q_ref[rows, cols],
                k_ref[i, :, cols],
                v_ref[i, :, cols],
                F32(0.0),
                look_ref[rows, cols],
                masks,
                count,
            )
            dq_ref[rows, cols] = dq
            dk_ref[i, :, cols] = dk
            dv_ref[i, :, cols] = dv
            row_ref[3:4, cols] = row_ref[3:4, cols] + column_sum(dv)

    row_ref[3:4, :] = jnp.zeros((1, width), F32)
    repeat(items, attend)
    grad_cross = dq_ref[...]
    back = dot_t(grad_cross, w_ref[:, pl.ds(0, width)])
    first_ref[...] = grad_two + by_place(back, order)
    row_ref[0:1, :] = gain_grad
    row_ref[1:2, :] = shift_grad
    row_ref[2:3, :] = column_sum(grad_cross)
    row_ref[4:5, :] = column_sum(low)


def cross_weights_kernel(refs):
    dq_ref, dk_ref, dv_ref, low_ref, first_ref, look_ref, feature_ref, order_ref = refs[:8]
    kept_ref, sent_ref = refs[8:]
    items, _, image_width = feature_ref.shape
    half, width = order_ref.shape[0] // 2, order_ref.shape[1]
    for part, out_ref in enumerate((kept_ref, sent_ref)):
        order = order_ref[pl.ds(part * half, half), :]
        for n, grad_ref in enumerate((dk_ref, dv_ref)):
            total = None
            for i in range(items):
                turned = by_slot_turned(grad_ref[i], order)
                product = dot(turned, feature_ref[i])
                total = product if total is None else total + product
            out_ref[:, pl.ds(n * image_width, image_width)] = total.astype(BF)
        start = 2 * image_width
        turned = by_slot_turned(first_ref[...].astype(BF), order)
        out_ref[:, pl.ds(start, width)] = dot(turned, dq_ref[...]).astype(BF)
        turned = by_slot_turned(look_ref[...], order)
        out_ref[:, pl.ds(start + width, width)] = dot(turned, low_ref[...]).astype(BF)


def feature_kernel(n_pieces, refs):
    dk_ref, dv_ref, order_ref = refs[:3]
    pieces = refs[3 : 3 + n_pieces]
    out_ref, w_ref, sems = refs[3 + n_pieces :]
    items, _, image_width = out_ref.shape
    copies = fetch(pieces, 0, w_ref, sems)
    finish(copies)

    def back(i):
        keys, values = (by_slot(ref[i], order_ref[...]) for ref in (dk_ref, dv_ref))
        total = dot(keys, w_ref[:, pl.ds(0, image_width)])
        out_ref[i] = total + dot(values, w_ref[:, pl.ds(image_width, image_width)])

    repeat(items, back)


def self_backward_kernel(items, n_pieces, refs):
    length_ref, query_ref, kept_ref, got_ref, text_ref, pre_ref, qkv_ref = refs[:7]
    mix_ref, hidden_ref, order_ref, vec_ref = refs[7:11]
    row_refs = refs[11:14]
    pieces = refs[14 : 14 + n_pieces]
    grad_ref, one_ref, g_kept_ref, g_sent_ref, w_ref, sum_ref, mixed_ref, sems = refs[
        14 + n_pieces :
    ]
    copies = fetch(pieces, 3 * pre_ref.shape[1], w_ref, sems)
    rows_all, width = pre_ref.shape
    count = rows_all // items
    text = count - NQ
    order = order_ref[...]
    vec = vec_ref[...]
    masks = head_masks()
    text_grad = kept_ref[...].astype(F32) + got_ref[...].astype(F32) + text_ref[...]
    query_grad = query_ref[...]
    gradient = []
    for i in range(items):
        gradient.append(query_grad[i * NQ : (i + 1) * NQ])
        gradient.append(text_grad[i * text : (i + 1) * text])
    gradient = jnp.concatenate(gradient, axis=0)
    grad_one, gain_grad, shift_grad = norm_back(pre_ref[...], vec[3:4], gradient)
    one_ref[...] = grad_one
    low = grad_one.astype(BF)
    finish(copies)
    mixed_ref[...] = by_place(dot_t(low, w_ref[...]), order).astype(BF)

    def attend(i):
        rows = stretch(i, count)
        mask_add = self_mask(length_ref[i], count)
        for g in range(width // GROUP):
            cols = [pl.ds(n * width + g * GROUP, GROUP) for n in range(3)]
            results = attend_group_back(
                *[qkv_ref[rows, col] for col in cols],
                mask_add,
                mixed_ref[rows, cols[0]],
                masks,
                count,
            )
            for col, value in zip(cols, results):
                grad_ref[rows, col] = value

    repeat(items, attend)
    query_rows, query_ends, text_ends = row_refs
    sum_ref[...] = jnp.zeros(sum_ref.shape, F32)
    total = column_sum(grad_ref[...])
    listed = [
        total[:, :width],
        total[:, 2 * width :],
        column_sum(low),
        gain_grad,
        query_rows[0:1, :],
        query_ends[0:1, :],
        text_ends[0:1, :],
        shift_grad,
        query_rows[1:2, :],
        query_ends[1:2, :],
        text_ends[1:2, :],
        query_rows[2:3, :],
        query_rows[3:4, :],
        query_rows[4:5, :],
        query_ends[2:3, :],
        text_ends[2:3, :],
    ]
    for n, value in enumerate(listed):
        sum_ref[n : n + 1, :] = value
    sums = sum_ref[...].astype(BF)
    half = width // 2
    for part, out_ref in enumerate((g_kept_ref, g_sent_ref)):
        block = order_ref[pl.ds(part * half, half), :]
        turned = by_slot_turned(hidden_ref[...], block)

        def weigh(n):
            cols = stretch(n, width)
            out_ref[:, cols] = dot(turned, grad_ref[:, cols]).astype(BF)

        repeat(3, weigh)
        turned = by_slot_turned(mix_ref[...], block)
        out_ref[:, pl.ds(3 * width, width)] = dot(turned, low).astype(BF)
        out_ref[:, pl.ds(4 * width, 128)] = dot_t(block, sums).astype(BF)


def hidden_kernel(n_pieces, refs):
    grad_ref, one_ref, order_ref = refs[:3]
    pieces = refs[3 : 3 + n_pieces]
    out_ref, w_ref, sems = refs[3 + n_pieces :]
    copies = fetch(pieces, 0, w_ref, sems)
    finish(copies)
    width = one_ref.shape[1]

    def part(n, total):
        cols = stretch(n, width)
        return total + dot_t(grad_ref[:, cols], w_ref[:, cols])

    back = lax.fori_loop(0, 3, part, jnp.zeros(one_ref.shape, F32))
    out_ref[...] = one_ref[...] + by_place(back, order_ref[...])


def shaped(*dims, kind=F32):
    return jax.ShapeDtypeStruct(dims, kind)


def kernel_call(
    body, name, outs, inputs, pieces=(), loaded=None, lengths=None, extra=(), cost=8
):
    vmem = pl.BlockSpec(memory_space=pltpu.VMEM)
    specs = [vmem] * len(inputs) + [pl.BlockSpec(memory_space=pl.ANY)] * len(pieces)
    arrays = tuple(inputs) + tuple(pieces)
    if lengths is not None:
        specs = [pl.BlockSpec(memory_space=pltpu.SMEM)] + specs
        arrays = (lengths,) + arrays
    scratch = []
    if loaded is not None:
        rows = sum(piece.shape[0] for piece in pieces)
        scratch = [pltpu.VMEM((rows, loaded), BF)] + list(extra)
        scratch.append(pltpu.SemaphoreType.DMA((len(pieces),)))
    return pl.pallas_call(
        lambda *refs: body(refs),
        name=name,
        out_shape=outs,
        in_specs=specs,
        out_specs=jax.tree.map(lambda _: vmem, outs),
        scratch_shapes=scratch,
        cost_estimate=pl.CostEstimate(
            flops=cost * 900_000_000, bytes_accessed=cost * 3_000_000, transcendentals=0
        ),
    )(*arrays)


def shards(
    hidden,
    features,
    text_lengths,
    cotangent,
    self_project,
    self_output,
    self_bias,
    norm_gain,
    norm_bias,
    cross_query,
    cross_output,
    image_project,
    cross_bias,
    expand_weight,
    expand_bias,
    reduce_weight,
    reduce_bias,
):
    part = functools.partial
    items, item_rows, width = hidden.shape
    each = self_output.shape[0]
    image_rows, image_width = features.shape[1:]
    ff_each = reduce_weight.shape[1]
    planes = lax.axis_size("z")
    rows = items * item_rows
    query_rows, text_rows = items * NQ, items * (item_rows - NQ)
    ff = planes * ff_each
    order = place_of_slot(width)
    flat = hidden.reshape(rows, width)

    vectors = (self_bias, norm_gain, norm_bias, cross_bias, reduce_bias)
    n_vectors = sum(v.shape[0] for v in vectors)
    ff_width = 2 * width + 128
    up_turned = jnp.swapaxes(expand_weight, 1, 2)
    unit_self, unit_ff = kernel_call(
        pack_kernel,
        "pack",
        (shaped(each, 4 * width + 128, kind=BF), shaped(ff_each, 2 * ff_width, kind=BF)),
        (self_project, self_output, up_turned, reduce_weight, expand_bias, *vectors),
        cost=1,
    )
    image_turned = jnp.swapaxes(image_project, 1, 2)
    unit_cross = jnp.concatenate(
        [image_turned[0], image_turned[1], cross_query, cross_output], axis=1
    )
    w_ff = [lax.all_gather(unit_ff, "z", axis=0, tiled=True)]
    near_self = gather_z_direct(unit_self)
    w_self = finish_all(gather_all(near_self))
    near_cross = gather_z(after(unit_cross, near_self))
    w_cross = gather_all(near_cross, w_self[1:3], w_self[3:4])
    cross_start = 2 * image_width

    qkv, mixture, pre_one, first_query, first_text, text_low, vec = kernel_call(
        part(self_forward_kernel, items, len(w_self)),
        "self_forward",
        (
            shaped(rows, 3 * width, kind=BF),
            shaped(rows, width, kind=BF),
            shaped(rows, width),
            shaped(query_rows, width),
            shaped(text_rows, width),
            shaped(text_rows, width, kind=BF),
            shaped(n_vectors, width),
        ),
        (flat, order),
        w_self,
        4 * width + 128,
        text_lengths,
    )

    w_cross = finish_all(w_cross, first_query)
    wide = shaped(items, image_rows, width, kind=BF)
    image_keys, image_values = kernel_call(
        part(image_kernel, len(w_cross)),
        "image_rows",
        (wide, wide),
        (features, order, vec),
        w_cross,
        cross_start,
    )
    cross_rows, looked, pre_two, second, second_low = kernel_call(
        part(cross_forward_kernel, cross_start, len(w_cross)),
        "cross_forward",
        (
            shaped(query_rows, width, kind=BF),
            shaped(query_rows, width, kind=BF),
            shaped(query_rows, width),
            shaped(query_rows, width),
            shaped(query_rows, width, kind=BF),
        ),
        (first_query, image_keys, image_values, order, vec),
        w_cross,
        2 * width,
    )

    branches = [None, None]
    for j, values, low in ((1, first_text, text_low), (0, second, second_low)):
        count = values.shape[0]
        if j:
            low_all = gather_plane(low, (image_keys,), (second_low,))
        else:
            low_all = gather_plane(low)
        half = 4 * count
        pre_act, active, kept, sent = kernel_call(
            part(branch_up_kernel, j, len(w_ff)),
            "branch_up_%d" % j,
            (
                shaped(2 * half, ff),
                shaped(2 * half, ff, kind=BF),
                shaped(half, width),
                shaped(half, width, kind=BF),
            ),
            low_all,
            w_ff,
            ff_width,
        )
        out, grad_sum, grad_low, ends = kernel_call(
            part(branch_end_kernel, j),
            "branch_end_%d" % j,
            (
                shaped(count, width, kind=BF),
                shaped(count, width),
                shaped(count, width, kind=BF),
                shaped(8, width),
            ),
            (*scatter_plane(kept, sent), values, cotangent, vec),
        )
        kept, sent, grads = kernel_call(
            part(branch_down_kernel, j, len(w_ff)),
            "branch_down_%d" % j,
            (
                shaped(half, width),
                shaped(half, width, kind=BF),
                shaped(ff, ff_width, kind=BF),
            ),
            (*gather_plane(grad_low), *low_all, pre_act, active),
            w_ff,
            2 * width,
        )
        own = lax.psum_scatter(grads, "z", scatter_dimension=0, tiled=True)
        branches[j] = (out, grad_sum, ends, scatter_plane(kept, sent), own)
    query, text = branches
    layer_out = jnp.concatenate(
        [query[0].reshape(items, NQ, width), text[0].reshape(items, item_rows - NQ, width)],
        axis=1,
    )

    query_got = after(query[3][1], text[3][1])
    grad_cross, grad_ikey, grad_ivalue, two_low, grad_first, cross_ends = kernel_call(
        part(cross_backward_kernel, cross_start, len(w_cross)),
        "cross_backward",
        (
            shaped(query_rows, width, kind=BF),
            wide,
            wide,
            shaped(query_rows, width, kind=BF),
            shaped(query_rows, width),
            shaped(8, width),
        ),
        (query[3][0], query_got, query[1], pre_two, cross_rows, image_keys, image_values, order, vec),
        w_cross,
        2 * width,
        extra=(pltpu.VMEM((query_rows, width), BF),),
        cost=LATE,
    )
    grad_first = after(grad_first, branches[1][4])
    packed = shaped(width // 2, 4 * width + 128, kind=BF)
    grad_qkv, grad_one, kept, sent = kernel_call(
        part(self_backward_kernel, items, len(w_self)),
        "self_backward",
        (shaped(rows, 3 * width, kind=BF), shaped(rows, width), packed, packed),
        (
            grad_first,
            *text[3],
            text[1],
            pre_one,
            qkv,
            mixture,
            flat,
            order,
            vec,
            cross_ends,
            query[2],
            text[2],
        ),
        w_self,
        width,
        text_lengths,
        (pltpu.VMEM((128, width), F32), pltpu.VMEM((rows, width), BF)),
        LATE,
    )

    feature_order = after(order, sent)
    feature_grad = kernel_call(
        part(feature_kernel, len(w_cross)),
        "feature_grad",
        shaped(items, image_rows, image_width),
        (grad_ikey, grad_ivalue, feature_order),
        w_cross,
        cross_start,
        cost=LATE,
    )
    kept, sent = halved(kept, after(swap(sent, step_c), feature_grad))
    packed = shaped(width // 2, cross_start + 2 * width, kind=BF)
    grad_cross = after(grad_cross, sent)
    cross_kept, cross_sent = kernel_call(
        cross_weights_kernel,
        "cross_weights",
        (packed, packed),
        (grad_cross, grad_ikey, grad_ivalue, two_low, first_query, looked, features, order),
        cost=LATE,
    )
    got = swap(sent, step_b)
    cross_sent = after(cross_sent, got)
    kept, sent = halved(kept, got)
    hidden_order = after(order, cross_sent, sent)
    hidden_grad = kernel_call(
        part(hidden_kernel, len(w_self)),
        "hidden_grad",
        shaped(rows, width),
        (grad_qkv, grad_one, hidden_order),
        w_self,
        3 * width,
        cost=LATE,
    )
    got = swap(sent, step_a)
    cross_got = after(swap(cross_sent, step_c), hidden_grad, got)
    cross_kept, cross_sent = halved(cross_kept, cross_got)
    if planes == 4:
        kept, sent = halved(kept, got)
        cross_got = after(swap(cross_sent, step_b), sent, branches[0][4])
        cross_kept, cross_sent = halved(cross_kept, cross_got)
        kept, sent = halved(kept, after(swap(sent, step_z1), cross_sent))
        cross_got = after(swap(cross_sent, step_a), sent)
        cross_kept, cross_sent = halved(cross_kept, cross_got)
        own_self = kept.astype(F32) + swap(sent, step_z2).astype(F32)
        cross_kept, cross_sent = halved(cross_kept, swap(cross_sent, step_z1))
        own_cross = cross_kept.astype(F32) + swap(cross_sent, step_z2).astype(F32)
    else:
        own_self = scatter_rest(kept, got)
        cross_kept, cross_sent = halved(cross_kept, swap(cross_sent, step_b))
        own_cross = scatter_rest(cross_kept, swap(cross_sent, step_a))
    own_ff = [after(branch[4], cross_sent).astype(F32) for branch in branches]
    own_sums = own_self[:, 4 * width : 4 * width + n_vectors].T
    own_up = [own[:, :width].T for own in own_ff]
    own_down = [own[:, width : 2 * width] for own in own_ff]
    own_up_bias = [own[:, 2 * width] for own in own_ff]
    return (
        layer_out,
        hidden_grad.reshape(items, item_rows, width),
        feature_grad,
        jnp.stack([own_self[:, n * width : (n + 1) * width] for n in range(3)]),
        own_self[:, 3 * width : 4 * width],
        own_sums[0:3],
        own_sums[3:7],
        own_sums[7:11],
        own_cross[:, cross_start : cross_start + width],
        own_cross[:, cross_start + width :],
        jnp.stack([own_cross[:, n * image_width : (n + 1) * image_width].T for n in range(2)]),
        own_sums[11:14],
        jnp.stack(own_up),
        jnp.stack(own_up_bias),
        jnp.stack(own_down),
        own_sums[14:16],
    )


def solution(mesh):
    dp, pair = mesh.devices.shape
    fine = Mesh(mesh.devices.reshape(dp // 4, 2, 2, pair), AXES)
    first, second, third = P(AXES), P(None, AXES), P(None, None, AXES)
    in_specs = (
        first, first, first, first,
        second, first, second, second, second, first, first,
        third, second, third, second, second, second,
    )
    out_specs = (
        first, first, first,
        second, first, second, second, second, first, first,
        third, second, third, second, second, second,
    )
    return jax.shard_map(shards, mesh=fine, in_specs=in_specs, out_specs=out_specs, check_vma=False)
```

```python
import functools

import jax
import jax.numpy as jnp
from jax import lax
from jax.experimental import pallas as pl
from jax.experimental.layout import Layout, with_layout_constraint
from jax.experimental.pallas import tpu as pltpu
from jax.sharding import Mesh, PartitionSpec as P

HEAD = 64
NQ = 32
GROUP = 256
PER = GROUP // HEAD
eps = 1e-06
masked_off = 1000000000.0
LATE = 4
AXES = ("z", "x", "c", "y")
BF = jnp.bfloat16
F32 = jnp.float32


def coords(index):
    return (index // 8, index // 4 % 2, index // 2 % 2, index % 2)


def pairs(count, move):
    result = []
    for source in range(count):
        z, x, c, y = move(*coords(source))
        result.append((source, ((z * 2 + x) * 2 + c) * 2 + y))
    return result


def step_a(z, x, c, y):
    return (z, x ^ 1, c, y) if c == 0 else (z, x, c, y ^ 1)


def step_b(z, x, c, y):
    return (z, x, c, y ^ 1) if c == 0 else (z, x ^ 1, c, y)


def step_c(z, x, c, y):
    return (z, x, c ^ 1, y)


def swap(value, move):
    count = lax.axis_size(AXES)
    return lax.ppermute(value, AXES, pairs(count, move))


def swap_z(value, distance):
    return swap(value, lambda z, x, c, y: (z ^ distance, x, c, y))


def gather_z(unit):
    if lax.axis_size("z") == 4:
        near = jnp.concatenate([unit, swap_z(unit, 2)], axis=0)
        return jnp.concatenate([near, swap_z(near, 1)], axis=0)
    return lax.all_gather(unit, "z", axis=0, tiled=True)


def gather_z_direct(unit):
    if lax.axis_size("z") == 4:
        one, two, three = (swap_z(unit, k) for k in (1, 2, 3))
        return jnp.concatenate([unit, two, one, three], axis=0)
    return lax.all_gather(unit, "z", axis=0, tiled=True)


def gather_all(near, first=(), last=()):
    a = swap(after(near, *first), step_a)
    b = swap(after(near, *last), step_b)
    pieces = [near, a, b, swap(a, step_b)]
    pieces.append(swap(after(near, *last), step_c))
    return pieces + [swap(piece, step_c) for piece in pieces[1:3]]


def finish_all(pieces, *gates):
    return pieces + [swap(after(pieces[3], *gates), step_c)]


def gather_plane(rows, first=(), second=()):
    rows = jnp.concatenate([rows, after(swap(rows, step_a), *first)], axis=0)
    rows = jnp.concatenate([rows, after(swap(rows, step_b), *second)], axis=0)
    return [rows, swap(rows, step_c)]


def after(value, *earlier):
    return lax.optimization_barrier((value,) + earlier)[0]


def add_low(left, right):
    return (left.astype(F32) + right.astype(F32)).astype(BF)


def halved(kept, got):
    half = got.shape[0] // 2
    return add_low(kept[:half], got[:half]), add_low(kept[half:], got[half:])


def scatter_plane(kept, sent):
    for move in (step_c, step_b):
        kept, sent = halved(kept, swap(sent, move))
    return kept, swap(sent, step_a)


def step_z1(z, x, c, y):
    return (z ^ 1, x, c, y)


def step_z2(z, x, c, y):
    return (z ^ 2, x, c, y)


def scatter_rest(kept, got):
    return lax.psum_scatter(add_low(kept, got), "z", scatter_dimension=0, tiled=True).astype(F32)


def slot_owner(count):
    z, x, c, y = (lax.axis_index(name) for name in AXES)
    planes = count // 8
    slot = jnp.arange(count)
    k = slot % planes
    alpha = slot // planes % 2
    beta = slot // (2 * planes) % 2
    core = c ^ (slot // (4 * planes))
    flip_x = jnp.where(core == 0, alpha, beta)
    flip_y = jnp.where(core == 0, beta, alpha)
    plane = z ^ (k % 2 * 2 + k // 2) if planes == 4 else k
    return ((plane * 2 + (x ^ flip_x)) * 2 + core) * 2 + (y ^ flip_y)


def place_of_slot(width):
    count = lax.axis_size(AXES)
    each = width // count
    source = (slot_owner(count)[:, None] * each + jnp.arange(each)[None, :]).reshape(-1)
    return (source[:, None] == jnp.arange(width)[None, :]).astype(BF)


def by_slot(values, order):
    return dot_t(values, order).astype(BF)


def by_slot_turned(values, order):
    return dot_t(order, values).astype(BF)


def by_place(values, order):
    return dot(values.astype(BF), order)


def dot(left, right):
    return lax.dot_general(
        left, right, (((left.ndim - 1,), (0,)), ((), ())), preferred_element_type=F32
    )


def dot_t(left, right):
    return lax.dot_general(
        left, right, (((left.ndim - 1,), (1,)), ((), ())), preferred_element_type=F32
    )


def outer(left, right):
    lead = tuple(range(left.ndim - 1))
    return lax.dot_general(left, right, ((lead, lead), ((), ())), preferred_element_type=F32)


def column_sum(values):
    return jnp.sum(values.astype(F32), axis=0, keepdims=True)


def layer_norm(values, scale, shift):
    center = values - jnp.mean(values, axis=-1, keepdims=True)
    spread = jnp.mean(center * center, axis=-1, keepdims=True)
    return center * lax.rsqrt(spread + eps) * scale + shift


def norm_back(values, scale, gradient):
    center = values - jnp.mean(values, axis=-1, keepdims=True)
    spread = jnp.mean(center * center, axis=-1, keepdims=True)
    inverse = lax.rsqrt(spread + eps)
    normal = center * inverse
    inner = gradient * scale
    result = inverse * (
        inner
        - jnp.mean(inner, axis=-1, keepdims=True)
        - normal * jnp.mean(inner * normal, axis=-1, keepdims=True)
    )
    return result, column_sum(gradient * normal), column_sum(gradient)


def gelu_parts(values):
    half = F32(0.5) + F32(0.5) * lax.erf(values * F32(0.5**0.5))
    return half


def gelu_slope(values):
    density = jnp.exp(values * values * F32(-0.5)) * F32((2.0 * 3.141592653589793) ** -0.5)
    return gelu_parts(values) + values * density


def head_masks():
    lane = lax.broadcasted_iota(jnp.int32, (1, GROUP), 1) // HEAD
    return [(lane == h).astype(F32).astype(BF) for h in range(PER)]


def spread_heads(rows, masks):
    return jnp.concatenate([rows * mask for mask in masks], axis=0)


def fold_heads(stacked, masks, count):
    total = None
    for h, mask in enumerate(masks):
        part = stacked[h * count : (h + 1) * count] * mask.astype(F32)
        total = part if total is None else total + part
    return total


def softmax_rows(scores):
    shifted = jnp.exp(scores - jnp.max(scores, axis=-1, keepdims=True))
    return shifted / jnp.sum(shifted, axis=-1, keepdims=True)


def self_mask(length, rows):
    shape = (PER * rows, rows)
    row = lax.broadcasted_iota(jnp.int32, shape, 0) % rows
    col = lax.broadcasted_iota(jnp.int32, shape, 1)
    allowed = (col < NQ) | ((row >= NQ) & (col <= row) & (col - NQ < length))
    return jnp.where(allowed, F32(0.0), F32(-masked_off))


def attend_group_back(q, k, v, mask_add, grad, masks, count):
    q = spread_heads(q, masks)
    grad = spread_heads(grad, masks)
    weights = softmax_rows(dot_t(q, k) * HEAD ** (-0.5) + mask_add)
    grad_value = outer(weights.astype(BF), grad).astype(BF)
    grad_weight = dot_t(grad, v)
    grad_score = (
        weights * (grad_weight - jnp.sum(grad_weight * weights, axis=-1, keepdims=True))
    ).astype(BF)
    grad_query = fold_heads(dot(grad_score, k), masks, count) * HEAD ** (-0.5)
    grad_key = outer(grad_score, q) * HEAD ** (-0.5)
    return grad_query.astype(BF), grad_key.astype(BF), grad_value


def repeat(count, body):
    def step(i, carry):
        body(i)
        return carry

    lax.fori_loop(0, count, step, 0)


def stretch(i, count):
    return pl.ds(pl.multiple_of(i * count, count), count)


def fetch(pieces, start, target, sems):
    width = target.shape[1]
    copies = []
    row = 0
    for n, piece in enumerate(pieces):
        count = piece.shape[0]
        source = piece.at[:, pl.ds(start, width)]
        copies.append(
            pltpu.make_async_copy(source, target.at[pl.ds(row, count)], sems.at[n])
        )
        row += count
    for copy in copies:
        copy.start()
    return copies


def finish(copies):
    for copy in copies:
        copy.wait()


def turned_rows(rows):
    rows = list(rows)
    each = rows[0].shape[1]
    rows.append(jnp.zeros((128 - sum(row.shape[0] for row in rows), each), F32))
    return jnp.concatenate(rows, axis=0).T.astype(BF)


def pack_kernel(refs):
    project_ref, output_ref, up_ref, down_ref, bias_ref = refs[:5]
    vector_refs, self_ref, ff_ref = refs[5:-2], refs[-2], refs[-1]
    width = output_ref.shape[1]
    for n in range(3):
        self_ref[:, pl.ds(n * width, width)] = project_ref[n]
    self_ref[:, pl.ds(3 * width, width)] = output_ref[...]
    vectors = turned_rows(ref[...].astype(F32) for ref in vector_refs)
    self_ref[:, pl.ds(4 * width, 128)] = vectors
    for n in range(2):
        start = n * (2 * width + 128)
        ff_ref[:, pl.ds(start, width)] = up_ref[n]
        ff_ref[:, pl.ds(start + width, width)] = down_ref[n]
        bias = bias_ref[n : n + 1, :].astype(F32)
        ff_ref[:, pl.ds(start + 2 * width, 128)] = turned_rows([bias])


def self_forward_kernel(items, n_pieces, refs):
    length_ref, hidden_ref, order_ref = refs[:3]
    pieces = refs[3 : 3 + n_pieces]
    qkv_ref, mix_ref, pre_ref, query_ref, text_ref, low_ref, vec_ref, w_ref, sems = refs[
        3 + n_pieces :
    ]
    rows_all, width = hidden_ref.shape
    copies = fetch(pieces, 0, w_ref, sems)
    order = order_ref[...]
    hidden_slot = by_slot(hidden_ref[...], order)
    finish(copies)
    vec = outer(w_ref[:, pl.ds(4 * width, 128)], order)[: vec_ref.shape[0]]
    vec_ref[...] = vec
    bias = [vec[0:1], F32(0.0), vec[1:2]]
    for n in range(3):
        cols = pl.ds(n * width, width)
        qkv_ref[:, cols] = (dot(hidden_slot, w_ref[:, cols]) + bias[n]).astype(BF)
    masks = head_masks()
    count = rows_all // items

    def attend(i):
        rows = stretch(i, count)
        mask_add = self_mask(length_ref[i], count)
        for g in range(width // GROUP):
            cols = [pl.ds(n * width + g * GROUP, GROUP) for n in range(3)]
            q = spread_heads(qkv_ref[rows, cols[0]], masks)
            scores = dot_t(q, qkv_ref[rows, cols[1]]) * HEAD ** (-0.5) + mask_add
            weights = softmax_rows(scores).astype(BF)
            mixed = dot(weights, qkv_ref[rows, cols[2]])
            mix_ref[rows, cols[0]] = fold_heads(mixed, masks, count).astype(BF)

    repeat(items, attend)
    mixture_slot = by_slot(mix_ref[...], order)
    pre = dot(mixture_slot, w_ref[:, pl.ds(3 * width, width)])
    pre = pre + vec[2:3] + hidden_ref[...].astype(F32)
    pre_ref[...] = pre
    first = layer_norm(pre, vec[3:4], vec[7:8])
    text = count - NQ
    for i in range(items):
        query_ref[pl.ds(i * NQ, NQ), :] = first[i * count : i * count + NQ]
        part = first[i * count + NQ : (i + 1) * count]
        text_ref[pl.ds(i * text, text), :] = part
        low_ref[pl.ds(i * text, text), :] = part.astype(BF)


def image_kernel(n_pieces, refs):
    feature_ref, order_ref, vec_ref = refs[:3]
    pieces = refs[3 : 3 + n_pieces]
    key_ref, value_ref, w_ref, sems = refs[3 + n_pieces :]
    items, _, image_width = feature_ref.shape
    copies = fetch(pieces, 0, w_ref, sems)
    order = order_ref[...]
    bias_slot = dot_t(vec_ref[...].astype(BF), order)[12:13]
    finish(copies)

    def project(i):
        rows = feature_ref[i]
        keys = dot_t(rows, w_ref[:, pl.ds(0, image_width)])
        key_ref[i] = by_place(keys, order_ref[...]).astype(BF)
        values = dot_t(rows, w_ref[:, pl.ds(image_width, image_width)]) + bias_slot
        value_ref[i] = by_place(values, order_ref[...]).astype(BF)

    repeat(items, project)


def cross_forward_kernel(start, n_pieces, refs):
    first_ref, key_ref, value_ref, order_ref, vec_ref = refs[:5]
    pieces = refs[5 : 5 + n_pieces]
    rows_ref, look_ref, pre_ref, second_ref, low_ref, w_ref, sems = refs[5 + n_pieces :]
    copies = fetch(pieces, start, w_ref, sems)
    items = key_ref.shape[0]
    width = first_ref.shape[1]
    count = first_ref.shape[0] // items
    order = order_ref[...]
    vec = vec_ref[...]
    masks = head_masks()
    first_slot = by_slot(first_ref[...].astype(BF), order)
    finish(copies)
    rows_ref[...] = (dot(first_slot, w_ref[:, pl.ds(0, width)]) + vec[11:12]).astype(BF)

    def attend(i):
        rows = stretch(i, count)
        for g in range(width // GROUP):
            cols = pl.ds(g * GROUP, GROUP)
            q = spread_heads(rows_ref[rows, cols], masks)
            scores = dot_t(q, key_ref[i, :, cols]) * HEAD ** (-0.5)
            mixed = dot(softmax_rows(scores).astype(BF), value_ref[i, :, cols])
            look_ref[rows, cols] = fold_heads(mixed, masks, count).astype(BF)

    repeat(items, attend)
    pre = dot(by_slot(look_ref[...], order), w_ref[:, pl.ds(width, width)])
    pre = pre + vec[13:14] + first_ref[...]
    pre_ref[...] = pre
    second = layer_norm(pre, vec[4:5], vec[8:9])
    second_ref[...] = second
    low_ref[...] = second.astype(BF)


def branch_up_kernel(branch, n_pieces, refs):
    low_refs = refs[:2]
    pieces = refs[2 : 2 + n_pieces]
    pre_ref, act_ref, kept_ref, sent_ref, w_ref, sems = refs[2 + n_pieces :]
    half, width = low_refs[0].shape
    copies = fetch(pieces, branch * (2 * width + 128), w_ref, sems)
    finish(copies)
    first_lane = (lax.broadcasted_iota(jnp.int32, (8, 128), 1) == 0).astype(F32).astype(BF)
    bias = dot_t(first_lane, w_ref[:, pl.ds(2 * width, 128)])[0:1]
    for n, (low_ref, out_ref) in enumerate(zip(low_refs, (kept_ref, sent_ref))):
        rows = pl.ds(n * half, half)
        pre = dot_t(low_ref[...], w_ref[:, pl.ds(0, width)]) + bias
        pre_ref[rows, :] = pre
        active = (pre * gelu_parts(pre)).astype(BF)
        act_ref[rows, :] = active
        out_ref[...] = dot(active, w_ref[:, pl.ds(width, width)]).astype(out_ref.dtype)


def branch_end_kernel(branch, refs):
    kept_ref, got_ref, value_ref, cot_ref, vec_ref = refs[:5]
    out_ref, grad_ref, low_ref, sum_ref = refs[5:]
    items, count, _ = cot_ref.shape
    vec = vec_ref[...]
    gain, shift = vec[5 + branch : 6 + branch], vec[9 + branch : 10 + branch]
    total = kept_ref[...].astype(F32) + got_ref[...].astype(F32)
    total = total + vec[14 + branch : 15 + branch] + value_ref[...]
    start, size = (NQ, count - NQ) if branch else (0, NQ)
    cot = jnp.concatenate([cot_ref[i, start : start + size, :] for i in range(items)], axis=0)
    out_ref[...] = layer_norm(total, gain, shift).astype(BF)
    grad, gain_grad, shift_grad = norm_back(total, gain, cot.astype(F32))
    grad_ref[...] = grad
    low = grad.astype(BF)
    low_ref[...] = low
    sum_ref[0:1, :] = gain_grad
    sum_ref[1:2, :] = shift_grad
    sum_ref[2:3, :] = column_sum(low)


def branch_down_kernel(branch, n_pieces, refs):
    grad_refs, low_refs, (pre_ref, act_ref) = refs[:2], refs[2:4], refs[4:6]
    pieces = refs[6 : 6 + n_pieces]
    rest = refs[6 + n_pieces :]
    kept_ref, sent_ref, own_ref, w_ref, sems = rest
    half, width = low_refs[0].shape
    copies = fetch(pieces, branch * (2 * width + 128), w_ref, sems)
    finish(copies)
    grads = []
    for n, out_ref in enumerate((kept_ref, sent_ref)):
        rows = pl.ds(n * half, half)
        back = dot_t(grad_refs[n][...], w_ref[:, pl.ds(width, width)])
        grad_pre = (gelu_slope(pre_ref[rows, :]) * back).astype(BF)
        grads.append(grad_pre)
        out_ref[...] = dot(grad_pre, w_ref[:, pl.ds(0, width)]).astype(out_ref.dtype)
    grad_pre = jnp.concatenate(grads, axis=0)
    low = jnp.concatenate([ref[...] for ref in low_refs], axis=0)
    grad_low = jnp.concatenate([ref[...] for ref in grad_refs], axis=0)
    own_ref[:, pl.ds(0, width)] = outer(grad_pre, low).astype(BF)
    own_ref[:, pl.ds(width, width)] = outer(act_ref[...], grad_low).astype(BF)
    sums = outer(grad_pre, jnp.ones((2 * half, 128), BF)).astype(BF)
    own_ref[:, pl.ds(2 * width, 128)] = sums


def cross_backward_kernel(start, n_pieces, refs):
    kept_ref, got_ref, sum_ref, pre_ref, q_ref, k_ref, v_ref, order_ref, vec_ref = refs[:9]
    pieces = refs[9 : 9 + n_pieces]
    dq_ref, dk_ref, dv_ref, low_ref, first_ref, row_ref, w_ref, look_ref, sems = refs[
        9 + n_pieces :
    ]
    copies = fetch(pieces, start, w_ref, sems)
    items = k_ref.shape[0]
    width = q_ref.shape[1]
    count = q_ref.shape[0] // items
    order = order_ref[...]
    vec = vec_ref[...]
    masks = head_masks()
    gradient = kept_ref[...].astype(F32) + got_ref[...].astype(F32) + sum_ref[...]
    grad_two, gain_grad, shift_grad = norm_back(pre_ref[...], vec[4:5], gradient)
    low = grad_two.astype(BF)
    low_ref[...] = low
    finish(copies)
    look_ref[...] = by_place(dot_t(low, w_ref[:, pl.ds(width, width)]), order).astype(BF)

    def attend(i):
        rows = stretch(i, count)
        for g in range(width // GROUP):
            cols = pl.ds(g * GROUP, GROUP)
            dq, dk, dv = attend_group_back(
                q_ref[rows, cols],
                k_ref[i, :, cols],
                v_ref[i, :, cols],
                F32(0.0),
                look_ref[rows, cols],
                masks,
                count,
            )
            dq_ref[rows, cols] = dq
            dk_ref[i, :, cols] = dk
            dv_ref[i, :, cols] = dv
            row_ref[3:4, cols] = row_ref[3:4, cols] + column_sum(dv)

    row_ref[3:4, :] = jnp.zeros((1, width), F32)
    repeat(items, attend)
    grad_cross = dq_ref[...]
    back = dot_t(grad_cross, w_ref[:, pl.ds(0, width)])
    first_ref[...] = grad_two + by_place(back, order)
    row_ref[0:1, :] = gain_grad
    row_ref[1:2, :] = shift_grad
    row_ref[2:3, :] = column_sum(grad_cross)
    row_ref[4:5, :] = column_sum(low)


def cross_weights_kernel(refs):
    dq_ref, dk_ref, dv_ref, low_ref, first_ref, look_ref, feature_ref, order_ref = refs[:8]
    kept_ref, sent_ref = refs[8:]
    items, _, image_width = feature_ref.shape
    half, width = order_ref.shape[0] // 2, order_ref.shape[1]
    for part, out_ref in enumerate((kept_ref, sent_ref)):
        order = order_ref[pl.ds(part * half, half), :]
        for n, grad_ref in enumerate((dk_ref, dv_ref)):
            total = None
            for i in range(items):
                turned = by_slot_turned(grad_ref[i], order)
                product = dot(turned, feature_ref[i])
                total = product if total is None else total + product
            out_ref[:, pl.ds(n * image_width, image_width)] = total.astype(BF)
        start = 2 * image_width
        turned = by_slot_turned(first_ref[...].astype(BF), order)
        out_ref[:, pl.ds(start, width)] = dot(turned, dq_ref[...]).astype(BF)
        turned = by_slot_turned(look_ref[...], order)
        out_ref[:, pl.ds(start + width, width)] = dot(turned, low_ref[...]).astype(BF)


def feature_kernel(n_pieces, refs):
    dk_ref, dv_ref, order_ref = refs[:3]
    pieces = refs[3 : 3 + n_pieces]
    out_ref, w_ref, sems = refs[3 + n_pieces :]
    items, _, image_width = out_ref.shape
    copies = fetch(pieces, 0, w_ref, sems)
    finish(copies)

    def back(i):
        keys, values = (by_slot(ref[i], order_ref[...]) for ref in (dk_ref, dv_ref))
        total = dot(keys, w_ref[:, pl.ds(0, image_width)])
        out_ref[i] = total + dot(values, w_ref[:, pl.ds(image_width, image_width)])

    repeat(items, back)


def self_backward_kernel(items, n_pieces, refs):
    length_ref, query_ref, kept_ref, got_ref, text_ref, pre_ref, qkv_ref = refs[:7]
    mix_ref, hidden_ref, order_ref, vec_ref = refs[7:11]
    row_refs = refs[11:14]
    pieces = refs[14 : 14 + n_pieces]
    grad_ref, one_ref, g_kept_ref, g_sent_ref, w_ref, sum_ref, mixed_ref, sems = refs[
        14 + n_pieces :
    ]
    copies = fetch(pieces, 3 * pre_ref.shape[1], w_ref, sems)
    rows_all, width = pre_ref.shape
    count = rows_all // items
    text = count - NQ
    order = order_ref[...]
    vec = vec_ref[...]
    masks = head_masks()
    text_grad = kept_ref[...].astype(F32) + got_ref[...].astype(F32) + text_ref[...]
    query_grad = query_ref[...]
    gradient = []
    for i in range(items):
        gradient.append(query_grad[i * NQ : (i + 1) * NQ])
        gradient.append(text_grad[i * text : (i + 1) * text])
    gradient = jnp.concatenate(gradient, axis=0)
    grad_one, gain_grad, shift_grad = norm_back(pre_ref[...], vec[3:4], gradient)
    one_ref[...] = grad_one
    low = grad_one.astype(BF)
    finish(copies)
    mixed_ref[...] = by_place(dot_t(low, w_ref[...]), order).astype(BF)

    def attend(i):
        rows = stretch(i, count)
        mask_add = self_mask(length_ref[i], count)
        for g in range(width // GROUP):
            cols = [pl.ds(n * width + g * GROUP, GROUP) for n in range(3)]
            results = attend_group_back(
                *[qkv_ref[rows, col] for col in cols],
                mask_add,
                mixed_ref[rows, cols[0]],
                masks,
                count,
            )
            for col, value in zip(cols, results):
                grad_ref[rows, col] = value

    repeat(items, attend)
    query_rows, query_ends, text_ends = row_refs
    sum_ref[...] = jnp.zeros(sum_ref.shape, F32)
    total = column_sum(grad_ref[...])
    listed = [
        total[:, :width],
        total[:, 2 * width :],
        column_sum(low),
        gain_grad,
        query_rows[0:1, :],
        query_ends[0:1, :],
        text_ends[0:1, :],
        shift_grad,
        query_rows[1:2, :],
        query_ends[1:2, :],
        text_ends[1:2, :],
        query_rows[2:3, :],
        query_rows[3:4, :],
        query_rows[4:5, :],
        query_ends[2:3, :],
        text_ends[2:3, :],
    ]
    for n, value in enumerate(listed):
        sum_ref[n : n + 1, :] = value
    sums = sum_ref[...].astype(BF)
    half = width // 2
    for part, out_ref in enumerate((g_kept_ref, g_sent_ref)):
        block = order_ref[pl.ds(part * half, half), :]
        turned = by_slot_turned(hidden_ref[...], block)

        def weigh(n):
            cols = stretch(n, width)
            out_ref[:, cols] = dot(turned, grad_ref[:, cols]).astype(BF)

        repeat(3, weigh)
        turned = by_slot_turned(mix_ref[...], block)
        out_ref[:, pl.ds(3 * width, width)] = dot(turned, low).astype(BF)
        out_ref[:, pl.ds(4 * width, 128)] = dot_t(block, sums).astype(BF)


def hidden_kernel(n_pieces, refs):
    grad_ref, one_ref, order_ref = refs[:3]
    pieces = refs[3 : 3 + n_pieces]
    out_ref, w_ref, sems = refs[3 + n_pieces :]
    copies = fetch(pieces, 0, w_ref, sems)
    finish(copies)
    width = one_ref.shape[1]

    def part(n, total):
        cols = stretch(n, width)
        return total + dot_t(grad_ref[:, cols], w_ref[:, cols])

    back = lax.fori_loop(0, 3, part, jnp.zeros(one_ref.shape, F32))
    out_ref[...] = one_ref[...] + by_place(back, order_ref[...])


def shaped(*dims, kind=F32):
    return jax.ShapeDtypeStruct(dims, kind)


def kernel_call(
    body, name, outs, inputs, pieces=(), loaded=None, lengths=None, extra=(), cost=8
):
    vmem = pl.BlockSpec(memory_space=pltpu.VMEM)
    specs = [vmem] * len(inputs) + [pl.BlockSpec(memory_space=pl.ANY)] * len(pieces)
    arrays = tuple(inputs) + tuple(pieces)
    if lengths is not None:
        specs = [pl.BlockSpec(memory_space=pltpu.SMEM)] + specs
        arrays = (lengths,) + arrays
    scratch = []
    if loaded is not None:
        rows = sum(piece.shape[0] for piece in pieces)
        scratch = [pltpu.VMEM((rows, loaded), BF)] + list(extra)
        scratch.append(pltpu.SemaphoreType.DMA((len(pieces),)))
    return pl.pallas_call(
        lambda *refs: body(refs),
        name=name,
        out_shape=outs,
        in_specs=specs,
        out_specs=jax.tree.map(lambda _: vmem, outs),
        scratch_shapes=scratch,
        cost_estimate=pl.CostEstimate(
            flops=int(cost * 900_000_000), bytes_accessed=int(cost * 3_000_000), transcendentals=0
        ),
    )(*arrays)


def shards(
    hidden,
    features,
    text_lengths,
    cotangent,
    self_project,
    self_output,
    self_bias,
    norm_gain,
    norm_bias,
    cross_query,
    cross_output,
    image_project,
    cross_bias,
    expand_weight,
    expand_bias,
    reduce_weight,
    reduce_bias,
):
    part = functools.partial
    items, item_rows, width = hidden.shape
    each = self_output.shape[0]
    image_rows, image_width = features.shape[1:]
    ff_each = reduce_weight.shape[1]
    planes = lax.axis_size("z")
    rows = items * item_rows
    query_rows, text_rows = items * NQ, items * (item_rows - NQ)
    ff = planes * ff_each
    order = place_of_slot(width)
    flat = hidden.reshape(rows, width)

    vectors = (self_bias, norm_gain, norm_bias, cross_bias, reduce_bias)
    n_vectors = sum(v.shape[0] for v in vectors)
    ff_width = 2 * width + 128
    up_turned = jnp.swapaxes(expand_weight, 1, 2)
    unit_self, unit_ff = kernel_call(
        pack_kernel,
        "pack",
        (shaped(each, 4 * width + 128, kind=BF), shaped(ff_each, 2 * ff_width, kind=BF)),
        (self_project, self_output, up_turned, reduce_weight, expand_bias, *vectors),
        cost=1,
    )
    image_turned = jnp.swapaxes(image_project, 1, 2)
    unit_cross = jnp.concatenate(
        [image_turned[0], image_turned[1], cross_query, cross_output], axis=1
    )
    w_ff = [lax.all_gather(unit_ff, "z", axis=0, tiled=True)]
    near_self = gather_z_direct(unit_self)
    w_self = finish_all(gather_all(near_self))
    near_cross = gather_z(after(unit_cross, near_self))
    w_cross = gather_all(near_cross, w_self[1:3], w_self[3:4])
    cross_start = 2 * image_width

    qkv, mixture, pre_one, first_query, first_text, text_low, vec = kernel_call(
        part(self_forward_kernel, items, len(w_self)),
        "self_forward",
        (
            shaped(rows, 3 * width, kind=BF),
            shaped(rows, width, kind=BF),
            shaped(rows, width),
            shaped(query_rows, width),
            shaped(text_rows, width),
            shaped(text_rows, width, kind=BF),
            shaped(n_vectors, width),
        ),
        (flat, order),
        w_self,
        4 * width + 128,
        text_lengths,
    )

    w_cross = finish_all(w_cross, first_query)
    wide = shaped(items, image_rows, width, kind=BF)
    image_keys, image_values = kernel_call(
        part(image_kernel, len(w_cross)),
        "image_rows",
        (wide, wide),
        (features, order, vec),
        w_cross,
        cross_start,
    )
    cross_rows, looked, pre_two, second, second_low = kernel_call(
        part(cross_forward_kernel, cross_start, len(w_cross)),
        "cross_forward",
        (
            shaped(query_rows, width, kind=BF),
            shaped(query_rows, width, kind=BF),
            shaped(query_rows, width),
            shaped(query_rows, width),
            shaped(query_rows, width, kind=BF),
        ),
        (first_query, image_keys, image_values, order, vec),
        w_cross,
        2 * width,
    )

    branches = [None, None]
    for j, values, low in ((1, first_text, text_low), (0, second, second_low)):
        count = values.shape[0]
        if j:
            low_all = gather_plane(low, (image_keys,), (second_low,))
        else:
            low_all = gather_plane(low)
        half = 4 * count
        pre_act, active, kept, sent = kernel_call(
            part(branch_up_kernel, j, len(w_ff)),
            "branch_up_%d" % j,
            (
                shaped(2 * half, ff),
                shaped(2 * half, ff, kind=BF),
                shaped(half, width),
                shaped(half, width, kind=BF),
            ),
            low_all,
            w_ff,
            ff_width,
        )
        out, grad_sum, grad_low, ends = kernel_call(
            part(branch_end_kernel, j),
            "branch_end_%d" % j,
            (
                shaped(count, width, kind=BF),
                shaped(count, width),
                shaped(count, width, kind=BF),
                shaped(8, width),
            ),
            (*scatter_plane(kept, sent), values, cotangent, vec),
        )
        kept, sent, grads = kernel_call(
            part(branch_down_kernel, j, len(w_ff)),
            "branch_down_%d" % j,
            (
                shaped(half, width),
                shaped(half, width, kind=BF),
                shaped(ff, ff_width, kind=BF),
            ),
            (*gather_plane(grad_low), *low_all, pre_act, active),
            w_ff,
            2 * width,
        )
        own = lax.psum_scatter(grads, "z", scatter_dimension=0, tiled=True)
        branches[j] = (out, grad_sum, ends, scatter_plane(kept, sent), own)
    query, text = branches
    layer_out = jnp.concatenate(
        [query[0].reshape(items, NQ, width), text[0].reshape(items, item_rows - NQ, width)],
        axis=1,
    )

    query_got = after(query[3][1], text[3][1])
    grad_cross, grad_ikey, grad_ivalue, two_low, grad_first, cross_ends = kernel_call(
        part(cross_backward_kernel, cross_start, len(w_cross)),
        "cross_backward",
        (
            shaped(query_rows, width, kind=BF),
            wide,
            wide,
            shaped(query_rows, width, kind=BF),
            shaped(query_rows, width),
            shaped(8, width),
        ),
        (query[3][0], query_got, query[1], pre_two, cross_rows, image_keys, image_values, order, vec),
        w_cross,
        2 * width,
        extra=(pltpu.VMEM((query_rows, width), BF),),
        cost=LATE,
    )
    packed = shaped(width // 2, cross_start + 2 * width, kind=BF)
    grad_cross = after(grad_cross, branches[1][4])
    cross_kept, cross_sent = kernel_call(
        cross_weights_kernel,
        "cross_weights",
        (packed, packed),
        (grad_cross, grad_ikey, grad_ivalue, two_low, first_query, looked, features, order),
        cost=LATE,
    )
    feature_order = after(order, cross_sent)
    feature_grad = kernel_call(
        part(feature_kernel, len(w_cross)),
        "feature_grad",
        shaped(items, image_rows, image_width),
        (grad_ikey, grad_ivalue, feature_order),
        w_cross,
        cross_start,
        cost=LATE,
    )
    cross_got = after(swap(cross_sent, step_c), feature_grad)
    cross_kept, cross_sent = halved(cross_kept, cross_got)

    grad_first = after(grad_first, cross_sent)
    packed = shaped(width // 2, 4 * width + 128, kind=BF)
    grad_qkv, grad_one, kept, sent = kernel_call(
        part(self_backward_kernel, items, len(w_self)),
        "self_backward",
        (shaped(rows, 3 * width, kind=BF), shaped(rows, width), packed, packed),
        (
            grad_first,
            *text[3],
            text[1],
            pre_one,
            qkv,
            mixture,
            flat,
            order,
            vec,
            cross_ends,
            query[2],
            text[2],
        ),
        w_self,
        width,
        text_lengths,
        (pltpu.VMEM((128, width), F32), pltpu.VMEM((rows, width), BF)),
        LATE,
    )
    feature_grad = with_layout_constraint(feature_grad, Layout((1, 0, 2)))
    cross_got = after(swap(cross_sent, step_b), feature_grad)
    sent = after(sent, cross_got, branches[0][4])
    cross_kept, cross_sent = halved(cross_kept, cross_got)
    kept, sent = halved(kept, swap(sent, step_c))
    hidden_order = after(order, sent)
    hidden_grad = kernel_call(
        part(hidden_kernel, len(w_self)),
        "hidden_grad",
        shaped(rows, width),
        (grad_qkv, grad_one, hidden_order),
        w_self,
        3 * width,
        cost=LATE,
    )
    cross_got = after(swap(cross_sent, step_a), hidden_grad)
    got = swap(sent, step_b)
    if planes == 4:
        cross_kept, cross_sent = halved(cross_kept, cross_got)
        kept, sent = halved(kept, after(got, cross_sent))
        cross_got = after(swap(cross_sent, step_z1), sent)
        cross_kept, cross_sent = halved(cross_kept, cross_got)
        kept, sent = halved(kept, after(swap(sent, step_a), cross_sent))
        cross_got = after(swap(cross_sent, step_z2), sent)
        own_cross = cross_kept.astype(F32) + cross_got.astype(F32)
        kept, sent = halved(kept, swap(sent, step_z1))
        own_self = kept.astype(F32) + swap(sent, step_z2).astype(F32)
    else:
        own_cross = scatter_rest(cross_kept, cross_got)
        kept, sent = halved(kept, got)
        own_self = scatter_rest(kept, swap(sent, step_a))
    own_ff = [after(branch[4], sent).astype(F32) for branch in branches]
    own_sums = own_self[:, 4 * width : 4 * width + n_vectors].T
    own_up = [own[:, :width].T for own in own_ff]
    own_down = [own[:, width : 2 * width] for own in own_ff]
    own_up_bias = [own[:, 2 * width] for own in own_ff]
    return (
        layer_out,
        hidden_grad.reshape(items, item_rows, width),
        feature_grad,
        jnp.stack([own_self[:, n * width : (n + 1) * width] for n in range(3)]),
        own_self[:, 3 * width : 4 * width],
        own_sums[0:3],
        own_sums[3:7],
        own_sums[7:11],
        own_cross[:, cross_start : cross_start + width],
        own_cross[:, cross_start + width :],
        jnp.stack([own_cross[:, n * image_width : (n + 1) * image_width].T for n in range(2)]),
        own_sums[11:14],
        jnp.stack(own_up),
        jnp.stack(own_up_bias),
        jnp.stack(own_down),
        own_sums[14:16],
    )


def solution(mesh):
    dp, pair = mesh.devices.shape
    fine = Mesh(mesh.devices.reshape(dp // 4, 2, 2, pair), AXES)
    first, second, third = P(AXES), P(None, AXES), P(None, None, AXES)
    in_specs = (
        first, first, first, first,
        second, first, second, second, second, first, first,
        third, second, third, second, second, second,
    )
    out_specs = (
        first, first, first,
        second, first, second, second, second, first, first,
        third, second, third, second, second, second,
    )
    return jax.shard_map(shards, mesh=fine, in_specs=in_specs, out_specs=out_specs, check_vma=False)
```

```python
import functools

import jax
import jax.numpy as jnp
from jax import lax
from jax.experimental import pallas as pl
from jax.experimental.layout import Layout, with_layout_constraint
from jax.experimental.pallas import tpu as pltpu
from jax.sharding import Mesh, PartitionSpec as P

HEAD = 64
NQ = 32
GROUP = 256
PER = GROUP // HEAD
eps = 1e-06
masked_off = 1000000000.0
LATE = 4
AXES = ("z", "x", "c", "y")
BF = jnp.bfloat16
F32 = jnp.float32


def coords(index):
    return (index // 8, index // 4 % 2, index // 2 % 2, index % 2)


def pairs(count, move):
    result = []
    for source in range(count):
        z, x, c, y = move(*coords(source))
        result.append((source, ((z * 2 + x) * 2 + c) * 2 + y))
    return result


def step_a(z, x, c, y):
    return (z, x ^ 1, c, y) if c == 0 else (z, x, c, y ^ 1)


def step_b(z, x, c, y):
    return (z, x, c, y ^ 1) if c == 0 else (z, x ^ 1, c, y)


def step_c(z, x, c, y):
    return (z, x, c ^ 1, y)


def swap(value, move):
    count = lax.axis_size(AXES)
    return lax.ppermute(value, AXES, pairs(count, move))


def swap_z(value, distance):
    return swap(value, lambda z, x, c, y: (z ^ distance, x, c, y))


def gather_z(unit):
    if lax.axis_size("z") == 4:
        near = jnp.concatenate([unit, swap_z(unit, 2)], axis=0)
        return jnp.concatenate([near, swap_z(near, 1)], axis=0)
    return lax.all_gather(unit, "z", axis=0, tiled=True)


def gather_z_direct(unit):
    if lax.axis_size("z") == 4:
        one, two, three = (swap_z(unit, k) for k in (1, 2, 3))
        return jnp.concatenate([unit, two, one, three], axis=0)
    return lax.all_gather(unit, "z", axis=0, tiled=True)


def gather_all(near, first=(), last=()):
    a = swap(after(near, *first), step_a)
    b = swap(after(near, *last), step_b)
    pieces = [near, a, b, swap(a, step_b)]
    pieces.append(swap(after(near, *last), step_c))
    return pieces + [swap(piece, step_c) for piece in pieces[1:3]]


def finish_all(pieces, *gates):
    return pieces + [swap(after(pieces[3], *gates), step_c)]


def gather_plane(rows, first=(), second=()):
    rows = jnp.concatenate([rows, after(swap(rows, step_a), *first)], axis=0)
    rows = jnp.concatenate([rows, after(swap(rows, step_b), *second)], axis=0)
    return [rows, swap(rows, step_c)]


def after(value, *earlier):
    return lax.optimization_barrier((value,) + earlier)[0]


def add_low(left, right):
    return (left.astype(F32) + right.astype(F32)).astype(BF)


def halved(kept, got):
    half = got.shape[0] // 2
    return add_low(kept[:half], got[:half]), add_low(kept[half:], got[half:])


def scatter_plane(kept, sent):
    for move in (step_c, step_b):
        kept, sent = halved(kept, swap(sent, move))
    return kept, swap(sent, step_a)


def step_z1(z, x, c, y):
    return (z ^ 1, x, c, y)


def step_z2(z, x, c, y):
    return (z ^ 2, x, c, y)


def scatter_rest(kept, got):
    return lax.psum_scatter(add_low(kept, got), "z", scatter_dimension=0, tiled=True).astype(F32)


def slot_owner(count):
    z, x, c, y = (lax.axis_index(name) for name in AXES)
    planes = count // 8
    slot = jnp.arange(count)
    k = slot % planes
    alpha = slot // planes % 2
    beta = slot // (2 * planes) % 2
    core = c ^ (slot // (4 * planes))
    flip_x = jnp.where(core == 0, alpha, beta)
    flip_y = jnp.where(core == 0, beta, alpha)
    plane = z ^ (k % 2 * 2 + k // 2) if planes == 4 else k
    return ((plane * 2 + (x ^ flip_x)) * 2 + core) * 2 + (y ^ flip_y)


def place_of_slot(width):
    count = lax.axis_size(AXES)
    each = width // count
    source = (slot_owner(count)[:, None] * each + jnp.arange(each)[None, :]).reshape(-1)
    return (source[:, None] == jnp.arange(width)[None, :]).astype(BF)


def by_slot(values, order):
    return dot_t(values, order).astype(BF)


def by_slot_turned(values, order):
    return dot_t(order, values).astype(BF)


def by_place(values, order):
    return dot(values.astype(BF), order)


def dot(left, right):
    return lax.dot_general(
        left, right, (((left.ndim - 1,), (0,)), ((), ())), preferred_element_type=F32
    )


def dot_t(left, right):
    return lax.dot_general(
        left, right, (((left.ndim - 1,), (1,)), ((), ())), preferred_element_type=F32
    )


def outer(left, right):
    lead = tuple(range(left.ndim - 1))
    return lax.dot_general(left, right, ((lead, lead), ((), ())), preferred_element_type=F32)


def column_sum(values):
    return jnp.sum(values.astype(F32), axis=0, keepdims=True)


def layer_norm(values, scale, shift):
    center = values - jnp.mean(values, axis=-1, keepdims=True)
    spread = jnp.mean(center * center, axis=-1, keepdims=True)
    return center * lax.rsqrt(spread + eps) * scale + shift


def norm_back(values, scale, gradient):
    center = values - jnp.mean(values, axis=-1, keepdims=True)
    spread = jnp.mean(center * center, axis=-1, keepdims=True)
    inverse = lax.rsqrt(spread + eps)
    normal = center * inverse
    inner = gradient * scale
    result = inverse * (
        inner
        - jnp.mean(inner, axis=-1, keepdims=True)
        - normal * jnp.mean(inner * normal, axis=-1, keepdims=True)
    )
    return result, column_sum(gradient * normal), column_sum(gradient)


def gelu_parts(values):
    half = F32(0.5) + F32(0.5) * lax.erf(values * F32(0.5**0.5))
    return half


def gelu_slope(values):
    density = jnp.exp(values * values * F32(-0.5)) * F32((2.0 * 3.141592653589793) ** -0.5)
    return gelu_parts(values) + values * density


def head_masks():
    lane = lax.broadcasted_iota(jnp.int32, (1, GROUP), 1) // HEAD
    return [(lane == h).astype(F32).astype(BF) for h in range(PER)]


def spread_heads(rows, masks):
    return jnp.concatenate([rows * mask for mask in masks], axis=0)


def fold_heads(stacked, masks, count):
    total = None
    for h, mask in enumerate(masks):
        part = stacked[h * count : (h + 1) * count] * mask.astype(F32)
        total = part if total is None else total + part
    return total


def softmax_rows(scores):
    shifted = jnp.exp(scores - jnp.max(scores, axis=-1, keepdims=True))
    return shifted / jnp.sum(shifted, axis=-1, keepdims=True)


def self_mask(length, rows):
    shape = (PER * rows, rows)
    row = lax.broadcasted_iota(jnp.int32, shape, 0) % rows
    col = lax.broadcasted_iota(jnp.int32, shape, 1)
    allowed = (col < NQ) | ((row >= NQ) & (col <= row) & (col - NQ < length))
    return jnp.where(allowed, F32(0.0), F32(-masked_off))


def attend_group_back(q, k, v, mask_add, grad, masks, count):
    q = spread_heads(q, masks)
    grad = spread_heads(grad, masks)
    weights = softmax_rows(dot_t(q, k) * HEAD ** (-0.5) + mask_add)
    grad_value = outer(weights.astype(BF), grad).astype(BF)
    grad_weight = dot_t(grad, v)
    grad_score = (
        weights * (grad_weight - jnp.sum(grad_weight * weights, axis=-1, keepdims=True))
    ).astype(BF)
    grad_query = fold_heads(dot(grad_score, k), masks, count) * HEAD ** (-0.5)
    grad_key = outer(grad_score, q) * HEAD ** (-0.5)
    return grad_query.astype(BF), grad_key.astype(BF), grad_value


def repeat(count, body):
    def step(i, carry):
        body(i)
        return carry

    lax.fori_loop(0, count, step, 0)


def stretch(i, count):
    return pl.ds(pl.multiple_of(i * count, count), count)


def fetch(pieces, start, target, sems):
    width = target.shape[1]
    copies = []
    row = 0
    for n, piece in enumerate(pieces):
        count = piece.shape[0]
        source = piece.at[:, pl.ds(start, width)]
        copies.append(
            pltpu.make_async_copy(source, target.at[pl.ds(row, count)], sems.at[n])
        )
        row += count
    for copy in copies:
        copy.start()
    return copies


def finish(copies):
    for copy in copies:
        copy.wait()


def turned_rows(rows):
    rows = list(rows)
    each = rows[0].shape[1]
    rows.append(jnp.zeros((128 - sum(row.shape[0] for row in rows), each), F32))
    return jnp.concatenate(rows, axis=0).T.astype(BF)


def pack_kernel(refs):
    project_ref, output_ref, up_ref, down_ref, bias_ref = refs[:5]
    vector_refs, self_ref, ff_ref = refs[5:-2], refs[-2], refs[-1]
    width = output_ref.shape[1]
    for n in range(3):
        self_ref[:, pl.ds(n * width, width)] = project_ref[n]
    self_ref[:, pl.ds(3 * width, width)] = output_ref[...]
    vectors = turned_rows(ref[...].astype(F32) for ref in vector_refs)
    self_ref[:, pl.ds(4 * width, 128)] = vectors
    for n in range(2):
        start = n * (2 * width + 128)
        ff_ref[:, pl.ds(start, width)] = up_ref[n]
        ff_ref[:, pl.ds(start + width, width)] = down_ref[n]
        bias = bias_ref[n : n + 1, :].astype(F32)
        ff_ref[:, pl.ds(start + 2 * width, 128)] = turned_rows([bias])


def self_forward_kernel(items, n_pieces, refs):
    length_ref, hidden_ref, order_ref = refs[:3]
    pieces = refs[3 : 3 + n_pieces]
    qkv_ref, mix_ref, pre_ref, query_ref, text_ref, low_ref, vec_ref, w_ref, sems = refs[
        3 + n_pieces :
    ]
    rows_all, width = hidden_ref.shape
    copies = fetch(pieces, 0, w_ref, sems)
    order = order_ref[...]
    hidden_slot = by_slot(hidden_ref[...], order)
    finish(copies)
    vec = outer(w_ref[:, pl.ds(4 * width, 128)], order)[: vec_ref.shape[0]]
    vec_ref[...] = vec
    bias = [vec[0:1], F32(0.0), vec[1:2]]
    for n in range(3):
        cols = pl.ds(n * width, width)
        qkv_ref[:, cols] = (dot(hidden_slot, w_ref[:, cols]) + bias[n]).astype(BF)
    masks = head_masks()
    count = rows_all // items

    def attend(i):
        rows = stretch(i, count)
        mask_add = self_mask(length_ref[i], count)
        for g in range(width // GROUP):
            cols = [pl.ds(n * width + g * GROUP, GROUP) for n in range(3)]
            q = spread_heads(qkv_ref[rows, cols[0]], masks)
            scores = dot_t(q, qkv_ref[rows, cols[1]]) * HEAD ** (-0.5) + mask_add
            weights = softmax_rows(scores).astype(BF)
            mixed = dot(weights, qkv_ref[rows, cols[2]])
            mix_ref[rows, cols[0]] = fold_heads(mixed, masks, count).astype(BF)

    repeat(items, attend)
    mixture_slot = by_slot(mix_ref[...], order)
    pre = dot(mixture_slot, w_ref[:, pl.ds(3 * width, width)])
    pre = pre + vec[2:3] + hidden_ref[...].astype(F32)
    pre_ref[...] = pre
    first = layer_norm(pre, vec[3:4], vec[7:8])
    text = count - NQ
    for i in range(items):
        query_ref[pl.ds(i * NQ, NQ), :] = first[i * count : i * count + NQ]
        part = first[i * count + NQ : (i + 1) * count]
        text_ref[pl.ds(i * text, text), :] = part
        low_ref[pl.ds(i * text, text), :] = part.astype(BF)


def image_kernel(n_pieces, refs):
    feature_ref, order_ref, vec_ref = refs[:3]
    pieces = refs[3 : 3 + n_pieces]
    key_ref, value_ref, w_ref, sems = refs[3 + n_pieces :]
    items, _, image_width = feature_ref.shape
    copies = fetch(pieces, 0, w_ref, sems)
    order = order_ref[...]
    bias_slot = dot_t(vec_ref[...].astype(BF), order)[12:13]
    finish(copies)

    def project(i):
        rows = feature_ref[i]
        keys = dot_t(rows, w_ref[:, pl.ds(0, image_width)])
        key_ref[i] = by_place(keys, order_ref[...]).astype(BF)
        values = dot_t(rows, w_ref[:, pl.ds(image_width, image_width)]) + bias_slot
        value_ref[i] = by_place(values, order_ref[...]).astype(BF)

    repeat(items, project)


def cross_forward_kernel(start, n_pieces, refs):
    first_ref, key_ref, value_ref, order_ref, vec_ref = refs[:5]
    pieces = refs[5 : 5 + n_pieces]
    rows_ref, look_ref, pre_ref, second_ref, low_ref, w_ref, sems = refs[5 + n_pieces :]
    copies = fetch(pieces, start, w_ref, sems)
    items = key_ref.shape[0]
    width = first_ref.shape[1]
    count = first_ref.shape[0] // items
    order = order_ref[...]
    vec = vec_ref[...]
    masks = head_masks()
    first_slot = by_slot(first_ref[...].astype(BF), order)
    finish(copies)
    rows_ref[...] = (dot(first_slot, w_ref[:, pl.ds(0, width)]) + vec[11:12]).astype(BF)

    def attend(i):
        rows = stretch(i, count)
        for g in range(width // GROUP):
            cols = pl.ds(g * GROUP, GROUP)
            q = spread_heads(rows_ref[rows, cols], masks)
            scores = dot_t(q, key_ref[i, :, cols]) * HEAD ** (-0.5)
            mixed = dot(softmax_rows(scores).astype(BF), value_ref[i, :, cols])
            look_ref[rows, cols] = fold_heads(mixed, masks, count).astype(BF)

    repeat(items, attend)
    pre = dot(by_slot(look_ref[...], order), w_ref[:, pl.ds(width, width)])
    pre = pre + vec[13:14] + first_ref[...]
    pre_ref[...] = pre
    second = layer_norm(pre, vec[4:5], vec[8:9])
    second_ref[...] = second
    low_ref[...] = second.astype(BF)


def branch_up_kernel(branch, n_pieces, refs):
    low_refs = refs[:2]
    pieces = refs[2 : 2 + n_pieces]
    pre_ref, act_ref, kept_ref, sent_ref, w_ref, sems = refs[2 + n_pieces :]
    half, width = low_refs[0].shape
    copies = fetch(pieces, branch * (2 * width + 128), w_ref, sems)
    finish(copies)
    first_lane = (lax.broadcasted_iota(jnp.int32, (8, 128), 1) == 0).astype(F32).astype(BF)
    bias = dot_t(first_lane, w_ref[:, pl.ds(2 * width, 128)])[0:1]
    for n, (low_ref, out_ref) in enumerate(zip(low_refs, (kept_ref, sent_ref))):
        rows = pl.ds(n * half, half)
        pre = dot_t(low_ref[...], w_ref[:, pl.ds(0, width)]) + bias
        pre_ref[rows, :] = pre
        active = (pre * gelu_parts(pre)).astype(BF)
        act_ref[rows, :] = active
        out_ref[...] = dot(active, w_ref[:, pl.ds(width, width)]).astype(out_ref.dtype)


def branch_end_kernel(branch, refs):
    kept_ref, got_ref, value_ref, cot_ref, vec_ref = refs[:5]
    out_ref, grad_ref, low_ref, sum_ref = refs[5:]
    items, count, _ = cot_ref.shape
    vec = vec_ref[...]
    gain, shift = vec[5 + branch : 6 + branch], vec[9 + branch : 10 + branch]
    total = kept_ref[...].astype(F32) + got_ref[...].astype(F32)
    total = total + vec[14 + branch : 15 + branch] + value_ref[...]
    start, size = (NQ, count - NQ) if branch else (0, NQ)
    cot = jnp.concatenate([cot_ref[i, start : start + size, :] for i in range(items)], axis=0)
    out_ref[...] = layer_norm(total, gain, shift).astype(BF)
    grad, gain_grad, shift_grad = norm_back(total, gain, cot.astype(F32))
    grad_ref[...] = grad
    low = grad.astype(BF)
    low_ref[...] = low
    sum_ref[0:1, :] = gain_grad
    sum_ref[1:2, :] = shift_grad
    sum_ref[2:3, :] = column_sum(low)


def branch_down_kernel(branch, n_pieces, refs):
    grad_refs, low_refs, (pre_ref, act_ref) = refs[:2], refs[2:4], refs[4:6]
    pieces = refs[6 : 6 + n_pieces]
    rest = refs[6 + n_pieces :]
    kept_ref, sent_ref, own_ref, w_ref, sems = rest
    half, width = low_refs[0].shape
    copies = fetch(pieces, branch * (2 * width + 128), w_ref, sems)
    finish(copies)
    grads = []
    for n, out_ref in enumerate((kept_ref, sent_ref)):
        rows = pl.ds(n * half, half)
        back = dot_t(grad_refs[n][...], w_ref[:, pl.ds(width, width)])
        grad_pre = (gelu_slope(pre_ref[rows, :]) * back).astype(BF)
        grads.append(grad_pre)
        out_ref[...] = dot(grad_pre, w_ref[:, pl.ds(0, width)]).astype(out_ref.dtype)
    grad_pre = jnp.concatenate(grads, axis=0)
    low = jnp.concatenate([ref[...] for ref in low_refs], axis=0)
    grad_low = jnp.concatenate([ref[...] for ref in grad_refs], axis=0)
    own_ref[:, pl.ds(0, width)] = outer(grad_pre, low).astype(BF)
    own_ref[:, pl.ds(width, width)] = outer(act_ref[...], grad_low).astype(BF)
    sums = outer(grad_pre, jnp.ones((2 * half, 128), BF)).astype(BF)
    own_ref[:, pl.ds(2 * width, 128)] = sums


def cross_backward_kernel(start, n_pieces, refs):
    kept_ref, got_ref, sum_ref, pre_ref, q_ref, k_ref, v_ref, order_ref, vec_ref = refs[:9]
    pieces = refs[9 : 9 + n_pieces]
    dq_ref, dk_ref, dv_ref, low_ref, first_ref, row_ref, w_ref, look_ref, sems = refs[
        9 + n_pieces :
    ]
    copies = fetch(pieces, start, w_ref, sems)
    items = k_ref.shape[0]
    width = q_ref.shape[1]
    count = q_ref.shape[0] // items
    order = order_ref[...]
    vec = vec_ref[...]
    masks = head_masks()
    gradient = kept_ref[...].astype(F32) + got_ref[...].astype(F32) + sum_ref[...]
    grad_two, gain_grad, shift_grad = norm_back(pre_ref[...], vec[4:5], gradient)
    low = grad_two.astype(BF)
    low_ref[...] = low
    finish(copies)
    look_ref[...] = by_place(dot_t(low, w_ref[:, pl.ds(width, width)]), order).astype(BF)

    def attend(i):
        rows = stretch(i, count)
        for g in range(width // GROUP):
            cols = pl.ds(g * GROUP, GROUP)
            dq, dk, dv = attend_group_back(
                q_ref[rows, cols],
                k_ref[i, :, cols],
                v_ref[i, :, cols],
                F32(0.0),
                look_ref[rows, cols],
                masks,
                count,
            )
            dq_ref[rows, cols] = dq
            dk_ref[i, :, cols] = dk
            dv_ref[i, :, cols] = dv
            row_ref[3:4, cols] = row_ref[3:4, cols] + column_sum(dv)

    row_ref[3:4, :] = jnp.zeros((1, width), F32)
    repeat(items, attend)
    grad_cross = dq_ref[...]
    back = dot_t(grad_cross, w_ref[:, pl.ds(0, width)])
    first_ref[...] = grad_two + by_place(back, order)
    row_ref[0:1, :] = gain_grad
    row_ref[1:2, :] = shift_grad
    row_ref[2:3, :] = column_sum(grad_cross)
    row_ref[4:5, :] = column_sum(low)


def cross_weights_kernel(refs):
    dq_ref, dk_ref, dv_ref, low_ref, first_ref, look_ref, feature_ref, order_ref = refs[:8]
    kept_ref, sent_ref = refs[8:]
    items, _, image_width = feature_ref.shape
    half, width = order_ref.shape[0] // 2, order_ref.shape[1]
    for part, out_ref in enumerate((kept_ref, sent_ref)):
        order = order_ref[pl.ds(part * half, half), :]
        for n, grad_ref in enumerate((dk_ref, dv_ref)):
            total = None
            for i in range(items):
                turned = by_slot_turned(grad_ref[i], order)
                product = dot(turned, feature_ref[i])
                total = product if total is None else total + product
            out_ref[:, pl.ds(n * image_width, image_width)] = total.astype(BF)
        start = 2 * image_width
        turned = by_slot_turned(first_ref[...].astype(BF), order)
        out_ref[:, pl.ds(start, width)] = dot(turned, dq_ref[...]).astype(BF)
        turned = by_slot_turned(look_ref[...], order)
        out_ref[:, pl.ds(start + width, width)] = dot(turned, low_ref[...]).astype(BF)


def feature_kernel(n_pieces, refs):
    dk_ref, dv_ref, order_ref = refs[:3]
    pieces = refs[3 : 3 + n_pieces]
    out_ref, w_ref, sems = refs[3 + n_pieces :]
    items, _, image_width = out_ref.shape
    copies = fetch(pieces, 0, w_ref, sems)
    finish(copies)

    def back(i):
        keys, values = (by_slot(ref[i], order_ref[...]) for ref in (dk_ref, dv_ref))
        total = dot(keys, w_ref[:, pl.ds(0, image_width)])
        out_ref[i] = total + dot(values, w_ref[:, pl.ds(image_width, image_width)])

    repeat(items, back)


def self_backward_kernel(items, n_pieces, refs):
    length_ref, query_ref, kept_ref, got_ref, text_ref, pre_ref, qkv_ref = refs[:7]
    mix_ref, hidden_ref, order_ref, vec_ref = refs[7:11]
    row_refs = refs[11:14]
    pieces = refs[14 : 14 + n_pieces]
    grad_ref, one_ref, g_kept_ref, g_sent_ref, w_ref, sum_ref, mixed_ref, sems = refs[
        14 + n_pieces :
    ]
    copies = fetch(pieces, 3 * pre_ref.shape[1], w_ref, sems)
    rows_all, width = pre_ref.shape
    count = rows_all // items
    text = count - NQ
    order = order_ref[...]
    vec = vec_ref[...]
    masks = head_masks()
    text_grad = kept_ref[...].astype(F32) + got_ref[...].astype(F32) + text_ref[...]
    query_grad = query_ref[...]
    gradient = []
    for i in range(items):
        gradient.append(query_grad[i * NQ : (i + 1) * NQ])
        gradient.append(text_grad[i * text : (i + 1) * text])
    gradient = jnp.concatenate(gradient, axis=0)
    grad_one, gain_grad, shift_grad = norm_back(pre_ref[...], vec[3:4], gradient)
    one_ref[...] = grad_one
    low = grad_one.astype(BF)
    finish(copies)
    mixed_ref[...] = by_place(dot_t(low, w_ref[...]), order).astype(BF)

    def attend(i):
        rows = stretch(i, count)
        mask_add = self_mask(length_ref[i], count)
        for g in range(width // GROUP):
            cols = [pl.ds(n * width + g * GROUP, GROUP) for n in range(3)]
            results = attend_group_back(
                *[qkv_ref[rows, col] for col in cols],
                mask_add,
                mixed_ref[rows, cols[0]],
                masks,
                count,
            )
            for col, value in zip(cols, results):
                grad_ref[rows, col] = value

    repeat(items, attend)
    query_rows, query_ends, text_ends = row_refs
    sum_ref[...] = jnp.zeros(sum_ref.shape, F32)
    total = column_sum(grad_ref[...])
    listed = [
        total[:, :width],
        total[:, 2 * width :],
        column_sum(low),
        gain_grad,
        query_rows[0:1, :],
        query_ends[0:1, :],
        text_ends[0:1, :],
        shift_grad,
        query_rows[1:2, :],
        query_ends[1:2, :],
        text_ends[1:2, :],
        query_rows[2:3, :],
        query_rows[3:4, :],
        query_rows[4:5, :],
        query_ends[2:3, :],
        text_ends[2:3, :],
    ]
    for n, value in enumerate(listed):
        sum_ref[n : n + 1, :] = value
    sums = sum_ref[...].astype(BF)
    half = width // 2
    for part, out_ref in enumerate((g_kept_ref, g_sent_ref)):
        block = order_ref[pl.ds(part * half, half), :]
        turned = by_slot_turned(hidden_ref[...], block)

        def weigh(n):
            cols = stretch(n, width)
            out_ref[:, cols] = dot(turned, grad_ref[:, cols]).astype(BF)

        repeat(3, weigh)
        turned = by_slot_turned(mix_ref[...], block)
        out_ref[:, pl.ds(3 * width, width)] = dot(turned, low).astype(BF)
        out_ref[:, pl.ds(4 * width, 128)] = dot_t(block, sums).astype(BF)


def hidden_kernel(n_pieces, refs):
    grad_ref, one_ref, order_ref = refs[:3]
    pieces = refs[3 : 3 + n_pieces]
    out_ref, w_ref, sems = refs[3 + n_pieces :]
    copies = fetch(pieces, 0, w_ref, sems)
    finish(copies)
    width = one_ref.shape[1]

    def part(n, total):
        cols = stretch(n, width)
        return total + dot_t(grad_ref[:, cols], w_ref[:, cols])

    back = lax.fori_loop(0, 3, part, jnp.zeros(one_ref.shape, F32))
    out_ref[...] = one_ref[...] + by_place(back, order_ref[...])


def shaped(*dims, kind=F32):
    return jax.ShapeDtypeStruct(dims, kind)


def kernel_call(
    body, name, outs, inputs, pieces=(), loaded=None, lengths=None, extra=(), cost=12
):
    vmem = pl.BlockSpec(memory_space=pltpu.VMEM)
    specs = [vmem] * len(inputs) + [pl.BlockSpec(memory_space=pl.ANY)] * len(pieces)
    arrays = tuple(inputs) + tuple(pieces)
    if lengths is not None:
        specs = [pl.BlockSpec(memory_space=pltpu.SMEM)] + specs
        arrays = (lengths,) + arrays
    scratch = []
    if loaded is not None:
        rows = sum(piece.shape[0] for piece in pieces)
        scratch = [pltpu.VMEM((rows, loaded), BF)] + list(extra)
        scratch.append(pltpu.SemaphoreType.DMA((len(pieces),)))
    return pl.pallas_call(
        lambda *refs: body(refs),
        name=name,
        out_shape=outs,
        in_specs=specs,
        out_specs=jax.tree.map(lambda _: vmem, outs),
        scratch_shapes=scratch,
        cost_estimate=pl.CostEstimate(
            flops=int(cost * 900_000_000), bytes_accessed=int(cost * 3_000_000), transcendentals=0
        ),
    )(*arrays)


def shards(
    hidden,
    features,
    text_lengths,
    cotangent,
    self_project,
    self_output,
    self_bias,
    norm_gain,
    norm_bias,
    cross_query,
    cross_output,
    image_project,
    cross_bias,
    expand_weight,
    expand_bias,
    reduce_weight,
    reduce_bias,
):
    part = functools.partial
    items, item_rows, width = hidden.shape
    each = self_output.shape[0]
    image_rows, image_width = features.shape[1:]
    ff_each = reduce_weight.shape[1]
    planes = lax.axis_size("z")
    rows = items * item_rows
    query_rows, text_rows = items * NQ, items * (item_rows - NQ)
    ff = planes * ff_each
    order = place_of_slot(width)
    flat = hidden.reshape(rows, width)

    vectors = (self_bias, norm_gain, norm_bias, cross_bias, reduce_bias)
    n_vectors = sum(v.shape[0] for v in vectors)
    ff_width = 2 * width + 128
    up_turned = jnp.swapaxes(expand_weight, 1, 2)
    unit_self, unit_ff = kernel_call(
        pack_kernel,
        "pack",
        (shaped(each, 4 * width + 128, kind=BF), shaped(ff_each, 2 * ff_width, kind=BF)),
        (self_project, self_output, up_turned, reduce_weight, expand_bias, *vectors),
        cost=1,
    )
    image_turned = jnp.swapaxes(image_project, 1, 2)
    unit_cross = jnp.concatenate(
        [image_turned[0], image_turned[1], cross_query, cross_output], axis=1
    )
    w_ff = [lax.all_gather(unit_ff, "z", axis=0, tiled=True)]
    near_self = gather_z_direct(unit_self)
    w_self = finish_all(gather_all(near_self))
    near_cross = gather_z(after(unit_cross, near_self))
    w_cross = gather_all(near_cross, w_self[1:3], w_self[3:4])
    cross_start = 2 * image_width

    qkv, mixture, pre_one, first_query, first_text, text_low, vec = kernel_call(
        part(self_forward_kernel, items, len(w_self)),
        "self_forward",
        (
            shaped(rows, 3 * width, kind=BF),
            shaped(rows, width, kind=BF),
            shaped(rows, width),
            shaped(query_rows, width),
            shaped(text_rows, width),
            shaped(text_rows, width, kind=BF),
            shaped(n_vectors, width),
        ),
        (flat, order),
        w_self,
        4 * width + 128,
        text_lengths,
    )

    w_cross = finish_all(w_cross, first_query)
    wide = shaped(items, image_rows, width, kind=BF)
    image_keys, image_values = kernel_call(
        part(image_kernel, len(w_cross)),
        "image_rows",
        (wide, wide),
        (features, order, vec),
        w_cross,
        cross_start,
    )
    cross_rows, looked, pre_two, second, second_low = kernel_call(
        part(cross_forward_kernel, cross_start, len(w_cross)),
        "cross_forward",
        (
            shaped(query_rows, width, kind=BF),
            shaped(query_rows, width, kind=BF),
            shaped(query_rows, width),
            shaped(query_rows, width),
            shaped(query_rows, width, kind=BF),
        ),
        (first_query, image_keys, image_values, order, vec),
        w_cross,
        2 * width,
    )

    branches = [None, None]
    for j, values, low in ((1, first_text, text_low), (0, second, second_low)):
        count = values.shape[0]
        if j:
            low_all = gather_plane(low, (image_keys,), (second_low,))
        else:
            low_all = gather_plane(low)
        half = 4 * count
        pre_act, active, kept, sent = kernel_call(
            part(branch_up_kernel, j, len(w_ff)),
            "branch_up_%d" % j,
            (
                shaped(2 * half, ff),
                shaped(2 * half, ff, kind=BF),
                shaped(half, width),
                shaped(half, width, kind=BF),
            ),
            low_all,
            w_ff,
            ff_width,
        )
        out, grad_sum, grad_low, ends = kernel_call(
            part(branch_end_kernel, j),
            "branch_end_%d" % j,
            (
                shaped(count, width, kind=BF),
                shaped(count, width),
                shaped(count, width, kind=BF),
                shaped(8, width),
            ),
            (*scatter_plane(kept, sent), values, cotangent, vec),
        )
        kept, sent, grads = kernel_call(
            part(branch_down_kernel, j, len(w_ff)),
            "branch_down_%d" % j,
            (
                shaped(half, width),
                shaped(half, width, kind=BF),
                shaped(ff, ff_width, kind=BF),
            ),
            (*gather_plane(grad_low), *low_all, pre_act, active),
            w_ff,
            2 * width,
        )
        own = lax.psum_scatter(grads, "z", scatter_dimension=0, tiled=True)
        branches[j] = (out, grad_sum, ends, scatter_plane(kept, sent), own)
    query, text = branches
    layer_out = jnp.concatenate(
        [query[0].reshape(items, NQ, width), text[0].reshape(items, item_rows - NQ, width)],
        axis=1,
    )

    query_got = after(query[3][1], text[3][1])
    grad_cross, grad_ikey, grad_ivalue, two_low, grad_first, cross_ends = kernel_call(
        part(cross_backward_kernel, cross_start, len(w_cross)),
        "cross_backward",
        (
            shaped(query_rows, width, kind=BF),
            wide,
            wide,
            shaped(query_rows, width, kind=BF),
            shaped(query_rows, width),
            shaped(8, width),
        ),
        (query[3][0], query_got, query[1], pre_two, cross_rows, image_keys, image_values, order, vec),
        w_cross,
        2 * width,
        extra=(pltpu.VMEM((query_rows, width), BF),),
        cost=LATE,
    )
    packed = shaped(width // 2, cross_start + 2 * width, kind=BF)
    grad_cross = after(grad_cross, branches[1][4])
    cross_kept, cross_sent = kernel_call(
        cross_weights_kernel,
        "cross_weights",
        (packed, packed),
        (grad_cross, grad_ikey, grad_ivalue, two_low, first_query, looked, features, order),
        cost=LATE,
    )
    feature_order = after(order, cross_sent)
    feature_grad = kernel_call(
        part(feature_kernel, len(w_cross)),
        "feature_grad",
        shaped(items, image_rows, image_width),
        (grad_ikey, grad_ivalue, feature_order),
        w_cross,
        cross_start,
        cost=LATE,
    )
    cross_got = after(swap(cross_sent, step_c), feature_grad)
    cross_kept, cross_sent = halved(cross_kept, cross_got)

    grad_first = after(grad_first, cross_sent)
    packed = shaped(width // 2, 4 * width + 128, kind=BF)
    grad_qkv, grad_one, kept, sent = kernel_call(
        part(self_backward_kernel, items, len(w_self)),
        "self_backward",
        (shaped(rows, 3 * width, kind=BF), shaped(rows, width), packed, packed),
        (
            grad_first,
            *text[3],
            text[1],
            pre_one,
            qkv,
            mixture,
            flat,
            order,
            vec,
            cross_ends,
            query[2],
            text[2],
        ),
        w_self,
        width,
        text_lengths,
        (pltpu.VMEM((128, width), F32), pltpu.VMEM((rows, width), BF)),
        LATE,
    )
    feature_grad = with_layout_constraint(feature_grad, Layout((1, 0, 2)))
    cross_got = after(swap(cross_sent, step_b), feature_grad)
    sent = after(sent, cross_got, branches[0][4])
    cross_kept, cross_sent = halved(cross_kept, cross_got)
    kept, sent = halved(kept, swap(sent, step_c))
    hidden_order = after(order, sent)
    hidden_grad = kernel_call(
        part(hidden_kernel, len(w_self)),
        "hidden_grad",
        shaped(rows, width),
        (grad_qkv, grad_one, hidden_order),
        w_self,
        3 * width,
        cost=LATE,
    )
    cross_got = after(swap(cross_sent, step_a), hidden_grad)
    got = swap(sent, step_b)
    if planes == 4:
        cross_kept, cross_sent = halved(cross_kept, cross_got)
        kept, sent = halved(kept, after(got, cross_sent))
        cross_got = after(swap(cross_sent, step_z1), sent)
        cross_kept, cross_sent = halved(cross_kept, cross_got)
        kept, sent = halved(kept, after(swap(sent, step_a), cross_sent))
        cross_got = after(swap(cross_sent, step_z2), sent)
        own_cross = cross_kept.astype(F32) + cross_got.astype(F32)
        kept, sent = halved(kept, swap(sent, step_z1))
        own_self = kept.astype(F32) + swap(sent, step_z2).astype(F32)
    else:
        own_cross = scatter_rest(cross_kept, cross_got)
        kept, sent = halved(kept, got)
        own_self = scatter_rest(kept, swap(sent, step_a))
    own_ff = [after(branch[4], sent).astype(F32) for branch in branches]
    own_sums = own_self[:, 4 * width : 4 * width + n_vectors].T
    own_up = [own[:, :width].T for own in own_ff]
    own_down = [own[:, width : 2 * width] for own in own_ff]
    own_up_bias = [own[:, 2 * width] for own in own_ff]
    return (
        layer_out,
        hidden_grad.reshape(items, item_rows, width),
        feature_grad,
        jnp.stack([own_self[:, n * width : (n + 1) * width] for n in range(3)]),
        own_self[:, 3 * width : 4 * width],
        own_sums[0:3],
        own_sums[3:7],
        own_sums[7:11],
        own_cross[:, cross_start : cross_start + width],
        own_cross[:, cross_start + width :],
        jnp.stack([own_cross[:, n * image_width : (n + 1) * image_width].T for n in range(2)]),
        own_sums[11:14],
        jnp.stack(own_up),
        jnp.stack(own_up_bias),
        jnp.stack(own_down),
        own_sums[14:16],
    )


def solution(mesh):
    dp, pair = mesh.devices.shape
    fine = Mesh(mesh.devices.reshape(dp // 4, 2, 2, pair), AXES)
    first, second, third = P(AXES), P(None, AXES), P(None, None, AXES)
    in_specs = (
        first, first, first, first,
        second, first, second, second, second, first, first,
        third, second, third, second, second, second,
    )
    out_specs = (
        first, first, first,
        second, first, second, second, second, first, first,
        third, second, third, second, second, second,
    )
    return jax.shard_map(shards, mesh=fine, in_specs=in_specs, out_specs=out_specs, check_vma=False)
```

```python
import functools

import jax
import jax.numpy as jnp
from jax import lax
from jax.experimental import pallas as pl
from jax.experimental.layout import Layout, with_layout_constraint
from jax.experimental.pallas import tpu as pltpu
from jax.sharding import Mesh, PartitionSpec as P

HEAD = 64
NQ = 32
GROUP = 256
PER = GROUP // HEAD
eps = 1e-06
masked_off = 1000000000.0
LATE = 4
AXES = ("z", "x", "c", "y")
BF = jnp.bfloat16
F32 = jnp.float32


def coords(index):
    return (index // 8, index // 4 % 2, index // 2 % 2, index % 2)


def pairs(count, move):
    result = []
    for source in range(count):
        z, x, c, y = move(*coords(source))
        result.append((source, ((z * 2 + x) * 2 + c) * 2 + y))
    return result


def step_a(z, x, c, y):
    return (z, x ^ 1, c, y) if c == 0 else (z, x, c, y ^ 1)


def step_b(z, x, c, y):
    return (z, x, c, y ^ 1) if c == 0 else (z, x ^ 1, c, y)


def step_c(z, x, c, y):
    return (z, x, c ^ 1, y)


def swap(value, move):
    count = lax.axis_size(AXES)
    return lax.ppermute(value, AXES, pairs(count, move))


def swap_z(value, distance):
    return swap(value, lambda z, x, c, y: (z ^ distance, x, c, y))


def gather_z(unit):
    if lax.axis_size("z") == 4:
        near = jnp.concatenate([unit, swap_z(unit, 2)], axis=0)
        return jnp.concatenate([near, swap_z(near, 1)], axis=0)
    return lax.all_gather(unit, "z", axis=0, tiled=True)


def gather_z_direct(unit):
    if lax.axis_size("z") == 4:
        one, two, three = (swap_z(unit, k) for k in (1, 2, 3))
        return jnp.concatenate([unit, two, one, three], axis=0)
    return lax.all_gather(unit, "z", axis=0, tiled=True)


def gather_all(near, first=(), last=()):
    a = swap(after(near, *first), step_a)
    b = swap(after(near, *last), step_b)
    pieces = [near, a, b, swap(a, step_b)]
    pieces.append(swap(after(near, *last), step_c))
    return pieces + [swap(piece, step_c) for piece in pieces[1:3]]


def finish_all(pieces, *gates):
    return pieces + [swap(after(pieces[3], *gates), step_c)]


def gather_plane(rows, first=(), second=()):
    rows = jnp.concatenate([rows, after(swap(rows, step_a), *first)], axis=0)
    rows = jnp.concatenate([rows, after(swap(rows, step_b), *second)], axis=0)
    return [rows, swap(rows, step_c)]


def after(value, *earlier):
    return lax.optimization_barrier((value,) + earlier)[0]


def add_low(left, right):
    return (left.astype(F32) + right.astype(F32)).astype(BF)


def halved(kept, got):
    half = got.shape[0] // 2
    return add_low(kept[:half], got[:half]), add_low(kept[half:], got[half:])


def scatter_plane(kept, sent):
    for move in (step_c, step_b):
        kept, sent = halved(kept, swap(sent, move))
    return kept, swap(sent, step_a)


def step_z1(z, x, c, y):
    return (z ^ 1, x, c, y)


def step_z2(z, x, c, y):
    return (z ^ 2, x, c, y)


def scatter_rest(kept, got):
    return lax.psum_scatter(add_low(kept, got), "z", scatter_dimension=0, tiled=True).astype(F32)


def slot_owner(count):
    z, x, c, y = (lax.axis_index(name) for name in AXES)
    planes = count // 8
    slot = jnp.arange(count)
    k = slot % planes
    alpha = slot // planes % 2
    beta = slot // (2 * planes) % 2
    core = c ^ (slot // (4 * planes))
    flip_x = jnp.where(core == 0, alpha, beta)
    flip_y = jnp.where(core == 0, beta, alpha)
    plane = z ^ (k % 2 * 2 + k // 2) if planes == 4 else k
    return ((plane * 2 + (x ^ flip_x)) * 2 + core) * 2 + (y ^ flip_y)


def place_of_slot(width):
    count = lax.axis_size(AXES)
    each = width // count
    source = (slot_owner(count)[:, None] * each + jnp.arange(each)[None, :]).reshape(-1)
    return (source[:, None] == jnp.arange(width)[None, :]).astype(BF)


def by_slot(values, order):
    return dot_t(values, order).astype(BF)


def by_slot_turned(values, order):
    return dot_t(order, values).astype(BF)


def by_place(values, order):
    return dot(values.astype(BF), order)


def dot(left, right):
    return lax.dot_general(
        left, right, (((left.ndim - 1,), (0,)), ((), ())), preferred_element_type=F32
    )


def dot_t(left, right):
    return lax.dot_general(
        left, right, (((left.ndim - 1,), (1,)), ((), ())), preferred_element_type=F32
    )


def outer(left, right):
    lead = tuple(range(left.ndim - 1))
    return lax.dot_general(left, right, ((lead, lead), ((), ())), preferred_element_type=F32)


def column_sum(values):
    return jnp.sum(values.astype(F32), axis=0, keepdims=True)


def layer_norm(values, scale, shift):
    center = values - jnp.mean(values, axis=-1, keepdims=True)
    spread = jnp.mean(center * center, axis=-1, keepdims=True)
    return center * lax.rsqrt(spread + eps) * scale + shift


def norm_back(values, scale, gradient):
    center = values - jnp.mean(values, axis=-1, keepdims=True)
    spread = jnp.mean(center * center, axis=-1, keepdims=True)
    inverse = lax.rsqrt(spread + eps)
    normal = center * inverse
    inner = gradient * scale
    result = inverse * (
        inner
        - jnp.mean(inner, axis=-1, keepdims=True)
        - normal * jnp.mean(inner * normal, axis=-1, keepdims=True)
    )
    return result, column_sum(gradient * normal), column_sum(gradient)


def gelu_parts(values):
    half = F32(0.5) + F32(0.5) * lax.erf(values * F32(0.5**0.5))
    return half


def gelu_slope(values):
    density = jnp.exp(values * values * F32(-0.5)) * F32((2.0 * 3.141592653589793) ** -0.5)
    return gelu_parts(values) + values * density


def head_masks():
    lane = lax.broadcasted_iota(jnp.int32, (1, GROUP), 1) // HEAD
    return [(lane == h).astype(F32).astype(BF) for h in range(PER)]


def spread_heads(rows, masks):
    return jnp.concatenate([rows * mask for mask in masks], axis=0)


def fold_heads(stacked, masks, count):
    total = None
    for h, mask in enumerate(masks):
        part = stacked[h * count : (h + 1) * count] * mask.astype(F32)
        total = part if total is None else total + part
    return total


def softmax_rows(scores):
    shifted = jnp.exp(scores - jnp.max(scores, axis=-1, keepdims=True))
    return shifted / jnp.sum(shifted, axis=-1, keepdims=True)


def self_mask(length, rows):
    shape = (PER * rows, rows)
    row = lax.broadcasted_iota(jnp.int32, shape, 0) % rows
    col = lax.broadcasted_iota(jnp.int32, shape, 1)
    allowed = (col < NQ) | ((row >= NQ) & (col <= row) & (col - NQ < length))
    return jnp.where(allowed, F32(0.0), F32(-masked_off))


def attend_group_back(q, k, v, mask_add, grad, masks, count):
    q = spread_heads(q, masks)
    grad = spread_heads(grad, masks)
    weights = softmax_rows(dot_t(q, k) * HEAD ** (-0.5) + mask_add)
    grad_value = outer(weights.astype(BF), grad).astype(BF)
    grad_weight = dot_t(grad, v)
    grad_score = (
        weights * (grad_weight - jnp.sum(grad_weight * weights, axis=-1, keepdims=True))
    ).astype(BF)
    grad_query = fold_heads(dot(grad_score, k), masks, count) * HEAD ** (-0.5)
    grad_key = outer(grad_score, q) * HEAD ** (-0.5)
    return grad_query.astype(BF), grad_key.astype(BF), grad_value


def repeat(count, body):
    def step(i, carry):
        body(i)
        return carry

    lax.fori_loop(0, count, step, 0)


def stretch(i, count):
    return pl.ds(pl.multiple_of(i * count, count), count)


def fetch(pieces, start, target, sems):
    width = target.shape[1]
    copies = []
    row = 0
    for n, piece in enumerate(pieces):
        count = piece.shape[0]
        source = piece.at[:, pl.ds(start, width)]
        copies.append(
            pltpu.make_async_copy(source, target.at[pl.ds(row, count)], sems.at[n])
        )
        row += count
    for copy in copies:
        copy.start()
    return copies


def finish(copies):
    for copy in copies:
        copy.wait()


def turned_rows(rows):
    rows = list(rows)
    each = rows[0].shape[1]
    rows.append(jnp.zeros((128 - sum(row.shape[0] for row in rows), each), F32))
    return jnp.concatenate(rows, axis=0).T.astype(BF)


def pack_kernel(refs):
    project_ref, output_ref, up_ref, down_ref, bias_ref = refs[:5]
    vector_refs, self_ref, ff_ref = refs[5:-2], refs[-2], refs[-1]
    width = output_ref.shape[1]
    for n in range(3):
        self_ref[:, pl.ds(n * width, width)] = project_ref[n]
    self_ref[:, pl.ds(3 * width, width)] = output_ref[...]
    vectors = turned_rows(ref[...].astype(F32) for ref in vector_refs)
    self_ref[:, pl.ds(4 * width, 128)] = vectors
    for n in range(2):
        start = n * (2 * width + 128)
        ff_ref[:, pl.ds(start, width)] = up_ref[n]
        ff_ref[:, pl.ds(start + width, width)] = down_ref[n]
        bias = bias_ref[n : n + 1, :].astype(F32)
        ff_ref[:, pl.ds(start + 2 * width, 128)] = turned_rows([bias])


def self_forward_kernel(items, n_pieces, refs):
    length_ref, hidden_ref, order_ref = refs[:3]
    pieces = refs[3 : 3 + n_pieces]
    qkv_ref, mix_ref, pre_ref, query_ref, text_ref, low_ref, vec_ref, w_ref, sems = refs[
        3 + n_pieces :
    ]
    rows_all, width = hidden_ref.shape
    copies = fetch(pieces, 0, w_ref, sems)
    order = order_ref[...]
    hidden_slot = by_slot(hidden_ref[...], order)
    finish(copies)
    vec = outer(w_ref[:, pl.ds(4 * width, 128)], order)[: vec_ref.shape[0]]
    vec_ref[...] = vec
    bias = [vec[0:1], F32(0.0), vec[1:2]]
    for n in range(3):
        cols = pl.ds(n * width, width)
        qkv_ref[:, cols] = (dot(hidden_slot, w_ref[:, cols]) + bias[n]).astype(BF)
    masks = head_masks()
    count = rows_all // items

    def attend(i):
        rows = stretch(i, count)
        mask_add = self_mask(length_ref[i], count)
        for g in range(width // GROUP):
            cols = [pl.ds(n * width + g * GROUP, GROUP) for n in range(3)]
            q = spread_heads(qkv_ref[rows, cols[0]], masks)
            scores = dot_t(q, qkv_ref[rows, cols[1]]) * HEAD ** (-0.5) + mask_add
            weights = softmax_rows(scores).astype(BF)
            mixed = dot(weights, qkv_ref[rows, cols[2]])
            mix_ref[rows, cols[0]] = fold_heads(mixed, masks, count).astype(BF)

    repeat(items, attend)
    mixture_slot = by_slot(mix_ref[...], order)
    pre = dot(mixture_slot, w_ref[:, pl.ds(3 * width, width)])
    pre = pre + vec[2:3] + hidden_ref[...].astype(F32)
    pre_ref[...] = pre
    first = layer_norm(pre, vec[3:4], vec[7:8])
    text = count - NQ
    for i in range(items):
        query_ref[pl.ds(i * NQ, NQ), :] = first[i * count : i * count + NQ]
        part = first[i * count + NQ : (i + 1) * count]
        text_ref[pl.ds(i * text, text), :] = part
        low_ref[pl.ds(i * text, text), :] = part.astype(BF)


def image_kernel(n_pieces, refs):
    feature_ref, order_ref, vec_ref = refs[:3]
    pieces = refs[3 : 3 + n_pieces]
    key_ref, value_ref, w_ref, sems = refs[3 + n_pieces :]
    items, _, image_width = feature_ref.shape
    copies = fetch(pieces, 0, w_ref, sems)
    order = order_ref[...]
    bias_slot = dot_t(vec_ref[...].astype(BF), order)[12:13]
    finish(copies)

    def project(i):
        rows = feature_ref[i]
        keys = dot_t(rows, w_ref[:, pl.ds(0, image_width)])
        key_ref[i] = by_place(keys, order_ref[...]).astype(BF)
        values = dot_t(rows, w_ref[:, pl.ds(image_width, image_width)]) + bias_slot
        value_ref[i] = by_place(values, order_ref[...]).astype(BF)

    repeat(items, project)


def cross_forward_kernel(start, n_pieces, refs):
    first_ref, key_ref, value_ref, order_ref, vec_ref = refs[:5]
    pieces = refs[5 : 5 + n_pieces]
    rows_ref, look_ref, pre_ref, second_ref, low_ref, w_ref, sems = refs[5 + n_pieces :]
    copies = fetch(pieces, start, w_ref, sems)
    items = key_ref.shape[0]
    width = first_ref.shape[1]
    count = first_ref.shape[0] // items
    order = order_ref[...]
    vec = vec_ref[...]
    masks = head_masks()
    first_slot = by_slot(first_ref[...].astype(BF), order)
    finish(copies)
    rows_ref[...] = (dot(first_slot, w_ref[:, pl.ds(0, width)]) + vec[11:12]).astype(BF)

    def attend(i):
        rows = stretch(i, count)
        for g in range(width // GROUP):
            cols = pl.ds(g * GROUP, GROUP)
            q = spread_heads(rows_ref[rows, cols], masks)
            scores = dot_t(q, key_ref[i, :, cols]) * HEAD ** (-0.5)
            mixed = dot(softmax_rows(scores).astype(BF), value_ref[i, :, cols])
            look_ref[rows, cols] = fold_heads(mixed, masks, count).astype(BF)

    repeat(items, attend)
    pre = dot(by_slot(look_ref[...], order), w_ref[:, pl.ds(width, width)])
    pre = pre + vec[13:14] + first_ref[...]
    pre_ref[...] = pre
    second = layer_norm(pre, vec[4:5], vec[8:9])
    second_ref[...] = second
    low_ref[...] = second.astype(BF)


def branch_up_kernel(branch, n_pieces, refs):
    low_refs = refs[:2]
    pieces = refs[2 : 2 + n_pieces]
    pre_ref, act_ref, kept_ref, sent_ref, w_ref, sems = refs[2 + n_pieces :]
    half, width = low_refs[0].shape
    copies = fetch(pieces, branch * (2 * width + 128), w_ref, sems)
    finish(copies)
    first_lane = (lax.broadcasted_iota(jnp.int32, (8, 128), 1) == 0).astype(F32).astype(BF)
    bias = dot_t(first_lane, w_ref[:, pl.ds(2 * width, 128)])[0:1]
    for n, (low_ref, out_ref) in enumerate(zip(low_refs, (kept_ref, sent_ref))):
        rows = pl.ds(n * half, half)
        pre = dot_t(low_ref[...], w_ref[:, pl.ds(0, width)]) + bias
        pre_ref[rows, :] = pre
        active = (pre * gelu_parts(pre)).astype(BF)
        act_ref[rows, :] = active
        out_ref[...] = dot(active, w_ref[:, pl.ds(width, width)]).astype(out_ref.dtype)


def branch_end_kernel(branch, refs):
    kept_ref, got_ref, value_ref, cot_ref, vec_ref = refs[:5]
    out_ref, grad_ref, low_ref, sum_ref = refs[5:]
    items, count, _ = cot_ref.shape
    vec = vec_ref[...]
    gain, shift = vec[5 + branch : 6 + branch], vec[9 + branch : 10 + branch]
    total = kept_ref[...].astype(F32) + got_ref[...].astype(F32)
    total = total + vec[14 + branch : 15 + branch] + value_ref[...]
    start, size = (NQ, count - NQ) if branch else (0, NQ)
    cot = jnp.concatenate([cot_ref[i, start : start + size, :] for i in range(items)], axis=0)
    out_ref[...] = layer_norm(total, gain, shift).astype(BF)
    grad, gain_grad, shift_grad = norm_back(total, gain, cot.astype(F32))
    grad_ref[...] = grad
    low = grad.astype(BF)
    low_ref[...] = low
    sum_ref[0:1, :] = gain_grad
    sum_ref[1:2, :] = shift_grad
    sum_ref[2:3, :] = column_sum(low)


def branch_down_kernel(branch, n_pieces, refs):
    grad_refs, low_refs, (pre_ref, act_ref) = refs[:2], refs[2:4], refs[4:6]
    pieces = refs[6 : 6 + n_pieces]
    rest = refs[6 + n_pieces :]
    kept_ref, sent_ref, own_ref, w_ref, sems = rest
    half, width = low_refs[0].shape
    copies = fetch(pieces, branch * (2 * width + 128), w_ref, sems)
    finish(copies)
    grads = []
    for n, out_ref in enumerate((kept_ref, sent_ref)):
        rows = pl.ds(n * half, half)
        back = dot_t(grad_refs[n][...], w_ref[:, pl.ds(width, width)])
        grad_pre = (gelu_slope(pre_ref[rows, :]) * back).astype(BF)
        grads.append(grad_pre)
        out_ref[...] = dot(grad_pre, w_ref[:, pl.ds(0, width)]).astype(out_ref.dtype)
    grad_pre = jnp.concatenate(grads, axis=0)
    low = jnp.concatenate([ref[...] for ref in low_refs], axis=0)
    grad_low = jnp.concatenate([ref[...] for ref in grad_refs], axis=0)
    own_ref[:, pl.ds(0, width)] = outer(grad_pre, low).astype(BF)
    own_ref[:, pl.ds(width, width)] = outer(act_ref[...], grad_low).astype(BF)
    sums = outer(grad_pre, jnp.ones((2 * half, 128), BF)).astype(BF)
    own_ref[:, pl.ds(2 * width, 128)] = sums


def cross_backward_kernel(start, n_pieces, refs):
    kept_ref, got_ref, sum_ref, pre_ref, q_ref, k_ref, v_ref, order_ref, vec_ref = refs[:9]
    pieces = refs[9 : 9 + n_pieces]
    dq_ref, dk_ref, dv_ref, low_ref, first_ref, row_ref, w_ref, look_ref, sems = refs[
        9 + n_pieces :
    ]
    copies = fetch(pieces, start, w_ref, sems)
    items = k_ref.shape[0]
    width = q_ref.shape[1]
    count = q_ref.shape[0] // items
    order = order_ref[...]
    vec = vec_ref[...]
    masks = head_masks()
    gradient = kept_ref[...].astype(F32) + got_ref[...].astype(F32) + sum_ref[...]
    grad_two, gain_grad, shift_grad = norm_back(pre_ref[...], vec[4:5], gradient)
    low = grad_two.astype(BF)
    low_ref[...] = low
    finish(copies)
    look_ref[...] = by_place(dot_t(low, w_ref[:, pl.ds(width, width)]), order).astype(BF)

    def attend(i):
        rows = stretch(i, count)
        for g in range(width // GROUP):
            cols = pl.ds(g * GROUP, GROUP)
            dq, dk, dv = attend_group_back(
                q_ref[rows, cols],
                k_ref[i, :, cols],
                v_ref[i, :, cols],
                F32(0.0),
                look_ref[rows, cols],
                masks,
                count,
            )
            dq_ref[rows, cols] = dq
            dk_ref[i, :, cols] = dk
            dv_ref[i, :, cols] = dv
            row_ref[3:4, cols] = row_ref[3:4, cols] + column_sum(dv)

    row_ref[3:4, :] = jnp.zeros((1, width), F32)
    repeat(items, attend)
    grad_cross = dq_ref[...]
    back = dot_t(grad_cross, w_ref[:, pl.ds(0, width)])
    first_ref[...] = grad_two + by_place(back, order)
    row_ref[0:1, :] = gain_grad
    row_ref[1:2, :] = shift_grad
    row_ref[2:3, :] = column_sum(grad_cross)
    row_ref[4:5, :] = column_sum(low)


def cross_weights_kernel(refs):
    dq_ref, dk_ref, dv_ref, low_ref, first_ref, look_ref, feature_ref, order_ref = refs[:8]
    kept_ref, sent_ref = refs[8:]
    items, _, image_width = feature_ref.shape
    half, width = order_ref.shape[0] // 2, order_ref.shape[1]
    for part, out_ref in enumerate((kept_ref, sent_ref)):
        order = order_ref[pl.ds(part * half, half), :]
        for n, grad_ref in enumerate((dk_ref, dv_ref)):
            total = None
            for i in range(items):
                turned = by_slot_turned(grad_ref[i], order)
                product = dot(turned, feature_ref[i])
                total = product if total is None else total + product
            out_ref[:, pl.ds(n * image_width, image_width)] = total.astype(BF)
        start = 2 * image_width
        turned = by_slot_turned(first_ref[...].astype(BF), order)
        out_ref[:, pl.ds(start, width)] = dot(turned, dq_ref[...]).astype(BF)
        turned = by_slot_turned(look_ref[...], order)
        out_ref[:, pl.ds(start + width, width)] = dot(turned, low_ref[...]).astype(BF)


def feature_kernel(n_pieces, refs):
    dk_ref, dv_ref, order_ref = refs[:3]
    pieces = refs[3 : 3 + n_pieces]
    out_ref, w_ref, sems = refs[3 + n_pieces :]
    items, _, image_width = out_ref.shape
    copies = fetch(pieces, 0, w_ref, sems)
    finish(copies)

    def back(i):
        keys, values = (by_slot(ref[i], order_ref[...]) for ref in (dk_ref, dv_ref))
        total = dot(keys, w_ref[:, pl.ds(0, image_width)])
        out_ref[i] = total + dot(values, w_ref[:, pl.ds(image_width, image_width)])

    repeat(items, back)


def self_backward_kernel(items, n_pieces, refs):
    length_ref, query_ref, kept_ref, got_ref, text_ref, pre_ref, qkv_ref = refs[:7]
    mix_ref, hidden_ref, order_ref, vec_ref = refs[7:11]
    row_refs = refs[11:14]
    pieces = refs[14 : 14 + n_pieces]
    grad_ref, one_ref, g_kept_ref, g_sent_ref, w_ref, sum_ref, mixed_ref, sems = refs[
        14 + n_pieces :
    ]
    copies = fetch(pieces, 3 * pre_ref.shape[1], w_ref, sems)
    rows_all, width = pre_ref.shape
    count = rows_all // items
    text = count - NQ
    order = order_ref[...]
    vec = vec_ref[...]
    masks = head_masks()
    text_grad = kept_ref[...].astype(F32) + got_ref[...].astype(F32) + text_ref[...]
    query_grad = query_ref[...]
    gradient = []
    for i in range(items):
        gradient.append(query_grad[i * NQ : (i + 1) * NQ])
        gradient.append(text_grad[i * text : (i + 1) * text])
    gradient = jnp.concatenate(gradient, axis=0)
    grad_one, gain_grad, shift_grad = norm_back(pre_ref[...], vec[3:4], gradient)
    one_ref[...] = grad_one
    low = grad_one.astype(BF)
    finish(copies)
    mixed_ref[...] = by_place(dot_t(low, w_ref[...]), order).astype(BF)

    def attend(i):
        rows = stretch(i, count)
        mask_add = self_mask(length_ref[i], count)
        for g in range(width // GROUP):
            cols = [pl.ds(n * width + g * GROUP, GROUP) for n in range(3)]
            results = attend_group_back(
                *[qkv_ref[rows, col] for col in cols],
                mask_add,
                mixed_ref[rows, cols[0]],
                masks,
                count,
            )
            for col, value in zip(cols, results):
                grad_ref[rows, col] = value

    repeat(items, attend)
    query_rows, query_ends, text_ends = row_refs
    sum_ref[...] = jnp.zeros(sum_ref.shape, F32)
    total = column_sum(grad_ref[...])
    listed = [
        total[:, :width],
        total[:, 2 * width :],
        column_sum(low),
        gain_grad,
        query_rows[0:1, :],
        query_ends[0:1, :],
        text_ends[0:1, :],
        shift_grad,
        query_rows[1:2, :],
        query_ends[1:2, :],
        text_ends[1:2, :],
        query_rows[2:3, :],
        query_rows[3:4, :],
        query_rows[4:5, :],
        query_ends[2:3, :],
        text_ends[2:3, :],
    ]
    for n, value in enumerate(listed):
        sum_ref[n : n + 1, :] = value
    sums = sum_ref[...].astype(BF)
    half = width // 2
    for part, out_ref in enumerate((g_kept_ref, g_sent_ref)):
        block = order_ref[pl.ds(part * half, half), :]
        turned = by_slot_turned(hidden_ref[...], block)

        def weigh(n):
            cols = stretch(n, width)
            out_ref[:, cols] = dot(turned, grad_ref[:, cols]).astype(BF)

        repeat(3, weigh)
        turned = by_slot_turned(mix_ref[...], block)
        out_ref[:, pl.ds(3 * width, width)] = dot(turned, low).astype(BF)
        out_ref[:, pl.ds(4 * width, 128)] = dot_t(block, sums).astype(BF)


def hidden_kernel(n_pieces, refs):
    grad_ref, one_ref, order_ref = refs[:3]
    pieces = refs[3 : 3 + n_pieces]
    out_ref, w_ref, sems = refs[3 + n_pieces :]
    copies = fetch(pieces, 0, w_ref, sems)
    finish(copies)
    width = one_ref.shape[1]

    def part(n, total):
        cols = stretch(n, width)
        return total + dot_t(grad_ref[:, cols], w_ref[:, cols])

    back = lax.fori_loop(0, 3, part, jnp.zeros(one_ref.shape, F32))
    out_ref[...] = one_ref[...] + by_place(back, order_ref[...])


def shaped(*dims, kind=F32):
    return jax.ShapeDtypeStruct(dims, kind)


def kernel_call(
    body, name, outs, inputs, pieces=(), loaded=None, lengths=None, extra=(), cost=12
):
    vmem = pl.BlockSpec(memory_space=pltpu.VMEM)
    specs = [vmem] * len(inputs) + [pl.BlockSpec(memory_space=pl.ANY)] * len(pieces)
    arrays = tuple(inputs) + tuple(pieces)
    if lengths is not None:
        specs = [pl.BlockSpec(memory_space=pltpu.SMEM)] + specs
        arrays = (lengths,) + arrays
    scratch = []
    if loaded is not None:
        rows = sum(piece.shape[0] for piece in pieces)
        scratch = [pltpu.VMEM((rows, loaded), BF)] + list(extra)
        scratch.append(pltpu.SemaphoreType.DMA((len(pieces),)))
    return pl.pallas_call(
        lambda *refs: body(refs),
        name=name,
        out_shape=outs,
        in_specs=specs,
        out_specs=jax.tree.map(lambda _: vmem, outs),
        scratch_shapes=scratch,
        cost_estimate=pl.CostEstimate(
            flops=int(cost * 900_000_000), bytes_accessed=int(cost * 3_000_000), transcendentals=0
        ),
    )(*arrays)


def shards(
    hidden,
    features,
    text_lengths,
    cotangent,
    self_project,
    self_output,
    self_bias,
    norm_gain,
    norm_bias,
    cross_query,
    cross_output,
    image_project,
    cross_bias,
    expand_weight,
    expand_bias,
    reduce_weight,
    reduce_bias,
):
    part = functools.partial
    items, item_rows, width = hidden.shape
    each = self_output.shape[0]
    image_rows, image_width = features.shape[1:]
    ff_each = reduce_weight.shape[1]
    planes = lax.axis_size("z")
    rows = items * item_rows
    query_rows, text_rows = items * NQ, items * (item_rows - NQ)
    ff = planes * ff_each
    order = place_of_slot(width)
    features = with_layout_constraint(features, Layout((0, 1, 2)))
    flat = after(hidden.reshape(rows, width), features)

    vectors = (self_bias, norm_gain, norm_bias, cross_bias, reduce_bias)
    n_vectors = sum(v.shape[0] for v in vectors)
    ff_width = 2 * width + 128
    up_turned = jnp.swapaxes(expand_weight, 1, 2)
    unit_self, unit_ff = kernel_call(
        pack_kernel,
        "pack",
        (shaped(each, 4 * width + 128, kind=BF), shaped(ff_each, 2 * ff_width, kind=BF)),
        (self_project, self_output, up_turned, reduce_weight, expand_bias, *vectors),
        cost=1,
    )
    image_turned = jnp.swapaxes(image_project, 1, 2)
    unit_cross = jnp.concatenate(
        [image_turned[0], image_turned[1], cross_query, cross_output], axis=1
    )
    w_ff = [lax.all_gather(unit_ff, "z", axis=0, tiled=True)]
    near_self = gather_z_direct(unit_self)
    w_self = finish_all(gather_all(near_self))
    near_cross = gather_z(after(unit_cross, near_self))
    w_cross = gather_all(near_cross, w_self[1:3], w_self[3:4])
    cross_start = 2 * image_width

    qkv, mixture, pre_one, first_query, first_text, text_low, vec = kernel_call(
        part(self_forward_kernel, items, len(w_self)),
        "self_forward",
        (
            shaped(rows, 3 * width, kind=BF),
            shaped(rows, width, kind=BF),
            shaped(rows, width),
            shaped(query_rows, width),
            shaped(text_rows, width),
            shaped(text_rows, width, kind=BF),
            shaped(n_vectors, width),
        ),
        (flat, order),
        w_self,
        4 * width + 128,
        text_lengths,
    )

    w_cross = finish_all(w_cross, first_query)
    wide = shaped(items, image_rows, width, kind=BF)
    image_keys, image_values = kernel_call(
        part(image_kernel, len(w_cross)),
        "image_rows",
        (wide, wide),
        (features, order, vec),
        w_cross,
        cross_start,
    )
    cross_rows, looked, pre_two, second, second_low = kernel_call(
        part(cross_forward_kernel, cross_start, len(w_cross)),
        "cross_forward",
        (
            shaped(query_rows, width, kind=BF),
            shaped(query_rows, width, kind=BF),
            shaped(query_rows, width),
            shaped(query_rows, width),
            shaped(query_rows, width, kind=BF),
        ),
        (first_query, image_keys, image_values, order, vec),
        w_cross,
        2 * width,
    )

    branches = [None, None]
    for j, values, low in ((1, first_text, text_low), (0, second, second_low)):
        count = values.shape[0]
        if j:
            low_all = gather_plane(low, (image_keys,), (second_low,))
        else:
            low_all = gather_plane(low)
        half = 4 * count
        pre_act, active, kept, sent = kernel_call(
            part(branch_up_kernel, j, len(w_ff)),
            "branch_up_%d" % j,
            (
                shaped(2 * half, ff),
                shaped(2 * half, ff, kind=BF),
                shaped(half, width),
                shaped(half, width, kind=BF),
            ),
            low_all,
            w_ff,
            ff_width,
        )
        out, grad_sum, grad_low, ends = kernel_call(
            part(branch_end_kernel, j),
            "branch_end_%d" % j,
            (
                shaped(count, width, kind=BF),
                shaped(count, width),
                shaped(count, width, kind=BF),
                shaped(8, width),
            ),
            (*scatter_plane(kept, sent), values, cotangent, vec),
        )
        kept, sent, grads = kernel_call(
            part(branch_down_kernel, j, len(w_ff)),
            "branch_down_%d" % j,
            (
                shaped(half, width),
                shaped(half, width, kind=BF),
                shaped(ff, ff_width, kind=BF),
            ),
            (*gather_plane(grad_low), *low_all, pre_act, active),
            w_ff,
            2 * width,
        )
        own = lax.psum_scatter(grads, "z", scatter_dimension=0, tiled=True)
        branches[j] = (out, grad_sum, ends, scatter_plane(kept, sent), own)
    query, text = branches
    layer_out = jnp.concatenate(
        [query[0].reshape(items, NQ, width), text[0].reshape(items, item_rows - NQ, width)],
        axis=1,
    )

    query_got = after(query[3][1], text[3][1])
    grad_cross, grad_ikey, grad_ivalue, two_low, grad_first, cross_ends = kernel_call(
        part(cross_backward_kernel, cross_start, len(w_cross)),
        "cross_backward",
        (
            shaped(query_rows, width, kind=BF),
            wide,
            wide,
            shaped(query_rows, width, kind=BF),
            shaped(query_rows, width),
            shaped(8, width),
        ),
        (query[3][0], query_got, query[1], pre_two, cross_rows, image_keys, image_values, order, vec),
        w_cross,
        2 * width,
        extra=(pltpu.VMEM((query_rows, width), BF),),
        cost=LATE,
    )
    packed = shaped(width // 2, cross_start + 2 * width, kind=BF)
    grad_cross = after(grad_cross, branches[1][4])
    cross_kept, cross_sent = kernel_call(
        cross_weights_kernel,
        "cross_weights",
        (packed, packed),
        (grad_cross, grad_ikey, grad_ivalue, two_low, first_query, looked, features, order),
        cost=LATE,
    )
    feature_order = after(order, cross_sent)
    feature_grad = kernel_call(
        part(feature_kernel, len(w_cross)),
        "feature_grad",
        shaped(items, image_rows, image_width),
        (grad_ikey, grad_ivalue, feature_order),
        w_cross,
        cross_start,
        cost=LATE,
    )
    cross_got = after(swap(cross_sent, step_c), feature_grad)
    cross_kept, cross_sent = halved(cross_kept, cross_got)

    grad_first = after(grad_first, cross_sent)
    packed = shaped(width // 2, 4 * width + 128, kind=BF)
    grad_qkv, grad_one, kept, sent = kernel_call(
        part(self_backward_kernel, items, len(w_self)),
        "self_backward",
        (shaped(rows, 3 * width, kind=BF), shaped(rows, width), packed, packed),
        (
            grad_first,
            *text[3],
            text[1],
            pre_one,
            qkv,
            mixture,
            flat,
            order,
            vec,
            cross_ends,
            query[2],
            text[2],
        ),
        w_self,
        width,
        text_lengths,
        (pltpu.VMEM((128, width), F32), pltpu.VMEM((rows, width), BF)),
        LATE,
    )
    feature_grad = with_layout_constraint(feature_grad, Layout((1, 0, 2)))
    cross_got = after(swap(cross_sent, step_b), feature_grad)
    sent = after(sent, cross_got, branches[0][4])
    cross_kept, cross_sent = halved(cross_kept, cross_got)
    kept, sent = halved(kept, swap(sent, step_c))
    hidden_order = after(order, sent)
    hidden_grad = kernel_call(
        part(hidden_kernel, len(w_self)),
        "hidden_grad",
        shaped(rows, width),
        (grad_qkv, grad_one, hidden_order),
        w_self,
        3 * width,
        cost=LATE,
    )
    cross_got = after(swap(cross_sent, step_a), hidden_grad)
    got = swap(sent, step_b)
    if planes == 4:
        cross_kept, cross_sent = halved(cross_kept, cross_got)
        kept, sent = halved(kept, after(got, cross_sent))
        cross_got = after(swap(cross_sent, step_z1), sent)
        cross_kept, cross_sent = halved(cross_kept, cross_got)
        kept, sent = halved(kept, after(swap(sent, step_a), cross_sent))
        cross_got = after(swap(cross_sent, step_z2), sent)
        own_cross = cross_kept.astype(F32) + cross_got.astype(F32)
        kept, sent = halved(kept, swap(sent, step_z1))
        own_self = kept.astype(F32) + swap(sent, step_z2).astype(F32)
    else:
        own_cross = scatter_rest(cross_kept, cross_got)
        kept, sent = halved(kept, got)
        own_self = scatter_rest(kept, swap(sent, step_a))
    own_ff = [after(branch[4], sent).astype(F32) for branch in branches]
    own_sums = own_self[:, 4 * width : 4 * width + n_vectors].T
    own_up = [own[:, :width].T for own in own_ff]
    own_down = [own[:, width : 2 * width] for own in own_ff]
    own_up_bias = [own[:, 2 * width] for own in own_ff]
    return (
        layer_out,
        hidden_grad.reshape(items, item_rows, width),
        feature_grad,
        jnp.stack([own_self[:, n * width : (n + 1) * width] for n in range(3)]),
        own_self[:, 3 * width : 4 * width],
        own_sums[0:3],
        own_sums[3:7],
        own_sums[7:11],
        own_cross[:, cross_start : cross_start + width],
        own_cross[:, cross_start + width :],
        jnp.stack([own_cross[:, n * image_width : (n + 1) * image_width].T for n in range(2)]),
        own_sums[11:14],
        jnp.stack(own_up),
        jnp.stack(own_up_bias),
        jnp.stack(own_down),
        own_sums[14:16],
    )


def solution(mesh):
    dp, pair = mesh.devices.shape
    fine = Mesh(mesh.devices.reshape(dp // 4, 2, 2, pair), AXES)
    first, second, third = P(AXES), P(None, AXES), P(None, None, AXES)
    in_specs = (
        first, first, first, first,
        second, first, second, second, second, first, first,
        third, second, third, second, second, second,
    )
    out_specs = (
        first, first, first,
        second, first, second, second, second, first, first,
        third, second, third, second, second, second,
    )
    return jax.shard_map(shards, mesh=fine, in_specs=in_specs, out_specs=out_specs, check_vma=False)
```
